256 devices in a mesh: slab: 64 (over z, x, core), tile: 4 (over y).
Axes of the slice: x: 4, y: 4, z: 8, core: 2. Of those that a mesh axis runs over, the one named last changes fastest.
Arguments:
- solution: float32 [128, 1024, 256], P('tile', 'slab'), may hold values from -6 to 6
- source: float32 [128, 1024, 256], P('tile', 'slab'), may hold values from 0 to 2
- phase_label: int32 [128, 1024, 256], P('tile', 'slab'), may hold values from 0 to 2
- phase_diffusivity: float32 [3], replicated, may hold values from 0.1 to 2
- phase_uptake: float32 [3], replicated, may hold values from 0.2 to 1
- send_tiles: int32 [64, 4, 64, 1], P('slab', 'tile'), may hold values from 0 to 31
- support_slot: int32 [64, 4, 64], P('slab', 'tile'), may hold values from 0 to 63, each once within a row
- support_len: int32 [64, 4, 8], P('slab', 'tile'), may hold values from 1 to 8, 40 in all within a row
- coarse_ids: int32 [2048], P(('slab', 'tile')), may hold values from 0 to 2047, each once
- basis_values: bfloat16 [2048, 8, 4096], P(('slab', 'tile')), may hold values from 0 to 0.25
- coarse_diag: float32 [2048], P(('slab', 'tile')), may hold values from 320 to 480
- coarse_off: float32 [2048, 26], P(('slab', 'tile')), may hold values from -12 to -4
- coarse_cols: int32 [2048, 26], P(('slab', 'tile')), may hold values from 0 to 2047
Outputs:
- new_solution: float32 [128, 1024, 256], P('tile', 'slab')
- coarse_correction: float32 [2048], P(('slab', 'tile'))
The draws below stay inside these ranges and needn't reach their ends.
Inputs may be any that keep to these rules, and one draw needn't show every extreme that they name: `support_slot`: on each device the 64 entries are the numbers 0 to 63, each once. `support_len`: on each device the lengths sum to 40, and some cell has 8. `coarse_ids`: every coarse cell appears once.
All inputs are finite; a program needn't handle non-finite values.
Results may differ from the reference program's by a relative error of at most 0.00062.
Values may be sent and summed in bfloat16 or wider, within the bound.
A program may use at most 64 MiB of HBM per device.

```python
import math
import jax
import jax.numpy as jnp
import numpy as np
from jax import lax

CY = 32
NX = 256
SUPPORT = 8
NPHASE = 3
NNZ = 26
COARSE_SWEEPS = 4
SMOOTH_SWEEPS = 2
TV = 4096
CELLS = 8
CAP = 1
LIVE = 40
NY = 128
NZ = 1024
NC = 2048
N_SLAB = 64
N_TILE = 4


def set_ends(result, rng, low, top_value):
    dims = result.shape
    index_at = [jax.random.randint(jax.random.fold_in(rng, axis), (), 0, dims[axis]) for axis in range(len(dims))]
    result = result.at[tuple(index_at)].set(low)
    longest = dims.index(max(dims))
    index_at[longest] = (index_at[longest] + 1) % dims[longest]
    return result.at[tuple(index_at)].set(top_value)


def block_scale(stream_key, shape, split, low, top_value):
    def one(axis_at, parts):
        draws = jax.random.uniform(jax.random.fold_in(jax.random.fold_in(stream_key, 6), axis_at), (parts,), jnp.float32, low / len(split), top_value / len(split))
        return jnp.repeat(jnp.exp(draws), shape[axis_at] // parts).reshape((-1,) + (1,) * (len(shape) - axis_at - 1))

    loudness = one(*split[0])
    for cut in split[1:]:
        loudness = loudness * one(*cut)
    return loudness


def length_profile(count, total, bound, lean):
    portions = [(1 << 20) // math.isqrt(standing ** lean) + 1 for standing in range(2, count + 1)]
    surplus, holding = total - bound - (count - 1), [1] * (count - 1)
    while surplus > 0:
        free = [i for i in range(count - 1) if holding[i] < bound]
        whole, remaining = sum([portions[i] for i in free]), surplus
        for i in free:
            extra = min(bound - holding[i], max(1, remaining * portions[i] // whole), surplus)
            holding[i] = holding[i] + extra
            surplus = surplus - extra
    return np.array([bound] + holding)


def uneven(key, count, total, limit, slope):
    if count == 2:
        one = jax.random.randint(key, (), max(1, total - limit), min(limit, total - 1) + 1)
        return jnp.stack([one, total - one])
    sizes = jnp.asarray(length_profile(count, total, limit, slope), jnp.int32)
    pairs = (count - 1) // 2
    giver, receiver = sizes[1:1 + 2 * pairs:2], sizes[2:2 + 2 * pairs:2]
    room = jnp.minimum(giver - 1, limit - receiver)
    moved = jax.random.randint(jax.random.fold_in(key, 1), (pairs,), 0, 1 << 20) % (room + 1)
    sizes = sizes.at[1:1 + 2 * pairs:2].set(giver - moved).at[2:2 + 2 * pairs:2].set(receiver + moved)
    return sizes[jax.random.permutation(jax.random.fold_in(key, 2), count)]


def centred(key, dims, spread, limit, cuts=(), kind=jnp.bfloat16):
    drawn = spread * jax.random.normal(key, dims, jnp.float32)
    if cuts:
        drawn = drawn * block_scale(key, dims, cuts, -0.22, 0.18)
    return jnp.clip(drawn, -limit, limit).astype(kind)


def setup_inputs(seed: int = 0) -> dict:
    key_of = jax.random.split(jax.random.key(seed), 14)
    solution = centred(key_of[0], (NY, NZ, NX), 1.0, 6.0, ((0, 4), (1, 64)), jnp.float32)
    source = jnp.clip(2.0 * jax.random.uniform(key_of[1], (NY, NZ, NX), jnp.float32) ** block_scale(key_of[1], (NY, NZ, NX), ((0, 4), (1, 64)), -0.2, 0.2), 0.0, 2.0)
    phase_label = set_ends(jax.random.randint(key_of[2], (NY, NZ, NX), 0, NPHASE), jax.random.fold_in(key_of[2], 1), 0, NPHASE - 1).astype(jnp.int32)
    phase_diffusivity = jnp.clip(jnp.exp(jax.random.uniform(key_of[3], (NPHASE,), jnp.float32, math.log(0.1), math.log(2.0))), 0.1, 2.0)
    phase_uptake = jnp.clip(jnp.exp(jax.random.uniform(key_of[4], (NPHASE,), jnp.float32, math.log(0.2), math.log(1.0))), 0.2, 1.0)
    send_tiles = set_ends(jax.random.randint(key_of[5], (N_SLAB, N_TILE, N_SLAB, CAP), 0, CY), jax.random.fold_in(key_of[5], 1), 0, CY - 1).astype(jnp.int32)
    support_slot = jax.vmap(lambda own: jax.random.permutation(own, CELLS * SUPPORT))(jax.random.split(key_of[6], N_SLAB * N_TILE)).reshape((N_SLAB, N_TILE, CELLS * SUPPORT)).astype(jnp.int32)
    support_len = jax.vmap(lambda own: uneven(own, CELLS, LIVE, SUPPORT, 1))(jax.random.split(key_of[7], N_SLAB * N_TILE)).reshape((N_SLAB, N_TILE, CELLS)).astype(jnp.int32)
    coarse_ids = jax.random.permutation(key_of[8], NC).astype(jnp.int32)
    basis_values = jnp.clip(0.25 * jax.random.uniform(key_of[9], (NC, SUPPORT, TV), jnp.float32) ** block_scale(key_of[9], (NC, SUPPORT, TV), ((0, 256),), -0.2, 0.2), 0.0, 0.25).astype(jnp.bfloat16)
    coarse_diag = jnp.clip(jnp.exp(math.log(480.0) - 0.4054651 * jax.random.uniform(key_of[10], (NC,), jnp.float32) ** block_scale(key_of[10], (NC,), ((0, 256),), -0.2, 0.2)), 320.0, 480.0)
    coarse_off = jnp.clip(-12.0 + 8.0 * jax.random.uniform(key_of[11], (NC, NNZ), jnp.float32) ** block_scale(key_of[11], (NC, NNZ), ((0, 256),), -0.2, 0.2), -12.0, -4.0)
    coarse_cols = set_ends(jax.random.randint(key_of[12], (NC, NNZ), 0, NC), jax.random.fold_in(key_of[12], 1), 0, NC - 1).astype(jnp.int32)
    return dict(solution=solution, source=source, phase_label=phase_label, phase_diffusivity=phase_diffusivity, phase_uptake=phase_uptake, send_tiles=send_tiles, support_slot=support_slot, support_len=support_len, coarse_ids=coarse_ids, basis_values=basis_values, coarse_diag=coarse_diag, coarse_off=coarse_off, coarse_cols=coarse_cols)


OMEGA = 0.8


def neighbours(padded):
    return (padded[2:, 1:-1, 1:-1], padded[:-2, 1:-1, 1:-1], padded[1:-1, 2:, 1:-1],
            padded[1:-1, :-2, 1:-1], padded[1:-1, 1:-1, 2:], padded[1:-1, 1:-1, :-2])


def face_weights(center, padded):
    return tuple(0.5 * (center + other) for other in neighbours(padded))


def operate(values, weights, diagonal):
    beside_all = neighbours(jnp.pad(values, 1))
    coupled = weights[0] * beside_all[0]
    for number in range(1, 6):
        coupled = coupled + weights[number] * beside_all[number]
    return diagonal * values - coupled


def reference(solution, source, phase_label, phase_diffusivity, phase_uptake, send_tiles, support_slot, support_len, coarse_ids, basis_values, coarse_diag, coarse_off, coarse_cols):
    conduct = phase_diffusivity[phase_label]
    uptake = phase_uptake[phase_label]
    weights = face_weights(conduct, jnp.pad(conduct, 1))
    diagonal = uptake + weights[0] + weights[1] + weights[2] + weights[3] + weights[4] + weights[5]
    residual = source - operate(solution, weights, diagonal)
    tile_stack = residual.astype(jnp.bfloat16).reshape(NY, N_SLAB, TV)
    owners = N_SLAB * N_TILE
    slot_all = support_slot.reshape(owners, CELLS * SUPPORT)
    live_all = jnp.arange(SUPPORT)[None, None, :] < support_len.reshape(owners, CELLS)[:, :, None]
    basis_all = basis_values.reshape(owners, CELLS * SUPPORT, TV)

    def locate(owner):
        owner_slab = owner // N_TILE
        owner_tile = owner % N_TILE
        slot_list = slot_all[owner]
        source_slab = (slot_list // CAP).astype(jnp.int32)
        position = (slot_list % CAP).astype(jnp.int32)
        tile_row = (owner_tile * CY + send_tiles[source_slab, owner_tile, owner_slab, position]).astype(jnp.int32)
        return tile_row, source_slab

    def restrict(owner):
        tile_row, source_slab = locate(owner)
        pieces = tile_stack[tile_row, source_slab].astype(jnp.float32)
        products = jnp.sum(pieces * basis_all[owner].astype(jnp.float32), axis=1).reshape(CELLS, SUPPORT)
        return jnp.sum(jnp.where(live_all[owner], products, 0.0), axis=1)

    restricted = lax.map(restrict, jnp.arange(owners, dtype=jnp.int32)).reshape(NC)
    coarse_rhs = jnp.zeros((NC,), jnp.float32).at[coarse_ids].set(restricted)
    coarse_state = coarse_rhs / coarse_diag
    for repeat in range(COARSE_SWEEPS - 1):
        coarse_state = (coarse_rhs - jnp.sum(coarse_off * coarse_state[coarse_cols], axis=1)) / coarse_diag
    coarse_correction = coarse_state[coarse_ids]
    correction_all = coarse_correction.reshape(owners, CELLS)

    def deposit(accumulated, owner):
        tile_row, source_slab = locate(owner)
        scaled = correction_all[owner][:, None, None] * basis_all[owner].reshape(CELLS, SUPPORT, TV).astype(jnp.float32)
        rounded = jnp.where(live_all[owner][:, :, None], scaled, 0.0).astype(jnp.bfloat16)
        rounded = lax.optimization_barrier(rounded).astype(jnp.float32)
        accumulated = accumulated.at[tile_row, source_slab].add(rounded.reshape(CELLS * SUPPORT, TV))
        return accumulated, None

    prolonged, unused = lax.scan(deposit, jnp.zeros((NY, N_SLAB, TV), jnp.float32), jnp.arange(owners, dtype=jnp.int32))
    corrected = solution + prolonged.reshape(NY, NZ, NX)
    for repeat in range(SMOOTH_SWEEPS):
        corrected = corrected + OMEGA * (source - operate(corrected, weights, diagonal)) / diagonal
    return corrected, coarse_correction
```

```python
import functools

import jax
import jax.numpy as jnp
from jax import lax
from jax.experimental import pallas as pl
from jax.experimental.pallas import tpu as pltpu
from jax.sharding import PartitionSpec as P

COARSE_SWEEPS = 4
SMOOTH_SWEEPS = 2
OMEGA = 0.8
MESH = pl.DeviceIdType.MESH
LANES = 128

ZS, XS, CORES, YS = 8, 4, 2, 4
NEAR = ZS * CORES
FAR = XS * YS
SLABS = ZS * XS * CORES


def split_slab(slab):
    return slab // (XS * CORES), (slab // CORES) % XS, slab % CORES


def near_slab(near, x):
    return ((near // CORES) * XS + x) * CORES + near % CORES


def far_slab(far, z, core):
    return (z * XS + far // YS) * CORES + core


def place_of(index):
    owner, row = index // 8, index % 8
    slab, tile = owner // YS, owner % YS
    z, x, core = split_slab(slab)
    return ((x * YS + tile) * NEAR + z * CORES + core) * 8 + row


VMEM = pl.BlockSpec(memory_space=pltpu.VMEM)
SMEM = pl.BlockSpec(memory_space=pltpu.SMEM)


def remote(src, dst, send_sem, recv_sem, slab, tile):
    return pltpu.make_async_remote_copy(
        src_ref=src, dst_ref=dst, send_sem=send_sem, recv_sem=recv_sem,
        device_id=(slab, tile), device_id_type=MESH,
    )


def exchange_kernel(basis, zface, yface, meta, got, zhalo, yhalo, table,
                    a_send, a_recv, n_send, n_recv, f_send, f_recv, h_send, h_recv, own):
    slab, tile = lax.axis_index("slab"), lax.axis_index("tile")
    z, x, core = split_slab(slab)
    near = z * CORES + core
    far = x * YS + tile
    order = x * NEAR + near
    place = far * NEAR + near

    barrier = pltpu.get_barrier_semaphore()

    def greet_slab(k, carry):
        pl.semaphore_signal(barrier, inc=1, device_id=(lax.rem(slab + k, SLABS), tile), device_id_type=MESH)
        return carry

    def greet_far(k, carry):
        step = k + 1
        x_to, y_to = (x + step % XS) % XS, (tile + 1 + k // XS) % YS
        pl.semaphore_signal(barrier, inc=1, device_id=((z * XS + x_to) * CORES + core, y_to), device_id_type=MESH)
        return carry

    lax.fori_loop(1, SLABS, greet_slab, 0)
    lax.fori_loop(0, XS * (YS - 1), greet_far, 0)
    pl.semaphore_wait(barrier, SLABS - 1 + XS * (YS - 1))

    up_slab, down_slab = lax.rem(slab + 1, SLABS), lax.rem(slab + SLABS - 1, SLABS)
    up_tile, down_tile = lax.rem(tile + 1, YS), lax.rem(tile + YS - 1, YS)
    halos = (
        remote(zface.at[1], zhalo.at[0], h_send.at[0], h_recv.at[0], up_slab, tile),
        remote(zface.at[0], zhalo.at[1], h_send.at[1], h_recv.at[1], down_slab, tile),
        remote(yface.at[1], yhalo.at[0], h_send.at[2], h_recv.at[2], slab, up_tile),
        remote(yface.at[0], yhalo.at[1], h_send.at[3], h_recv.at[3], slab, down_tile),
    )
    mine = pltpu.make_async_copy(meta, table.at[place], own.at[0])
    mine.start()
    kept = pltpu.make_async_copy(basis.at[slab], got.at[order], own.at[1])
    kept.start()

    def near_copy(k):
        return remote(meta, table.at[place], n_send.at[k], n_recv.at[k], near_slab(lax.rem(near + k, NEAR), x), tile)

    def far_copy(k):
        to = lax.rem(far + k, FAR)
        block = table.at[pl.ds(far * NEAR, NEAR)]
        return remote(block, block, f_send.at[k], f_recv.at[k], far_slab(to, z, core), to % YS)

    def basis_copy(k):
        to = lax.rem(slab + k, SLABS)
        return remote(basis.at[to], got.at[order], a_send.at[k], a_recv.at[k], to, tile)

    def loop(low, high, act):
        def body(k, carry):
            act(k)
            return carry
        lax.fori_loop(low, high, body, 0)

    loop(1, NEAR, lambda k: near_copy(k).start())
    for copy in halos:
        copy.start()
    loop(1, SLABS, lambda k: basis_copy(k).start())
    mine.wait()
    loop(1, NEAR, lambda k: near_copy(k).wait())
    loop(1, FAR, lambda k: far_copy(k).start())
    kept.wait()
    for copy in halos:
        copy.wait()
    loop(1, FAR, lambda k: far_copy(k).wait())
    loop(1, SLABS, lambda k: basis_copy(k).wait())


def exchange(basis, zface, yface, meta):
    return pl.pallas_call(
        exchange_kernel,
        out_shape=(
            jax.ShapeDtypeStruct(basis.shape, basis.dtype),
            jax.ShapeDtypeStruct(zface.shape, zface.dtype),
            jax.ShapeDtypeStruct(yface.shape, yface.dtype),
            jax.ShapeDtypeStruct((NEAR * FAR,) + meta.shape, meta.dtype),
        ),
        in_specs=[VMEM] * 4,
        out_specs=(VMEM,) * 4,
        scratch_shapes=[
            pltpu.SemaphoreType.DMA((SLABS,)), pltpu.SemaphoreType.DMA((SLABS,)),
            pltpu.SemaphoreType.DMA((NEAR,)), pltpu.SemaphoreType.DMA((NEAR,)),
            pltpu.SemaphoreType.DMA((FAR,)), pltpu.SemaphoreType.DMA((FAR,)),
            pltpu.SemaphoreType.DMA((4,)), pltpu.SemaphoreType.DMA((4,)),
            pltpu.SemaphoreType.DMA((2,)),
        ],
        compiler_params=pltpu.CompilerParams(collective_id=0, has_side_effects=True, vmem_limit_bytes=32 << 20),
        name="exchange",
    )(basis, zface, yface, meta)


def beside(mid, below, above, zlow, zhigh):
    depth, width = mid.shape
    zi = lax.broadcasted_iota(jnp.int32, mid.shape, 0)
    xi = lax.broadcasted_iota(jnp.int32, mid.shape, 1)
    total = below + above
    total = total + jnp.where(zi == 0, zlow, pltpu.roll(mid, 1, 0))
    total = total + jnp.where(zi == depth - 1, zhigh, pltpu.roll(mid, depth - 1, 0))
    total = total + jnp.where(xi == 0, 0.0, pltpu.roll(mid, 1, 1))
    total = total + jnp.where(xi == width - 1, 0.0, pltpu.roll(mid, width - 1, 1))
    return total


def lookup(label, table):
    result = jnp.full(label.shape, table[0], jnp.float32)
    for category in range(1, table.shape[0]):
        result = jnp.where(label == category, table[category], result)
    return result


def residual_kernel(edge, diffusivity, uptake, send, where, value, source, label, zhalo, yhalo, got, table,
                    partial, target, conduct, weight, cpad, vpad, upad, tiles, sums):
    rows = value.shape[0]
    slab, tile = where[0], where[1]

    def fill(y, carry):
        c = lookup(label[y], diffusivity)
        v = value[y]
        cpad[y + 1] = c
        vpad[y + 1] = v
        upad[y + 1] = c * v
        conduct[y] = c
        return carry

    lax.fori_loop(0, rows, fill, 0, unroll=4)
    for side, at, flag in ((0, 0, edge[2]), (1, rows + 1, edge[3])):
        c = yhalo[side, 0] * flag
        v = yhalo[side, 1] * flag
        cpad[at] = c
        vpad[at] = v
        upad[at] = c * v

    def plane(y, carry):
        c, v, u = cpad[y + 1], vpad[y + 1], upad[y + 1]
        clow = zhalo[0, 0, pl.ds(y, 1)] * edge[0]
        chigh = zhalo[1, 0, pl.ds(y, 1)] * edge[1]
        vlow = zhalo[0, 1, pl.ds(y, 1)] * edge[0]
        vhigh = zhalo[1, 1, pl.ds(y, 1)] * edge[1]
        csum = beside(c, cpad[y], cpad[y + 2], clow, chigh)
        vsum = beside(v, vpad[y], vpad[y + 2], vlow, vhigh)
        usum = beside(u, upad[y], upad[y + 2], clow * vlow, chigh * vhigh)
        diagonal = lookup(label[y], uptake) + 3.0 * c + 0.5 * csum
        residual = source[y] - (diagonal * v - 0.5 * (c * vsum + usum))
        tiles[y] = residual.astype(jnp.bfloat16).astype(jnp.float32)
        weight[y] = OMEGA / diagonal
        return carry

    lax.fori_loop(0, rows, plane, 0, unroll=2)

    def product(p, carry):
        terms = got[p].astype(jnp.float32) * tiles[send[p]]
        folded = terms[:, :LANES] + terms[:, LANES:]
        sums[pl.ds(p, 1)] = jnp.sum(folded, axis=0, keepdims=True)
        return carry

    lax.fori_loop(0, SLABS, product, 0, unroll=8)
    products = jnp.sum(sums[...], axis=1, keepdims=True)

    lane = lax.broadcasted_iota(jnp.int32, (SLABS, LANES), 1)

    def owner_rows(row):
        return jnp.concatenate(
            [table[pl.ds((x * YS + tile) * NEAR * 4 + row, NEAR, stride=4), :] for x in range(XS)], axis=0
        )

    first, second = owner_rows(1), owner_rows(3)
    half = SLABS // 2
    picked = jnp.where((lane == 96 + slab) & (slab < half), first, 0.0)
    picked = picked + jnp.where((lane == 80 + slab - half) & (slab >= half), second, 0.0)
    cell = jnp.sum(picked, axis=1, keepdims=True).astype(jnp.int32)
    index = jnp.sum(jnp.where(lane == 88 + cell, first, 0.0), axis=1, keepdims=True).astype(jnp.int32)
    target[...] = jnp.broadcast_to(index, (SLABS, LANES))
    for g in range(partial.shape[0]):
        hit = jnp.where(index == g * LANES + lane, products, 0.0)
        partial[pl.ds(g, 1)] = jnp.sum(hit, axis=0, keepdims=True)


def residual_products(edge, diffusivity, uptake, send, where, value, source, label, zhalo, yhalo, got, table, cells):
    rows, depth, width = value.shape
    block = jax.ShapeDtypeStruct(value.shape, jnp.float32)
    padded = pltpu.VMEM((rows + 2, depth, width), jnp.float32)
    return pl.pallas_call(
        residual_kernel,
        out_shape=(
            jax.ShapeDtypeStruct((cells // LANES, LANES), jnp.float32),
            jax.ShapeDtypeStruct((SLABS, LANES), jnp.int32),
            block,
            block,
        ),
        in_specs=[SMEM] * 5 + [VMEM] * 7,
        out_specs=(VMEM,) * 4,
        scratch_shapes=[padded, padded, padded, pltpu.VMEM(value.shape, jnp.float32),
                        pltpu.VMEM((SLABS, LANES), jnp.float32)],
        compiler_params=pltpu.CompilerParams(vmem_limit_bytes=40 << 20),
        name="residual",
    )(edge, diffusivity, uptake, send, where, value, source, label, zhalo, yhalo, got, table)


def total_kernel(part, out, near_buf, far_buf, n_send, n_recv, f_send, f_recv):
    slab, tile = lax.axis_index("slab"), lax.axis_index("tile")
    z, x, core = split_slab(slab)
    near = z * CORES + core
    far = x * YS + tile
    barrier = pltpu.get_barrier_semaphore()

    def loop(low, high, act):
        def body(k, carry):
            act(k)
            return carry
        lax.fori_loop(low, high, body, 0)

    def near_device(k):
        return near_slab(lax.rem(near + k, NEAR), x), tile

    def far_device(k):
        to = lax.rem(far + k, FAR)
        return far_slab(to, z, core), to % YS

    loop(1, NEAR, lambda k: pl.semaphore_signal(barrier, inc=1, device_id=near_device(k), device_id_type=MESH))
    loop(1, FAR, lambda k: pl.semaphore_signal(barrier, inc=1, device_id=far_device(k), device_id_type=MESH))
    near_buf[near] = part[...]
    pl.semaphore_wait(barrier, NEAR + FAR - 2)

    def near_copy(k):
        return remote(near_buf.at[near], near_buf.at[near], n_send.at[k], n_recv.at[k], *near_device(k))

    def far_copy(k):
        return remote(far_buf.at[far], far_buf.at[far], f_send.at[k], f_recv.at[k], *far_device(k))

    loop(1, NEAR, lambda k: near_copy(k).start())
    loop(1, NEAR, lambda k: near_copy(k).wait())
    far_buf[far] = jnp.sum(near_buf[...], axis=0)
    loop(1, FAR, lambda k: far_copy(k).start())
    loop(1, FAR, lambda k: far_copy(k).wait())
    out[...] = jnp.sum(far_buf[...], axis=0)


def total(part):
    return pl.pallas_call(
        total_kernel,
        out_shape=jax.ShapeDtypeStruct(part.shape, part.dtype),
        in_specs=[VMEM],
        out_specs=VMEM,
        scratch_shapes=[
            pltpu.VMEM((NEAR,) + part.shape, part.dtype),
            pltpu.VMEM((FAR,) + part.shape, part.dtype),
            pltpu.SemaphoreType.DMA((NEAR,)), pltpu.SemaphoreType.DMA((NEAR,)),
            pltpu.SemaphoreType.DMA((FAR,)), pltpu.SemaphoreType.DMA((FAR,)),
        ],
        compiler_params=pltpu.CompilerParams(collective_id=1, has_side_effects=True),
        name="total",
    )(part)


def pick(state, index):
    high, low = index // LANES, index % LANES
    result = jnp.zeros(index.shape, jnp.float32)
    for g in range(state.shape[0]):
        source = jnp.broadcast_to(state[g:g + 1], index.shape)
        found = jnp.take_along_axis(source, low, axis=1, mode="promise_in_bounds")
        result = jnp.where(high == g, found, result)
    return result


def solve_kernel(nnz, send, rhs, table, target, own, value, got, corrected, correction, diag, spread):
    groups = rhs.shape[0]
    rows = lax.broadcasted_iota(jnp.int32, (NEAR, LANES), 0)
    lane = lax.broadcasted_iota(jnp.int32, (NEAR, LANES), 1)
    diagonal_of = rows == lane // 8
    used = lane < (nnz - 16) * 8
    is_diag = lane // 8 == nnz - 16

    def part(g, row):
        return table[pl.ds(g * NEAR * 4 + row, NEAR, stride=4), :]

    def squeeze(values):
        for shift in (8, 16, 32, 64):
            values = values + pltpu.roll(values, shift, 1)
        return jnp.sum(jnp.where(diagonal_of, values, 0.0), axis=0, keepdims=True)

    for g in range(groups):
        diag[pl.ds(g, 1)] = squeeze(jnp.where(is_diag, part(g, 1), 0.0))

    def sweep(repeat, state):
        new = []
        for g in range(groups):
            first = part(g, 0) * pick(state, part(g, 2).astype(jnp.int32))
            second = jnp.where(used, part(g, 1), 0.0) * pick(state, part(g, 3).astype(jnp.int32))
            new.append(squeeze(first + second))
        return (rhs[...] - jnp.concatenate(new, axis=0)) / diag[...]

    state = lax.fori_loop(0, COARSE_SWEEPS - 1, sweep, rhs[...] / diag[...])
    correction[...] = pick(state, own[...])
    spread[...] = pick(state, target[...])
    corrected[...] = value[...]

    def deposit(p, carry):
        factor = spread[pl.ds(p, 1)]
        factor = jnp.concatenate([factor, factor], axis=1)
        term = (factor * got[p].astype(jnp.float32)).astype(jnp.bfloat16).astype(jnp.float32)
        at = send[p]
        corrected[at] = corrected[at] + term
        return carry

    lax.fori_loop(0, SLABS, deposit, 0, unroll=4)


def solve(nnz, send, rhs, table, target, own, value, got):
    return pl.pallas_call(
        functools.partial(solve_kernel, nnz),
        out_shape=(
            jax.ShapeDtypeStruct(value.shape, jnp.float32),
            jax.ShapeDtypeStruct(own.shape, jnp.float32),
        ),
        in_specs=[SMEM] + [VMEM] * 6,
        out_specs=(VMEM,) * 2,
        scratch_shapes=[pltpu.VMEM(rhs.shape, jnp.float32), pltpu.VMEM((SLABS, LANES), jnp.float32)],
        compiler_params=pltpu.CompilerParams(vmem_limit_bytes=32 << 20),
        name="solve",
    )(send, rhs, table, target, own, value, got)


def smooth_kernel(corrected, source, conduct, weight, zhalo, yhalo, out,
                  fields, couple, zsend, zrecv, yrecv, send_sem, recv_sem):
    slab, tile = lax.axis_index("slab"), lax.axis_index("tile")
    rows, depth, width = corrected.shape
    up_slab, down_slab = lax.rem(slab + 1, SLABS), lax.rem(slab + SLABS - 1, SLABS)
    up_tile, down_tile = lax.rem(tile + 1, YS), lax.rem(tile + YS - 1, YS)
    around = ((up_slab, tile), (down_slab, tile), (slab, up_tile), (slab, down_tile))
    barrier = pltpu.get_barrier_semaphore()
    for device in around:
        pl.semaphore_signal(barrier, inc=1, device_id=device, device_id_type=MESH)
    pl.semaphore_wait(barrier, 4)

    has_low = jnp.where(slab > 0, 1.0, 0.0)
    has_high = jnp.where(slab < SLABS - 1, 1.0, 0.0)
    has_below = jnp.where(tile > 0, 1.0, 0.0)
    has_above = jnp.where(tile < YS - 1, 1.0, 0.0)

    for step in range(SMOOTH_SWEEPS):
        now = corrected if step == 0 else fields
        later = fields if step == 0 else out

        def pack(y, carry):
            plane = now[y]
            zsend[step, 0, pl.ds(y, 1)] = plane[0:1]
            zsend[step, 1, pl.ds(y, 1)] = plane[depth - 1:depth]
            return carry

        lax.fori_loop(0, rows, pack, 0, unroll=4)
        copies = (
            remote(zsend.at[step, 1], zrecv.at[step, 0], send_sem.at[step, 0], recv_sem.at[step, 0], *around[0]),
            remote(zsend.at[step, 0], zrecv.at[step, 1], send_sem.at[step, 1], recv_sem.at[step, 1], *around[1]),
            remote(now.at[rows - 1], yrecv.at[step, 0], send_sem.at[step, 2], recv_sem.at[step, 2], *around[2]),
            remote(now.at[0], yrecv.at[step, 1], send_sem.at[step, 3], recv_sem.at[step, 3], *around[3]),
        )
        for copy in copies:
            copy.start()

        def product(y, carry):
            couple[y + 1] = conduct[y] * now[y]
            return carry

        lax.fori_loop(0, rows, product, 0, unroll=4)
        for copy in copies:
            copy.wait()
        below = yrecv[step, 0] * has_below
        above = yrecv[step, 1] * has_above
        couple[0] = below * yhalo[0, 0]
        couple[rows + 1] = above * yhalo[1, 0]

        def relax(y, under, over):
            v = now[y]
            vlow = zrecv[step, 0, pl.ds(y, 1)] * has_low
            vhigh = zrecv[step, 1, pl.ds(y, 1)] * has_high
            vsum = beside(v, under, over, vlow, vhigh)
            usum = beside(couple[y + 1], couple[y], couple[y + 2],
                          zhalo[0, 0, pl.ds(y, 1)] * vlow, zhalo[1, 0, pl.ds(y, 1)] * vhigh)
            coupled = 0.5 * (conduct[y] * vsum + usum)
            later[y] = (1.0 - OMEGA) * v + weight[y] * (source[y] + coupled)

        def inner(y, carry):
            relax(y, now[y - 1], now[y + 1])
            return carry

        relax(0, below, now[1])
        lax.fori_loop(1, rows - 1, inner, 0, unroll=2)
        relax(rows - 1, now[rows - 2], above)


def smooth(corrected, source, conduct, weight, zhalo, yhalo):
    rows, depth, width = corrected.shape
    return pl.pallas_call(
        smooth_kernel,
        out_shape=jax.ShapeDtypeStruct(corrected.shape, jnp.float32),
        in_specs=[VMEM] * 6,
        out_specs=VMEM,
        scratch_shapes=[
            pltpu.VMEM(corrected.shape, jnp.float32),
            pltpu.VMEM((rows + 2, depth, width), jnp.float32),
            pltpu.VMEM((SMOOTH_SWEEPS, 2, rows, width), jnp.float32),
            pltpu.VMEM((SMOOTH_SWEEPS, 2, rows, width), jnp.float32),
            pltpu.VMEM((SMOOTH_SWEEPS, 2, depth, width), jnp.float32),
            pltpu.SemaphoreType.DMA((SMOOTH_SWEEPS, 4)),
            pltpu.SemaphoreType.DMA((SMOOTH_SWEEPS, 4)),
        ],
        compiler_params=pltpu.CompilerParams(collective_id=2, has_side_effects=True, vmem_limit_bytes=32 << 20),
        name="smooth",
    )(corrected, source, conduct, weight, zhalo, yhalo)


def shards(solution, source, phase_label, phase_diffusivity, phase_uptake, send_tiles, support_slot, support_len,
           coarse_ids, basis_values, coarse_diag, coarse_off, coarse_cols):
    rows, depth, width = solution.shape
    cell_count, support_count, voxels = basis_values.shape
    entries = cell_count * support_count
    nnz = coarse_off.shape[1]
    cells = cell_count * NEAR * FAR
    slab, tile = lax.axis_index("slab"), lax.axis_index("tile")

    slots = support_slot.reshape(entries)
    entry_cell = jnp.arange(entries) // support_count
    live = (jnp.arange(support_count)[None, :] < support_len.reshape(cell_count)[:, None]).reshape(entries)
    chosen = slots[None, :] == jnp.arange(entries)[:, None]
    selector = (chosen & live[None, :]).astype(jnp.bfloat16)
    slot_cell = jnp.sum(jnp.where(chosen, entry_cell[None, :], 0), axis=1)
    sent = jnp.dot(selector, basis_values.reshape(entries, voxels), preferred_element_type=jnp.float32)
    sent = sent.astype(jnp.bfloat16).reshape(entries, depth, width)

    ids = place_of(coarse_ids)
    cols = place_of(coarse_cols)
    held = slot_cell.astype(jnp.float32).reshape(2, 4, 8)
    meta = jnp.concatenate([
        coarse_off.T, coarse_diag[None], ids.astype(jnp.float32)[None], held[0],
        cols.T.astype(jnp.float32), held[1], jnp.zeros((32 - nnz - 4, 8), jnp.float32),
    ], axis=0).reshape(4, LANES)

    def zfaces(block):
        return jnp.stack([block[:, 0], block[:, -1]])

    def yfaces(block):
        return jnp.stack([block[0], block[-1]])

    def look(label):
        result = jnp.zeros(label.shape, jnp.float32)
        for category in range(phase_diffusivity.shape[0]):
            result = result + jnp.where(label == category, phase_diffusivity[category], 0.0)
        return result

    zface = jnp.stack([look(zfaces(phase_label)), zfaces(solution)], axis=1)
    yface = jnp.stack([look(yfaces(phase_label)), yfaces(solution)], axis=1)
    got, zhalo, yhalo, table = exchange(sent, zface, yface, meta)
    table = table.reshape(NEAR * FAR * 4, LANES)

    edge = jnp.stack([slab > 0, slab < SLABS - 1, tile > 0, tile < YS - 1]).astype(jnp.float32)
    send = send_tiles.reshape(ZS, XS, CORES).transpose(1, 0, 2).reshape(SLABS)
    where = jnp.stack([slab, tile]).astype(jnp.int32)
    partial, target, conduct, weight = residual_products(
        edge, phase_diffusivity, phase_uptake, send, where, solution, source, phase_label,
        zhalo, yhalo, got, table, cells)
    restricted = total(partial)
    own = jnp.broadcast_to(ids[:, None], (cell_count, LANES))
    corrected, correction = solve(nnz, send, restricted, table, target, own, solution, got)
    new_solution = smooth(corrected, source, conduct, weight, zhalo, yhalo)
    return new_solution, correction[:, 0]


def solution(mesh):
    placed = (
        P("tile", "slab", None),
        P("tile", "slab", None),
        P("tile", "slab", None),
        P(),
        P(),
        P("slab", "tile", None, None),
        P("slab", "tile", None),
        P("slab", "tile", None),
        P(("slab", "tile")),
        P(("slab", "tile"), None, None),
        P(("slab", "tile")),
        P(("slab", "tile"), None),
        P(("slab", "tile"), None),
    )
    return jax.shard_map(
        shards,
        mesh=mesh,
        in_specs=placed,
        out_specs=(P("tile", "slab", None), P(("slab", "tile"))),
        check_vma=False,
    )
```

```python
import functools

import jax
import jax.numpy as jnp
from jax import lax
from jax.experimental import pallas as pl
from jax.experimental.pallas import tpu as pltpu
from jax.sharding import PartitionSpec as P

COARSE_SWEEPS = 4
SMOOTH_SWEEPS = 2
OMEGA = 0.8
MESH = pl.DeviceIdType.MESH
LANES = 128
FULL = 32760.0

ZS, XS, CORES, YS = 8, 4, 2, 4
NEAR = ZS * CORES
FAR = XS * YS
SLABS = ZS * XS * CORES


def split_slab(slab):
    return slab >> 3, (slab >> 1) & 3, slab & 1


def near_device(near, x, tile):
    return ((near >> 1) << 3) | (x << 1) | (near & 1), tile


def far_device(far, z, core):
    return (z << 3) | ((far >> 2) << 1) | core, far & 3


def ordered_slab(order):
    return near_device(order & (NEAR - 1), order >> 4, 0)[0]


def place_of(index):
    owner, row = index >> 3, index & 7
    slab, tile = owner >> 2, owner & 3
    z, x, core = split_slab(slab)
    return (((((x << 2) | tile) << 4) | (z << 1) | core) << 3) | row


VMEM = pl.BlockSpec(memory_space=pltpu.VMEM)
SMEM = pl.BlockSpec(memory_space=pltpu.SMEM)


def remote(src, dst, send_sem, recv_sem, device):
    return pltpu.make_async_remote_copy(
        src_ref=src, dst_ref=dst, send_sem=send_sem, recv_sem=recv_sem,
        device_id=device, device_id_type=MESH,
    )


def loop(low, high, act, unroll=1):
    def body(k, carry):
        act(k)
        return carry
    lax.fori_loop(low, high, body, 0, unroll=unroll)


def lane_gather(source, index):
    numbers = lax.GatherDimensionNumbers(
        offset_dims=(), collapsed_slice_dims=(1,), start_index_map=(1,),
        operand_batching_dims=(0,), start_indices_batching_dims=(0,),
    )
    return lax.gather(source, index[..., None], numbers, (1, 1), mode=lax.GatherScatterMode.PROMISE_IN_BOUNDS)


def beside(mid, below, above, zlow, zhigh):
    depth, width = mid.shape
    zi = lax.broadcasted_iota(jnp.int32, mid.shape, 0)
    xi = lax.broadcasted_iota(jnp.int32, mid.shape, 1)
    total = below + above
    total = total + jnp.where(zi == 0, zlow, pltpu.roll(mid, 1, 0))
    total = total + jnp.where(zi == depth - 1, zhigh, pltpu.roll(mid, depth - 1, 0))
    total = total + jnp.where(xi == 0, 0.0, pltpu.roll(mid, 1, 1))
    total = total + jnp.where(xi == width - 1, 0.0, pltpu.roll(mid, width - 1, 1))
    return total


def lookup(label, table):
    result = jnp.full(label.shape, table[0], jnp.float32)
    for category in range(1, table.shape[0]):
        result = jnp.where(label == category, table[category], result)
    return result


def restrict_kernel(nnz, diffusivity, uptake, send, slot, length, ids, diag, slot_row, off, cols,
                    value, source, label, basis,
                    summed, target, selector, conduct, weight, zhalo, yhalo, table, turned,
                    sent, got, zface, yface, meta, pieces, cpad, vpad, upad, tiles, sums, near_buf, far_buf,
                    a_send, a_recv, n_send, n_recv, f_send, f_recv, h_send, h_recv, own,
                    s_send, s_recv, t_send, t_recv):
    rows, depth, width = value.shape
    slab, tile = lax.axis_index("slab"), lax.axis_index("tile")
    z, x, core = split_slab(slab)
    near = (z << 1) | core
    far = (x << 2) | tile
    order = (x << 4) | near
    place = (far << 4) | near

    barrier = pltpu.get_barrier_semaphore()

    def to_near(k):
        return near_device((near + k) & (NEAR - 1), x, tile)

    def to_far(k):
        return far_device((far + k) & (FAR - 1), z, core)

    def to_slab(k):
        return (slab + k) & (SLABS - 1), tile

    def greet(device):
        pl.semaphore_signal(barrier, inc=1, device_id=device, device_id_type=MESH)

    loop(1, SLABS, lambda k: greet(to_slab(k)))
    loop(0, XS * (YS - 1), lambda k: greet(
        ((z << 3) | (((x + k) & 3) << 1) | core, (tile + 1 + (k >> 2)) & (YS - 1))))

    def fill(y):
        c = lookup(label[y], diffusivity)
        v = value[y]
        cpad[y + 1] = c
        vpad[y + 1] = v
        upad[y + 1] = c * v
        conduct[y] = c
        zface[0, 0, pl.ds(y, 1)] = c[0:1]
        zface[1, 0, pl.ds(y, 1)] = c[depth - 1:depth]
        zface[0, 1, pl.ds(y, 1)] = v[0:1]
        zface[1, 1, pl.ds(y, 1)] = v[depth - 1:depth]

    loop(0, rows, fill, 4)
    for side, at in ((0, 1), (1, rows)):
        yface[side, 0] = cpad[at]
        yface[side, 1] = vpad[at]

    lane8 = lax.broadcasted_iota(jnp.int32, (8, LANES), 1)
    row8 = lax.broadcasted_iota(jnp.int32, (8, LANES), 0)
    lane1 = lax.broadcasted_iota(jnp.int32, (1, LANES), 1)
    entry = jnp.minimum(((row8 & 1) << 4) + (lane8 >> 3), nnz - 1)
    blank = jnp.zeros((8, LANES - nnz), jnp.float32)
    wide_off = jnp.concatenate([off[...], blank], axis=1)
    wide_cols = jnp.concatenate([place_of(cols[...]).astype(jnp.float32), blank], axis=1)
    offs = jnp.zeros((8, LANES), jnp.float32)
    places = jnp.zeros((8, LANES), jnp.float32)
    diag_row = jnp.zeros((1, LANES), jnp.float32)
    id_row = jnp.zeros((1, LANES), jnp.int32)
    for r in range(8):
        mine = (lane8 & 7) == r
        offs = jnp.where(mine, lane_gather(jnp.broadcast_to(wide_off[r:r + 1], (8, LANES)), entry), offs)
        places = jnp.where(mine, lane_gather(jnp.broadcast_to(wide_cols[r:r + 1], (8, LANES)), entry), places)
        diag_row = jnp.where((lane1 & 7) == r, diag[r], diag_row)
        id_row = jnp.where((lane1 & 7) == r, place_of(ids[r]), id_row)
    slot_cell = jnp.zeros((1, LANES), jnp.int32)
    for e in range(SLABS):
        slot_cell = jnp.where(lane1 == slot[0, 0, e], e >> 3, slot_cell)
    held = slot_cell.astype(jnp.float32)
    group = lane1 >> 3
    second = offs[1:2]
    second = jnp.where(group == nnz - 16, diag_row, second)
    second = jnp.where(group == nnz - 15, id_row.astype(jnp.float32), second)
    second = jnp.where(group >= 12, pltpu.roll(held, 96, 1), second)
    fourth = jnp.where(group >= nnz - 16, pltpu.roll(held, 48, 1), places[1:2])
    meta[0:1] = offs[0:1]
    meta[1:2] = second
    meta[2:3] = places[0:1]
    meta[3:4] = fourth

    e_at = lax.broadcasted_iota(jnp.int32, (SLABS, SLABS), 1)
    m_at = lax.broadcasted_iota(jnp.int32, (SLABS, SLABS), 0)
    limit = jnp.zeros((SLABS, SLABS), jnp.int32)
    for c in range(8):
        limit = jnp.where((e_at >> 3) == c, length[0, 0, c], limit)
    chosen = (slot_row[0] == m_at) & ((e_at & 7) < limit)
    chooser = chosen.astype(jnp.float32).astype(jnp.bfloat16)

    def choose(k):
        at = pl.ds(pl.multiple_of(k * LANES, LANES), LANES)
        block = basis[:, :, at].astype(jnp.float32).reshape(SLABS, LANES).astype(jnp.bfloat16)
        pieces[k & 1, pl.ds(k >> 1, SLABS, stride=depth), :] = jnp.dot(
            chooser, block, preferred_element_type=jnp.float32)

    loop(0, 2 * depth, choose, 4)

    def settle(m):
        for h in range(2):
            sent[m, :, h * LANES:(h + 1) * LANES] = pieces[h, pl.ds(m * depth, depth), :].astype(jnp.bfloat16)

    loop(0, SLABS, settle, 4)
    pl.semaphore_wait(barrier, SLABS - 1 + XS * (YS - 1))

    halos = (
        remote(zface.at[1], zhalo.at[0], h_send.at[0], h_recv.at[0], to_slab(1)),
        remote(zface.at[0], zhalo.at[1], h_send.at[1], h_recv.at[1], to_slab(SLABS - 1)),
        remote(yface.at[1], yhalo.at[0], h_send.at[2], h_recv.at[2], (slab, (tile + 1) & 3)),
        remote(yface.at[0], yhalo.at[1], h_send.at[3], h_recv.at[3], (slab, (tile + 3) & 3)),
    )
    mine = pltpu.make_async_copy(meta, table.at[place], own.at[0])
    mine.start()
    kept = pltpu.make_async_copy(sent.at[slab], got.at[order], own.at[1])
    kept.start()
    block = table.at[pl.ds(far * NEAR, NEAR)]

    def near_copy(k):
        return remote(meta, table.at[place], n_send.at[k], n_recv.at[k], to_near(k))

    def far_copy(k):
        return remote(block, block, f_send.at[k], f_recv.at[k], to_far(k))

    def basis_copy(k):
        return remote(sent.at[(slab + k) & (SLABS - 1)], got.at[order], a_send.at[k], a_recv.at[k], to_slab(k))

    loop(1, NEAR, lambda k: near_copy(k).start())
    for copy in halos:
        copy.start()
    loop(1, SLABS, lambda k: basis_copy(k).start())
    mine.wait()
    kept.wait()
    loop(1, NEAR, lambda k: near_copy(k).wait())
    loop(1, FAR, lambda k: far_copy(k).start())
    for copy in halos:
        copy.wait()

    has_low = jnp.where(slab > 0, 1.0, 0.0)
    has_high = jnp.where(slab < SLABS - 1, 1.0, 0.0)
    for side, at, flag in ((0, 0, jnp.where(tile > 0, 1.0, 0.0)), (1, rows + 1, jnp.where(tile < YS - 1, 1.0, 0.0))):
        c = yhalo[side, 0] * flag
        v = yhalo[side, 1] * flag
        cpad[at] = c
        vpad[at] = v
        upad[at] = c * v

    def plane(y):
        c, v, u = cpad[y + 1], vpad[y + 1], upad[y + 1]
        clow = zhalo[0, 0, pl.ds(y, 1)] * has_low
        chigh = zhalo[1, 0, pl.ds(y, 1)] * has_high
        vlow = zhalo[0, 1, pl.ds(y, 1)] * has_low
        vhigh = zhalo[1, 1, pl.ds(y, 1)] * has_high
        csum = beside(c, cpad[y], cpad[y + 2], clow, chigh)
        vsum = beside(v, vpad[y], vpad[y + 2], vlow, vhigh)
        usum = beside(u, upad[y], upad[y + 2], clow * vlow, chigh * vhigh)
        diagonal = lookup(label[y], uptake) + 3.0 * c + 0.5 * csum
        residual = source[y] - (diagonal * v - 0.5 * (c * vsum + usum))
        tiles[y] = residual.astype(jnp.bfloat16).astype(jnp.float32)
        weight[y] = OMEGA / diagonal

    loop(0, rows, plane, 2)

    row_at = lax.broadcasted_iota(jnp.int32, (rows, LANES), 0)
    lane_at = lax.broadcasted_iota(jnp.int32, (rows, LANES), 1)
    to_row = jnp.full((rows, LANES), -1, jnp.int32)
    for p in range(SLABS):
        to_row = jnp.where(lane_at == p, send[0, 0, 0, ordered_slab(p)], to_row)
    selector[...] = jnp.where(to_row == row_at, 1.0, 0.0)

    loop(1, FAR, lambda k: far_copy(k).wait())
    lane = lax.broadcasted_iota(jnp.int32, (NEAR, LANES), 1)
    for x_from in range(XS):
        own_rows = table[pl.ds(((x_from << 2) | tile) << 4, NEAR)]
        first, second = own_rows[:, 1], own_rows[:, 3]
        picked = jnp.where((lane == 96 + slab) & (slab < 32), first, 0.0)
        picked = picked + jnp.where((lane == 48 + slab) & (slab >= 32), second, 0.0)
        cell = jnp.sum(picked, axis=1, keepdims=True).astype(jnp.int32)
        index = jnp.sum(jnp.where(lane == 88 + cell, first, 0.0), axis=1, keepdims=True).astype(jnp.int32)
        target[x_from * NEAR:(x_from + 1) * NEAR, :] = jnp.broadcast_to(index, (NEAR, LANES))

    loop(1, SLABS, lambda k: basis_copy(k).wait())

    def product(p):
        terms = got[p].astype(jnp.float32) * tiles[send[0, 0, 0, ordered_slab(p)]]
        folded = terms[:, :LANES] + terms[:, LANES:]
        sums[pl.ds(p, 1)] = jnp.sum(folded, axis=0, keepdims=True)

    loop(0, SLABS, product, 8)
    products = jnp.broadcast_to(jnp.sum(sums[...], axis=1, keepdims=True), (SLABS, LANES))
    lane64 = lax.broadcasted_iota(jnp.int32, (SLABS, LANES), 1)
    for g in range(summed.shape[0]):
        hit = jnp.where(target[...] == g * LANES + lane64, products, 0.0)
        near_buf[near, pl.ds(g, 1)] = jnp.sum(hit, axis=0, keepdims=True)

    def near_part(k):
        return remote(near_buf.at[near], near_buf.at[near], s_send.at[k], s_recv.at[k], to_near(k))

    def far_part(k):
        return remote(far_buf.at[far], far_buf.at[far], t_send.at[k], t_recv.at[k], to_far(k))

    loop(1, NEAR, lambda k: near_part(k).start())

    def unfold(p):
        for h in range(2):
            pieces[h, pl.ds(p * depth, depth), :] = got[p, :, h * LANES:(h + 1) * LANES].astype(jnp.float32)

    loop(0, SLABS, unfold, 4)
    loop(1, NEAR, lambda k: near_part(k).wait())
    far_buf[far] = jnp.sum(near_buf[...], axis=0)
    loop(1, FAR, lambda k: far_part(k).start())

    def turn(k):
        turned[k] = pieces[k & 1, pl.ds(k >> 1, SLABS, stride=depth), :].astype(jnp.bfloat16)

    loop(0, 2 * depth, turn, 4)
    loop(1, FAR, lambda k: far_part(k).wait())
    summed[...] = jnp.sum(far_buf[...], axis=0)


def restrict(nnz, cells, diffusivity, uptake, send, slot, length, ids, diag, off, cols, value, source, label, basis):
    rows, depth, width = value.shape
    f32, bf16 = jnp.float32, jnp.bfloat16
    shape = jax.ShapeDtypeStruct
    padded = pltpu.VMEM((rows + 2, depth, width), f32)
    dma = pltpu.SemaphoreType.DMA
    groups = cells // LANES
    return pl.pallas_call(
        functools.partial(restrict_kernel, nnz),
        out_shape=(
            shape((groups, LANES), f32),
            shape((SLABS, LANES), jnp.int32),
            shape((rows, LANES), f32),
            shape(value.shape, f32),
            shape(value.shape, f32),
            shape((2, 2, rows, width), f32),
            shape((2, 2, depth, width), f32),
            shape((NEAR * FAR, 4, LANES), f32),
            shape((2 * depth, SLABS, LANES), bf16),
        ),
        in_specs=[SMEM] * 7 + [VMEM] * 7,
        out_specs=(VMEM,) * 9,
        scratch_shapes=[
            pltpu.VMEM((SLABS, depth, width), bf16), pltpu.VMEM((SLABS, depth, width), bf16),
            pltpu.VMEM((2, 2, rows, width), f32), pltpu.VMEM((2, 2, depth, width), f32),
            pltpu.VMEM((4, LANES), f32), pltpu.VMEM((2, SLABS * depth, LANES), f32),
            padded, padded, padded, pltpu.VMEM(value.shape, f32), pltpu.VMEM((SLABS, LANES), f32),
            pltpu.VMEM((NEAR, groups, LANES), f32), pltpu.VMEM((FAR, groups, LANES), f32),
            dma((SLABS,)), dma((SLABS,)), dma((NEAR,)), dma((NEAR,)), dma((FAR,)), dma((FAR,)),
            dma((4,)), dma((4,)), dma((2,)), dma((NEAR,)), dma((NEAR,)), dma((FAR,)), dma((FAR,)),
        ],
        compiler_params=pltpu.CompilerParams(collective_id=0, has_side_effects=True, vmem_limit_bytes=40 << 20),
        name="restrict",
    )(diffusivity, uptake, send, slot, length, ids, diag, slot, off, cols, value, source, label, basis)


def finish_kernel(nnz, ids, rhs, target, selector, conduct, weight, zhalo, yhalo, table, turned, value, source,
                  out, correction, state, diag, packed, low, high, factor, lift, first_pad, second_pad, couple,
                  zgain, ygain, zsend, zrecv, yrecv, send_sem, recv_sem):
    rows, depth, width = value.shape
    groups = rhs.shape[0]
    slab, tile = lax.axis_index("slab"), lax.axis_index("tile")
    around = (((slab + 1) & (SLABS - 1), tile), ((slab + SLABS - 1) & (SLABS - 1), tile),
              (slab, (tile + 1) & 3), (slab, (tile + 3) & 3))
    barrier = pltpu.get_barrier_semaphore()
    for device in around:
        pl.semaphore_signal(barrier, inc=1, device_id=device, device_id_type=MESH)

    row_at = lax.broadcasted_iota(jnp.int32, (NEAR, LANES), 0)
    lane = lax.broadcasted_iota(jnp.int32, (NEAR, LANES), 1)
    mine = row_at == lane >> 3
    used = lane < (nnz - 16) * 8
    is_diag = lane >> 3 == nnz - 16

    def squeeze(values):
        for shift in (8, 16, 32, 64):
            values = values + pltpu.roll(values, shift, 1)
        return jnp.sum(jnp.where(mine, values, 0.0), axis=0, keepdims=True)

    def prepare(g):
        block = table[pl.ds(g * NEAR, NEAR)]
        second = block[:, 1]
        diag[pl.ds(g, 1)] = squeeze(jnp.where(is_diag, second, 0.0))
        factor[0, g] = block[:, 0]
        factor[1, g] = jnp.where(used, second, 0.0)
        for b in range(2):
            index = block[:, 2 + b].astype(jnp.int32)
            low[b, g] = index & (LANES - 1)
            high[b, g] = index >> 7

    loop(0, groups, prepare, 2)
    state[...] = rhs[...] / diag[...]

    def pick(b, g, half):
        rows_at = slice(half * 8, half * 8 + 8)
        at, row = low[b, g, rows_at], high[b, g, rows_at]
        found = [lane_gather(packed[q], at) for q in range(8)]
        bit = 1
        while len(found) > 1:
            odd = (row & bit) != 0
            found = [jnp.where(odd, found[2 * i + 1], found[2 * i]) for i in range(len(found) // 2)]
            bit = bit * 2
        word = found[0]
        number = jnp.where((row & 8) != 0, word >> 16, (word << 16) >> 16)
        return number.astype(jnp.float32) * factor[b, g, rows_at]

    for repeat in range(COARSE_SWEEPS - 1):
        now = state[...]
        top = jnp.maximum(jnp.max(jnp.max(jnp.abs(now), axis=1, keepdims=True), axis=0, keepdims=True), 1e-34)
        whole = jnp.round(now * (FULL / top)).astype(jnp.int32)
        word = (whole[8:16] << 16) + (whole[0:8] & 0xFFFF)
        for q in range(8):
            packed[q] = jnp.broadcast_to(word[q:q + 1], (8, LANES))
        scale = top * (1.0 / FULL)

        def relax_group(g):
            total = jnp.concatenate([pick(0, g, half) + pick(1, g, half) for half in range(2)], axis=0)
            state[pl.ds(g, 1)] = (rhs[pl.ds(g, 1)] - squeeze(total) * scale) / diag[pl.ds(g, 1)]

        loop(0, groups, relax_group, 4)

    lane1 = lax.broadcasted_iota(jnp.int32, (8, LANES), 1)
    own = jnp.zeros((8, LANES), jnp.int32)
    for r in range(8):
        own = jnp.where(lane1 == r, place_of(ids[r]), own)
    found = jnp.zeros((8, LANES), jnp.float32)
    lane64 = lax.broadcasted_iota(jnp.int32, (SLABS, LANES), 1)
    here = jnp.zeros((SLABS, LANES), jnp.float32)
    for g in range(groups):
        line = state[pl.ds(g, 1)]
        taken = lane_gather(jnp.broadcast_to(line, (8, LANES)), own & (LANES - 1))
        found = jnp.where((own >> 7) == g, taken, found)
        here = jnp.where(target[...] - g * LANES == lane64, line, here)
    correction[...] = found[0:1, 0:8]
    scaled = jnp.broadcast_to(jnp.sum(here, axis=1, keepdims=True), (SLABS, LANES))

    chooser = selector[:, 0:SLABS].astype(jnp.bfloat16)

    def deposit(k):
        terms = (scaled * turned[k].astype(jnp.float32)).astype(jnp.bfloat16)
        lift[k & 1, pl.ds(k >> 1, rows, stride=depth), :] = jnp.dot(chooser, terms, preferred_element_type=jnp.float32)

    loop(0, 2 * depth, deposit, 4)
    none = jnp.zeros((depth, width), jnp.float32)
    for pad in (first_pad, second_pad, couple):
        pad[0] = none
        pad[rows + 1] = none

    def correct(y):
        at = pl.ds(y * depth, depth)
        v = value[y] + jnp.concatenate([lift[0, at, :], lift[1, at, :]], axis=1)
        first_pad[y + 1] = v
        couple[y + 1] = conduct[y] * v
        zsend[0, 0, pl.ds(y, 1)] = v[0:1]
        zsend[0, 1, pl.ds(y, 1)] = v[depth - 1:depth]

    loop(0, rows, correct, 4)
    pl.semaphore_wait(barrier, 4)

    for step in range(SMOOTH_SWEEPS):
        now = first_pad if step == 0 else second_pad
        copies = (
            remote(zsend.at[step, 1], zrecv.at[step, 0], send_sem.at[step, 0], recv_sem.at[step, 0], around[0]),
            remote(zsend.at[step, 0], zrecv.at[step, 1], send_sem.at[step, 1], recv_sem.at[step, 1], around[1]),
            remote(now.at[rows], yrecv.at[step, 0], send_sem.at[step, 2], recv_sem.at[step, 2], around[2]),
            remote(now.at[1], yrecv.at[step, 1], send_sem.at[step, 3], recv_sem.at[step, 3], around[3]),
        )
        for copy in copies:
            copy.start()

        if step == 0:
            for side, at, inside in ((0, 0, slab > 0), (1, depth - 1, slab < SLABS - 1)):
                flag = jnp.where(inside, 0.5, 0.0)

                def gain(y):
                    line = pl.ds(y, 1)
                    pair = conduct[y][at:at + 1] + zhalo[side, 0, line]
                    zgain[side, line] = weight[y][at:at + 1] * pair * flag

                loop(0, rows, gain, 4)
            for side, at, inside in ((0, 0, tile > 0), (1, rows - 1, tile < YS - 1)):
                flag = jnp.where(inside, 0.5, 0.0)
                ygain[side] = weight[at] * (conduct[at] + yhalo[side, 0]) * flag
        else:
            def product(y):
                couple[y + 1] = conduct[y] * now[y + 1]
            loop(0, rows, product, 4)

        def inner(y):
            v = now[y + 1]
            vsum = beside(v, now[y], now[y + 2], 0.0, 0.0)
            usum = beside(couple[y + 1], couple[y], couple[y + 2], 0.0, 0.0)
            coupled = 0.5 * (conduct[y] * vsum + usum)
            relaxed = (1.0 - OMEGA) * v + weight[y] * (source[y] + coupled)
            if step == 0:
                second_pad[y + 1] = relaxed
            else:
                out[y] = relaxed

        loop(0, rows, inner, 2)
        for copy in copies:
            copy.wait()
        later, shift = (second_pad, 1) if step == 0 else (out, 0)
        later[shift] = later[shift] + ygain[0] * yrecv[step, 0]
        later[shift + rows - 1] = later[shift + rows - 1] + ygain[1] * yrecv[step, 1]

        def close(y):
            line = pl.ds(y, 1)
            lowest = later[y + shift, 0:1] + zgain[0, line] * zrecv[step, 0, line]
            highest = later[y + shift, depth - 1:depth] + zgain[1, line] * zrecv[step, 1, line]
            later[y + shift, 0:1] = lowest
            later[y + shift, depth - 1:depth] = highest
            if step + 1 < SMOOTH_SWEEPS:
                zsend[step + 1, 0, line] = lowest
                zsend[step + 1, 1, line] = highest

        loop(0, rows, close, 4)


def finish(nnz, ids, rhs, target, selector, conduct, weight, zhalo, yhalo, table, turned, value, source):
    rows, depth, width = value.shape
    f32 = jnp.float32
    groups = rhs.shape[0]
    padded = pltpu.VMEM((rows + 2, depth, width), f32)
    half = (2, groups, NEAR, LANES)
    return pl.pallas_call(
        functools.partial(finish_kernel, nnz),
        out_shape=(jax.ShapeDtypeStruct(value.shape, f32), jax.ShapeDtypeStruct((1, 8), f32)),
        in_specs=[SMEM] + [VMEM] * 11,
        out_specs=(VMEM,) * 2,
        scratch_shapes=[
            pltpu.VMEM(rhs.shape, f32), pltpu.VMEM(rhs.shape, f32), pltpu.VMEM((8, 8, LANES), jnp.int32),
            pltpu.VMEM(half, jnp.int32), pltpu.VMEM(half, jnp.int32), pltpu.VMEM(half, f32),
            pltpu.VMEM((2, rows * depth, LANES), f32), padded, padded, padded,
            pltpu.VMEM((2, rows, width), f32), pltpu.VMEM((2, depth, width), f32),
            pltpu.VMEM((SMOOTH_SWEEPS, 2, rows, width), f32), pltpu.VMEM((SMOOTH_SWEEPS, 2, rows, width), f32),
            pltpu.VMEM((SMOOTH_SWEEPS, 2, depth, width), f32),
            pltpu.SemaphoreType.DMA((SMOOTH_SWEEPS, 4)), pltpu.SemaphoreType.DMA((SMOOTH_SWEEPS, 4)),
        ],
        compiler_params=pltpu.CompilerParams(collective_id=1, has_side_effects=True, vmem_limit_bytes=40 << 20),
        name="finish",
    )(ids, rhs, target, selector, conduct, weight, zhalo, yhalo, table, turned, value, source)


def shards(solution, source, phase_label, phase_diffusivity, phase_uptake, send_tiles, support_slot, support_len,
           coarse_ids, basis_values, coarse_diag, coarse_off, coarse_cols):
    nnz = coarse_off.shape[1]
    cells = basis_values.shape[0] * NEAR * FAR
    send = send_tiles.transpose(0, 1, 3, 2)
    rhs, target, selector, conduct, weight, zhalo, yhalo, table, turned = restrict(
        nnz, cells, phase_diffusivity, phase_uptake, send, support_slot, support_len, coarse_ids, coarse_diag,
        coarse_off, coarse_cols, solution, source, phase_label, basis_values)
    new_solution, correction = finish(
        nnz, coarse_ids, rhs, target, selector, conduct, weight, zhalo, yhalo, table, turned, solution, source)
    return new_solution, correction.reshape(correction.shape[1])


def solution(mesh):
    placed = (
        P("tile", "slab", None),
        P("tile", "slab", None),
        P("tile", "slab", None),
        P(),
        P(),
        P("slab", "tile", None, None),
        P("slab", "tile", None),
        P("slab", "tile", None),
        P(("slab", "tile")),
        P(("slab", "tile"), None, None),
        P(("slab", "tile")),
        P(("slab", "tile"), None),
        P(("slab", "tile"), None),
    )
    return jax.shard_map(
        shards,
        mesh=mesh,
        in_specs=placed,
        out_specs=(P("tile", "slab", None), P(("slab", "tile"))),
        check_vma=False,
    )
```

```python
import functools

import jax
import jax.numpy as jnp
from jax import lax
from jax.experimental import pallas as pl
from jax.experimental.pallas import tpu as pltpu
from jax.sharding import PartitionSpec as P

COARSE_SWEEPS = 4
SMOOTH_SWEEPS = 2
OMEGA = 0.8
MESH = pl.DeviceIdType.MESH
LANES = 128
FULL = 32760.0

ZS, XS, CORES, YS = 8, 4, 2, 4
NEAR = ZS * CORES
FAR = XS * YS
SLABS = ZS * XS * CORES


def split_slab(slab):
    return slab >> 3, (slab >> 1) & 3, slab & 1


def near_device(near, x, tile):
    return ((near >> 1) << 3) | (x << 1) | (near & 1), tile


def far_device(far, z, core):
    return (z << 3) | ((far >> 2) << 1) | core, far & 3


def ordered_slab(order):
    return near_device(order & (NEAR - 1), order >> 4, 0)[0]


def place_of(index):
    owner, row = index >> 3, index & 7
    slab, tile = owner >> 2, owner & 3
    z, x, core = split_slab(slab)
    return (((((x << 2) | tile) << 4) | (z << 1) | core) << 3) | row


VMEM = pl.BlockSpec(memory_space=pltpu.VMEM)
HBM = pl.BlockSpec(memory_space=pltpu.HBM)


def remote(src, dst, send_sem, recv_sem, device):
    return pltpu.make_async_remote_copy(
        src_ref=src, dst_ref=dst, send_sem=send_sem, recv_sem=recv_sem,
        device_id=device, device_id_type=MESH,
    )


def loop(low, high, act, unroll=1):
    def body(k, carry):
        act(k)
        return carry
    lax.fori_loop(low, high, body, 0, unroll=unroll)


def lane_gather(source, index):
    numbers = lax.GatherDimensionNumbers(
        offset_dims=(), collapsed_slice_dims=(1,), start_index_map=(1,),
        operand_batching_dims=(0,), start_indices_batching_dims=(0,),
    )
    return lax.gather(source, index[..., None], numbers, (1, 1), mode=lax.GatherScatterMode.PROMISE_IN_BOUNDS)


def beside(mid, below, above, zlow, zhigh):
    depth, width = mid.shape
    zi = lax.broadcasted_iota(jnp.int32, mid.shape, 0)
    xi = lax.broadcasted_iota(jnp.int32, mid.shape, 1)
    total = below + above
    total = total + jnp.where(zi == 0, zlow, pltpu.roll(mid, 1, 0))
    total = total + jnp.where(zi == depth - 1, zhigh, pltpu.roll(mid, depth - 1, 0))
    total = total + jnp.where(xi == 0, 0.0, pltpu.roll(mid, 1, 1))
    total = total + jnp.where(xi == width - 1, 0.0, pltpu.roll(mid, width - 1, 1))
    return total


def lookup(label, table):
    result = jnp.full(label.shape, table[0], jnp.float32)
    for category in range(1, table.shape[0]):
        result = jnp.where(label == category, table[category], result)
    return result


def cycle_kernel(nnz, diffusivity_h, uptake_h, send_h, slot_h, length_h, ids_h, diag_h, off_h, cols_h,
                 value_h, source_h, label_h, basis_h,
                 out, correction,
                 diffusivity, uptake, send, slot, length, ids, diag_own, slot_row, off, cols,
                 value, source, label, basis,
                 sent, got, zface, yface, zhalo, yhalo, meta, table, pieces, turned,
                 conduct, weight, cpad, vpad, upad, tiles, sums, near_buf, far_buf,
                 target, target_s, selector, state, rhs, diag, packed, low, high, factor,
                 last_low, last_high, last_factor, zgain, ygain, zsend, zrecv, yrecv,
                 load_sem, target_sem, a_send, a_recv, n_send, n_recv, f_send, f_recv, h_send, h_recv, own,
                 s_send, s_recv, t_send, t_recv, v_send, v_recv):
    rows, depth, width = value.shape
    groups = rhs.shape[0]
    slab, tile = lax.axis_index("slab"), lax.axis_index("tile")
    z, x, core = split_slab(slab)
    near = (z << 1) | core
    far = (x << 2) | tile
    order = (x << 4) | near
    place = (far << 4) | near

    barrier = pltpu.get_barrier_semaphore()

    def to_near(k):
        return near_device((near + k) & (NEAR - 1), x, tile)

    def to_far(k):
        return far_device((far + k) & (FAR - 1), z, core)

    def to_slab(k):
        return (slab + k) & (SLABS - 1), tile

    def greet(device):
        pl.semaphore_signal(barrier, inc=1, device_id=device, device_id_type=MESH)

    loads = [pltpu.make_async_copy(*pair, load_sem.at[i]) for i, pair in enumerate((
        (slot_h, slot), (length_h, length), (slot_h, slot_row), (basis_h, basis), (off_h, off), (cols_h, cols),
        (ids_h, ids), (diag_h, diag_own), (diffusivity_h, diffusivity), (uptake_h, uptake), (send_h, send),
        (label_h, label), (value_h, value), (source_h, source)))]
    for load in loads:
        load.start()
    loop(1, SLABS, lambda k: greet(to_slab(k)))
    loop(0, XS * (YS - 1), lambda k: greet(
        ((z << 3) | (((x + k) & 3) << 1) | core, (tile + 1 + (k >> 2)) & (YS - 1))))
    for load in loads[:11]:
        load.wait()

    lane8 = lax.broadcasted_iota(jnp.int32, (8, LANES), 1)
    row8 = lax.broadcasted_iota(jnp.int32, (8, LANES), 0)
    lane1 = lax.broadcasted_iota(jnp.int32, (1, LANES), 1)
    entry = jnp.minimum(((row8 & 1) << 4) + (lane8 >> 3), nnz - 1)
    blank = jnp.zeros((8, LANES - nnz), jnp.float32)
    wide_off = jnp.concatenate([off[...], blank], axis=1)
    wide_cols = jnp.concatenate([place_of(cols[...]).astype(jnp.float32), blank], axis=1)
    offs = jnp.zeros((8, LANES), jnp.float32)
    places = jnp.zeros((8, LANES), jnp.float32)
    diag_row = jnp.zeros((1, LANES), jnp.float32)
    id_row = jnp.zeros((1, LANES), jnp.int32)
    for r in range(8):
        mine = (lane8 & 7) == r
        offs = jnp.where(mine, lane_gather(jnp.broadcast_to(wide_off[r:r + 1], (8, LANES)), entry), offs)
        places = jnp.where(mine, lane_gather(jnp.broadcast_to(wide_cols[r:r + 1], (8, LANES)), entry), places)
        diag_row = jnp.where((lane1 & 7) == r, diag_own[r], diag_row)
        id_row = jnp.where((lane1 & 7) == r, place_of(ids[r]), id_row)
    slot_cell = jnp.zeros((1, LANES), jnp.int32)
    for e in range(SLABS):
        slot_cell = jnp.where(lane1 == slot[0, 0, e], e >> 3, slot_cell)
    held = slot_cell.astype(jnp.float32)
    group = lane1 >> 3
    second = offs[1:2]
    second = jnp.where(group == nnz - 16, diag_row, second)
    second = jnp.where(group == nnz - 15, id_row.astype(jnp.float32), second)
    second = jnp.where(group >= 12, pltpu.roll(held, 96, 1), second)
    fourth = jnp.where(group >= nnz - 16, pltpu.roll(held, 48, 1), places[1:2])
    meta[0:1] = offs[0:1]
    meta[1:2] = second
    meta[2:3] = places[0:1]
    meta[3:4] = fourth

    e_at = lax.broadcasted_iota(jnp.int32, (SLABS, SLABS), 1)
    m_at = lax.broadcasted_iota(jnp.int32, (SLABS, SLABS), 0)
    limit = jnp.zeros((SLABS, SLABS), jnp.int32)
    for c in range(8):
        limit = jnp.where((e_at >> 3) == c, length[0, 0, c], limit)
    chosen = (slot_row[0] == m_at) & ((e_at & 7) < limit)
    chooser = chosen.astype(jnp.float32).astype(jnp.bfloat16)

    def choose(k):
        at = pl.ds(pl.multiple_of(k * LANES, LANES), LANES)
        block = basis[:, :, at].astype(jnp.float32).reshape(SLABS, LANES).astype(jnp.bfloat16)
        pieces[k & 1, pl.ds(k >> 1, SLABS, stride=depth), :] = jnp.dot(
            chooser, block, preferred_element_type=jnp.float32)

    loop(0, 2 * depth, choose, 4)

    def settle(m):
        for h in range(2):
            sent[m, :, h * LANES:(h + 1) * LANES] = pieces[h, pl.ds(m * depth, depth), :].astype(jnp.bfloat16)

    loop(0, SLABS, settle, 4)
    for load in loads[11:13]:
        load.wait()

    def fill(y):
        c = lookup(label[y], diffusivity)
        v = value[y]
        cpad[y + 1] = c
        vpad[y + 1] = v
        upad[y + 1] = c * v
        conduct[y] = c
        zface[0, 0, pl.ds(y, 1)] = c[0:1]
        zface[1, 0, pl.ds(y, 1)] = c[depth - 1:depth]
        zface[0, 1, pl.ds(y, 1)] = v[0:1]
        zface[1, 1, pl.ds(y, 1)] = v[depth - 1:depth]

    loop(0, rows, fill, 4)
    for side, at in ((0, 1), (1, rows)):
        yface[side, 0] = cpad[at]
        yface[side, 1] = vpad[at]

    pl.semaphore_wait(barrier, SLABS - 1 + XS * (YS - 1))

    halos = (
        remote(zface.at[1], zhalo.at[0], h_send.at[0], h_recv.at[0], to_slab(1)),
        remote(zface.at[0], zhalo.at[1], h_send.at[1], h_recv.at[1], to_slab(SLABS - 1)),
        remote(yface.at[1], yhalo.at[0], h_send.at[2], h_recv.at[2], (slab, (tile + 1) & 3)),
        remote(yface.at[0], yhalo.at[1], h_send.at[3], h_recv.at[3], (slab, (tile + 3) & 3)),
    )
    mine = pltpu.make_async_copy(meta, table.at[place], own.at[0])
    mine.start()
    kept = pltpu.make_async_copy(sent.at[slab], got.at[order], own.at[1])
    kept.start()
    block = table.at[pl.ds(far * NEAR, NEAR)]

    def near_copy(k):
        return remote(meta, table.at[place], n_send.at[k], n_recv.at[k], to_near(k))

    def far_copy(k):
        return remote(block, block, f_send.at[k], f_recv.at[k], to_far(k))

    def basis_copy(k):
        return remote(sent.at[(slab + k) & (SLABS - 1)], got.at[order], a_send.at[k], a_recv.at[k], to_slab(k))

    loop(1, NEAR, lambda k: near_copy(k).start())
    for copy in halos:
        copy.start()
    loop(1, SLABS, lambda k: basis_copy(k).start())
    mine.wait()
    kept.wait()
    loop(1, NEAR, lambda k: near_copy(k).wait())
    loop(1, FAR, lambda k: far_copy(k).start())
    for copy in halos:
        copy.wait()

    loads[13].wait()

    has_low = jnp.where(slab > 0, 1.0, 0.0)
    has_high = jnp.where(slab < SLABS - 1, 1.0, 0.0)
    for side, at, flag in ((0, 0, jnp.where(tile > 0, 1.0, 0.0)), (1, rows + 1, jnp.where(tile < YS - 1, 1.0, 0.0))):
        c = yhalo[side, 0] * flag
        v = yhalo[side, 1] * flag
        cpad[at] = c
        vpad[at] = v
        upad[at] = c * v

    def plane(y):
        c, v, u = cpad[y + 1], vpad[y + 1], upad[y + 1]
        clow = zhalo[0, 0, pl.ds(y, 1)] * has_low
        chigh = zhalo[1, 0, pl.ds(y, 1)] * has_high
        vlow = zhalo[0, 1, pl.ds(y, 1)] * has_low
        vhigh = zhalo[1, 1, pl.ds(y, 1)] * has_high
        csum = beside(c, cpad[y], cpad[y + 2], clow, chigh)
        vsum = beside(v, vpad[y], vpad[y + 2], vlow, vhigh)
        usum = beside(u, upad[y], upad[y + 2], clow * vlow, chigh * vhigh)
        diagonal = lookup(label[y], uptake) + 3.0 * c + 0.5 * csum
        residual = source[y] - (diagonal * v - 0.5 * (c * vsum + usum))
        tiles[y] = residual.astype(jnp.bfloat16).astype(jnp.float32)
        weight[y] = OMEGA / diagonal

    loop(0, rows, plane, 2)

    row_at = lax.broadcasted_iota(jnp.int32, (rows, LANES), 0)
    lane_at = lax.broadcasted_iota(jnp.int32, (rows, LANES), 1)
    to_row = jnp.full((rows, LANES), -1, jnp.int32)
    for p in range(SLABS):
        to_row = jnp.where(lane_at == p, send[0, 0, 0, ordered_slab(p)], to_row)
    selector[...] = jnp.where(to_row == row_at, 1.0, 0.0)

    loop(1, FAR, lambda k: far_copy(k).wait())
    lane = lax.broadcasted_iota(jnp.int32, (NEAR, LANES), 1)
    for x_from in range(XS):
        own_rows = table[pl.ds(((x_from << 2) | tile) << 4, NEAR)]
        first, second = own_rows[:, 1], own_rows[:, 3]
        picked = jnp.where((lane == 96 + slab) & (slab < 32), first, 0.0)
        picked = picked + jnp.where((lane == 48 + slab) & (slab >= 32), second, 0.0)
        cell = jnp.sum(picked, axis=1, keepdims=True).astype(jnp.int32)
        index = jnp.sum(jnp.where(lane == 88 + cell, first, 0.0), axis=1, keepdims=True).astype(jnp.int32)
        target[x_from * NEAR:(x_from + 1) * NEAR, :] = jnp.broadcast_to(index, (NEAR, LANES))
    own_row = lax.broadcasted_iota(jnp.int32, (NEAR, LANES), 0)
    own_place = jnp.zeros((NEAR, LANES), jnp.int32)
    for r in range(8):
        own_place = jnp.where(own_row == r, place_of(ids[r]), own_place)
    target[SLABS:] = own_place
    to_scalar = pltpu.make_async_copy(target, target_s, target_sem.at[0])
    to_scalar.start()

    row_at = lax.broadcasted_iota(jnp.int32, (NEAR, LANES), 0)
    mine = row_at == lane >> 3
    used = lane < (nnz - 16) * 8
    is_diag = lane >> 3 == nnz - 16

    def squeeze(values):
        for shift in (8, 16, 32, 64):
            values = values + pltpu.roll(values, shift, 1)
        return jnp.sum(jnp.where(mine, values, 0.0), axis=0, keepdims=True)

    def prepare(g):
        at = pl.ds(pl.multiple_of(g * NEAR, NEAR), NEAR)
        block = table[at]
        second = block[:, 1]
        diag[pl.ds(g, 1)] = squeeze(jnp.where(is_diag, second, 0.0))
        factor[0, at] = block[:, 0]
        factor[1, at] = jnp.where(used, second, 0.0)
        for b in range(2):
            index = block[:, 2 + b].astype(jnp.int32)
            low[b, at] = index & (LANES - 1)
            high[b, at] = index >> 7

    loop(0, groups, prepare, 2)
    to_scalar.wait()

    def fetch(p):
        index = target_s[p, 0]
        line, here = pl.ds((index >> 3) & (NEAR * FAR - 1), 1), pl.ds(p, 1)
        keep = (lane1 & 7) == (index & 7)
        for b in range(2):
            last_factor[b, here] = jnp.where(keep, factor[b, line], 0.0)
            last_low[b, here] = low[b, line]
            last_high[b, here] = high[b, line]

    loop(0, SLABS + NEAR, fetch, 4)

    for side, at, inside in ((0, 0, slab > 0), (1, depth - 1, slab < SLABS - 1)):
        flag = jnp.where(inside, 0.5, 0.0)

        def gain(y):
            line = pl.ds(y, 1)
            pair = conduct[y][at:at + 1] + zhalo[side, 0, line]
            zgain[side, line] = weight[y][at:at + 1] * pair * flag

        loop(0, rows, gain, 4)
    for side, at, inside in ((0, 0, tile > 0), (1, rows - 1, tile < YS - 1)):
        flag = jnp.where(inside, 0.5, 0.0)
        ygain[side] = weight[at] * (conduct[at] + yhalo[side, 0]) * flag

    loop(1, SLABS, lambda k: basis_copy(k).wait())

    def product(p):
        terms = got[p].astype(jnp.float32) * tiles[send[0, 0, 0, ordered_slab(p)]]
        folded = terms[:, :LANES] + terms[:, LANES:]
        sums[pl.ds(p, 1)] = jnp.sum(folded, axis=0, keepdims=True)

    loop(0, SLABS, product, 8)
    products = jnp.broadcast_to(jnp.sum(sums[...], axis=1, keepdims=True), (SLABS, LANES))
    lane64 = lax.broadcasted_iota(jnp.int32, (SLABS, LANES), 1)
    for g in range(groups):
        hit = jnp.where(target[0:SLABS] == g * LANES + lane64, products, 0.0)
        near_buf[near, pl.ds(g, 1)] = jnp.sum(hit, axis=0, keepdims=True)

    def near_part(k):
        return remote(near_buf.at[near], near_buf.at[near], s_send.at[k], s_recv.at[k], to_near(k))

    def far_part(k):
        return remote(far_buf.at[far], far_buf.at[far], t_send.at[k], t_recv.at[k], to_far(k))

    loop(1, NEAR, lambda k: near_part(k).start())

    def unfold(p):
        for h in range(2):
            pieces[h, pl.ds(p * depth, depth), :] = got[p, :, h * LANES:(h + 1) * LANES].astype(jnp.float32)

    loop(0, SLABS, unfold, 4)
    loop(1, NEAR, lambda k: near_part(k).wait())
    far_buf[far] = jnp.sum(near_buf[...], axis=0)
    loop(1, FAR, lambda k: far_part(k).start())

    def turn(k):
        turned[k] = pieces[k & 1, pl.ds(k >> 1, SLABS, stride=depth), :].astype(jnp.bfloat16)

    loop(0, 2 * depth, turn, 4)
    loop(1, FAR, lambda k: far_part(k).wait())
    rhs[...] = jnp.sum(far_buf[...], axis=0)

    state[...] = rhs[...] / diag[...]

    def pick(low_ref, high_ref, factor_ref, b, start):
        at = pl.ds(start, 8)
        lane_of, row = low_ref[b, at], high_ref[b, at]
        found = [lane_gather(packed[q], lane_of) for q in range(8)]
        bit = 1
        while len(found) > 1:
            odd = (row & bit) != 0
            found = [jnp.where(odd, found[2 * i + 1], found[2 * i]) for i in range(len(found) // 2)]
            bit = bit * 2
        word = found[0]
        number = jnp.where((row & 8) != 0, word >> 16, (word << 16) >> 16)
        return number.astype(jnp.float32) * factor_ref[b, at]

    def pack():
        now = state[...]
        top = jnp.maximum(jnp.max(jnp.max(jnp.abs(now), axis=1, keepdims=True), axis=0, keepdims=True), 1e-34)
        whole = jnp.round(now * (FULL / top)).astype(jnp.int32)
        word = (whole[8:16] << 16) + (whole[0:8] & 0xFFFF)
        for q in range(8):
            packed[q] = jnp.broadcast_to(word[q:q + 1], (8, LANES))
        return top * (1.0 / FULL)

    for repeat in range(COARSE_SWEEPS - 2):
        scale = pack()

        def relax_group(g):
            parts = []
            for half in range(2):
                start = pl.multiple_of(g * NEAR + half * 8, 8)
                parts.append(pick(low, high, factor, 0, start) + pick(low, high, factor, 1, start))
            total = jnp.concatenate(parts, axis=0)
            state[pl.ds(g, 1)] = (rhs[pl.ds(g, 1)] - squeeze(total) * scale) / diag[pl.ds(g, 1)]

        loop(0, groups, relax_group, 4)

    scale = pack()
    lane_all = lax.broadcasted_iota(jnp.int32, (SLABS + NEAR, LANES), 1)
    right = jnp.zeros((SLABS + NEAR, LANES), jnp.float32)
    below = jnp.zeros((SLABS + NEAR, LANES), jnp.float32)
    for g in range(groups):
        hit = target[...] - g * LANES == lane_all
        right = jnp.where(hit, rhs[pl.ds(g, 1)], right)
        below = jnp.where(hit, diag[pl.ds(g, 1)], below)
    coupled = jnp.concatenate([
        pick(last_low, last_high, last_factor, 0, p) + pick(last_low, last_high, last_factor, 1, p)
        for p in range(0, SLABS + NEAR, 8)], axis=0)
    solved = jnp.sum(right - coupled * scale, axis=1, keepdims=True) / jnp.sum(below, axis=1, keepdims=True)
    solved = jnp.broadcast_to(solved, (SLABS + NEAR, LANES))
    scaled = solved[0:SLABS]
    mine8 = solved[SLABS:SLABS + 8]
    correction[...] = jnp.sum(jnp.where(row8 == lane8, mine8, 0.0), axis=0, keepdims=True)[:, 0:8]

    chooser = selector[:, 0:SLABS].astype(jnp.bfloat16)

    def deposit(k):
        terms = (scaled * turned[k].astype(jnp.float32)).astype(jnp.bfloat16)
        pieces[k & 1, pl.ds(k >> 1, rows, stride=depth), :] = jnp.dot(chooser, terms, preferred_element_type=jnp.float32)

    loop(0, 2 * depth, deposit, 4)
    none = jnp.zeros((depth, width), jnp.float32)
    for pad in (vpad, cpad, upad):
        pad[0] = none
        pad[rows + 1] = none

    def correct(y):
        at = pl.ds(y * depth, depth)
        v = value[y] + jnp.concatenate([pieces[0, at, :], pieces[1, at, :]], axis=1)
        vpad[y + 1] = v
        upad[y + 1] = conduct[y] * v
        zsend[0, 0, pl.ds(y, 1)] = v[0:1]
        zsend[0, 1, pl.ds(y, 1)] = v[depth - 1:depth]

    loop(0, rows, correct, 4)

    around = (to_slab(1), to_slab(SLABS - 1), (slab, (tile + 1) & 3), (slab, (tile + 3) & 3))
    for step in range(SMOOTH_SWEEPS):
        now = vpad if step == 0 else cpad
        copies = (
            remote(zsend.at[step, 1], zrecv.at[step, 0], v_send.at[step, 0], v_recv.at[step, 0], around[0]),
            remote(zsend.at[step, 0], zrecv.at[step, 1], v_send.at[step, 1], v_recv.at[step, 1], around[1]),
            remote(now.at[rows], yrecv.at[step, 0], v_send.at[step, 2], v_recv.at[step, 2], around[2]),
            remote(now.at[1], yrecv.at[step, 1], v_send.at[step, 3], v_recv.at[step, 3], around[3]),
        )
        for copy in copies:
            copy.start()

        if step > 0:
            def product(y):
                upad[y + 1] = conduct[y] * now[y + 1]
            loop(0, rows, product, 4)

        def inner(y):
            v = now[y + 1]
            vsum = beside(v, now[y], now[y + 2], 0.0, 0.0)
            usum = beside(upad[y + 1], upad[y], upad[y + 2], 0.0, 0.0)
            coupled = 0.5 * (conduct[y] * vsum + usum)
            relaxed = (1.0 - OMEGA) * v + weight[y] * (source[y] + coupled)
            if step == 0:
                cpad[y + 1] = relaxed
            else:
                out[y] = relaxed

        loop(0, rows, inner, 2)
        for copy in copies:
            copy.wait()
        later, shift = (cpad, 1) if step == 0 else (out, 0)
        later[shift] = later[shift] + ygain[0] * yrecv[step, 0]
        later[shift + rows - 1] = later[shift + rows - 1] + ygain[1] * yrecv[step, 1]

        def close(y):
            line = pl.ds(y, 1)
            lowest = later[y + shift, 0:1] + zgain[0, line] * zrecv[step, 0, line]
            highest = later[y + shift, depth - 1:depth] + zgain[1, line] * zrecv[step, 1, line]
            later[y + shift, 0:1] = lowest
            later[y + shift, depth - 1:depth] = highest
            if step + 1 < SMOOTH_SWEEPS:
                zsend[step + 1, 0, line] = lowest
                zsend[step + 1, 1, line] = highest

        loop(0, rows, close, 4)


def cycle(nnz, cells, diffusivity, uptake, send, slot, length, ids, diag, off, cols, value, source, label, basis):
    rows, depth, width = value.shape
    f32, bf16, i32 = jnp.float32, jnp.bfloat16, jnp.int32
    vmem, smem, dma = pltpu.VMEM, pltpu.SMEM, pltpu.SemaphoreType.DMA
    groups = cells // LANES
    reads = SLABS + NEAR
    block, padded = vmem(value.shape, f32), vmem((rows + 2, depth, width), f32)
    zfaces, yfaces = vmem((2, 2, rows, width), f32), vmem((2, 2, depth, width), f32)
    entries = (2, NEAR * FAR, LANES)
    return pl.pallas_call(
        functools.partial(cycle_kernel, nnz),
        out_shape=(jax.ShapeDtypeStruct(value.shape, f32), jax.ShapeDtypeStruct((1, 8), f32)),
        in_specs=[HBM] * 13,
        out_specs=(VMEM,) * 2,
        scratch_shapes=[
            smem(diffusivity.shape, f32), smem(uptake.shape, f32), smem(send.shape, i32), smem(slot.shape, i32),
            smem(length.shape, i32), smem(ids.shape, i32), smem(diag.shape, f32),
            vmem(slot.shape, i32), vmem(off.shape, f32), vmem(cols.shape, i32),
            block, block, vmem(label.shape, i32), vmem(basis.shape, bf16),
            vmem((SLABS, depth, width), bf16), vmem((SLABS, depth, width), bf16), zfaces, yfaces, zfaces, yfaces,
            vmem((4, LANES), f32), vmem((NEAR * FAR, 4, LANES), f32), vmem((2, SLABS * depth, LANES), f32),
            vmem((2 * depth, SLABS, LANES), bf16),
            block, block, padded, padded, padded, block, vmem((SLABS, LANES), f32),
            vmem((NEAR, groups, LANES), f32), vmem((FAR, groups, LANES), f32),
            vmem((reads, LANES), i32), smem((reads, LANES), i32), vmem((rows, LANES), f32),
            vmem((groups, LANES), f32), vmem((groups, LANES), f32), vmem((groups, LANES), f32),
            vmem((8, 8, LANES), i32), vmem(entries, i32), vmem(entries, i32), vmem(entries, f32),
            vmem((2, reads, LANES), i32), vmem((2, reads, LANES), i32), vmem((2, reads, LANES), f32),
            vmem((2, rows, width), f32), vmem((2, depth, width), f32),
            vmem((SMOOTH_SWEEPS, 2, rows, width), f32), vmem((SMOOTH_SWEEPS, 2, rows, width), f32),
            vmem((SMOOTH_SWEEPS, 2, depth, width), f32),
            dma((14,)), dma((1,)),
            dma((SLABS,)), dma((SLABS,)), dma((NEAR,)), dma((NEAR,)), dma((FAR,)), dma((FAR,)),
            dma((4,)), dma((4,)), dma((2,)), dma((NEAR,)), dma((NEAR,)), dma((FAR,)), dma((FAR,)),
            dma((SMOOTH_SWEEPS, 4)), dma((SMOOTH_SWEEPS, 4)),
        ],
        compiler_params=pltpu.CompilerParams(collective_id=0, has_side_effects=True, vmem_limit_bytes=48 << 20),
        name="cycle",
    )(diffusivity, uptake, send, slot, length, ids, diag, off, cols, value, source, label, basis)


def shards(solution, source, phase_label, phase_diffusivity, phase_uptake, send_tiles, support_slot, support_len,
           coarse_ids, basis_values, coarse_diag, coarse_off, coarse_cols):
    nnz = coarse_off.shape[1]
    cells = basis_values.shape[0] * NEAR * FAR
    send = send_tiles.transpose(0, 1, 3, 2)
    new_solution, correction = cycle(
        nnz, cells, phase_diffusivity, phase_uptake, send, support_slot, support_len, coarse_ids, coarse_diag,
        coarse_off, coarse_cols, solution, source, phase_label, basis_values)
    return new_solution, correction.reshape(correction.shape[1])


def solution(mesh):
    placed = (
        P("tile", "slab", None),
        P("tile", "slab", None),
        P("tile", "slab", None),
        P(),
        P(),
        P("slab", "tile", None, None),
        P("slab", "tile", None),
        P("slab", "tile", None),
        P(("slab", "tile")),
        P(("slab", "tile"), None, None),
        P(("slab", "tile")),
        P(("slab", "tile"), None),
        P(("slab", "tile"), None),
    )
    return jax.shard_map(
        shards,
        mesh=mesh,
        in_specs=placed,
        out_specs=(P("tile", "slab", None), P(("slab", "tile"))),
        check_vma=False,
    )
```

```python
import functools

import jax
import jax.numpy as jnp
from jax import lax
from jax.experimental import pallas as pl
from jax.experimental.pallas import tpu as pltpu
from jax.sharding import PartitionSpec as P

COARSE_SWEEPS = 4
SMOOTH_SWEEPS = 2
OMEGA = 0.8
MESH = pl.DeviceIdType.MESH
LANES = 128
FULL = 32760.0

ZS, XS, CORES, YS = 8, 4, 2, 4
NEAR = ZS * CORES
FAR = XS * YS
SLABS = ZS * XS * CORES


def split_slab(slab):
    return slab >> 3, (slab >> 1) & 3, slab & 1


def near_device(near, x, tile):
    return ((near >> 1) << 3) | (x << 1) | (near & 1), tile


def far_device(far, z, core):
    return (z << 3) | ((far >> 2) << 1) | core, far & 3


def ordered_slab(order):
    return near_device(order & (NEAR - 1), order >> 4, 0)[0]


def place_of(index):
    owner, row = index >> 3, index & 7
    slab, tile = owner >> 2, owner & 3
    z, x, core = split_slab(slab)
    return (((((x << 2) | tile) << 4) | (z << 1) | core) << 3) | row


VMEM = pl.BlockSpec(memory_space=pltpu.VMEM)
HBM = pl.BlockSpec(memory_space=pltpu.HBM)


def remote(src, dst, send_sem, recv_sem, device):
    return pltpu.make_async_remote_copy(
        src_ref=src, dst_ref=dst, send_sem=send_sem, recv_sem=recv_sem,
        device_id=device, device_id_type=MESH,
    )


def loop(low, high, act, unroll=1):
    def body(k, carry):
        act(k)
        return carry
    lax.fori_loop(low, high, body, 0, unroll=unroll)


def lane_gather(source, index):
    numbers = lax.GatherDimensionNumbers(
        offset_dims=(), collapsed_slice_dims=(1,), start_index_map=(1,),
        operand_batching_dims=(0,), start_indices_batching_dims=(0,),
    )
    return lax.gather(source, index[..., None], numbers, (1, 1), mode=lax.GatherScatterMode.PROMISE_IN_BOUNDS)


def beside(mid, below, above, zlow, zhigh):
    depth, width = mid.shape
    zi = lax.broadcasted_iota(jnp.int32, mid.shape, 0)
    xi = lax.broadcasted_iota(jnp.int32, mid.shape, 1)
    total = below + above
    total = total + jnp.where(zi == 0, zlow, pltpu.roll(mid, 1, 0))
    total = total + jnp.where(zi == depth - 1, zhigh, pltpu.roll(mid, depth - 1, 0))
    total = total + jnp.where(xi == 0, 0.0, pltpu.roll(mid, 1, 1))
    total = total + jnp.where(xi == width - 1, 0.0, pltpu.roll(mid, width - 1, 1))
    return total


def lookup(label, table):
    result = jnp.full(label.shape, table[0], jnp.float32)
    for category in range(1, table.shape[0]):
        result = jnp.where(label == category, table[category], result)
    return result


def cycle_kernel(nnz, diffusivity_h, uptake_h, send_h, slot_h, length_h, ids_h, diag_h, off_h, cols_h,
                 value_h, source_h, label_h, basis_h,
                 out, correction,
                 diffusivity, uptake, send, slot, length, ids, diag_own, slot_row, off, cols,
                 value, source, label, basis,
                 sent, got, zface, yface, zhalo, yhalo, meta, table, pieces, turned,
                 conduct, weight, cpad, vpad, upad, tiles, sums, near_buf, far_buf,
                 target, target_s, spot, seconds, inverse, selector, state, rhs, diag, packed, low, high, factor,
                 last_low, last_high, last_factor, zgain, ygain, zsend, zrecv, yrecv,
                 load_sem, target_sem, a_send, a_recv, n_send, n_recv, f_send, f_recv, h_send, h_recv, own,
                 s_send, s_recv, t_send, t_recv, v_send, v_recv):
    rows, depth, width = value.shape
    groups = rhs.shape[0]
    slab, tile = lax.axis_index("slab"), lax.axis_index("tile")
    z, x, core = split_slab(slab)
    near = (z << 1) | core
    far = (x << 2) | tile
    order = (x << 4) | near
    place = (far << 4) | near

    barrier = pltpu.get_barrier_semaphore()

    def to_near(k):
        return near_device((near + k) & (NEAR - 1), x, tile)

    def to_far(k):
        return far_device((far + k) & (FAR - 1), z, core)

    def to_slab(k):
        return (slab + k) & (SLABS - 1), tile

    def greet(device):
        pl.semaphore_signal(barrier, inc=1, device_id=device, device_id_type=MESH)

    loop(SLABS // 4, SLABS, lambda k: greet(to_slab(k)))
    loop(1, SLABS // 4, lambda k: greet(to_slab(k)))
    loop(0, XS * (YS - 1), lambda k: greet(
        ((z << 3) | (((x + k) & 3) << 1) | core, (tile + 1 + (k >> 2)) & (YS - 1))))
    loads = [pltpu.make_async_copy(*pair, load_sem.at[i]) for i, pair in enumerate((
        (slot_h, slot), (length_h, length), (slot_h, slot_row), (basis_h, basis), (off_h, off), (cols_h, cols),
        (ids_h, ids), (diag_h, diag_own), (diffusivity_h, diffusivity), (uptake_h, uptake), (send_h, send),
        (label_h, label), (value_h, value), (source_h, source)))]
    for load in loads:
        load.start()
    for load in loads[:11]:
        load.wait()

    lane8 = lax.broadcasted_iota(jnp.int32, (8, LANES), 1)
    row8 = lax.broadcasted_iota(jnp.int32, (8, LANES), 0)
    lane1 = lax.broadcasted_iota(jnp.int32, (1, LANES), 1)
    entry = jnp.minimum(((row8 & 1) << 4) + (lane8 >> 3), nnz - 1)
    blank = jnp.zeros((8, LANES - nnz), jnp.float32)
    wide_off = jnp.concatenate([off[...], blank], axis=1)
    wide_cols = jnp.concatenate([place_of(cols[...]).astype(jnp.float32), blank], axis=1)
    offs = jnp.zeros((8, LANES), jnp.float32)
    places = jnp.zeros((8, LANES), jnp.float32)
    diag_row = jnp.zeros((1, LANES), jnp.float32)
    id_row = jnp.zeros((1, LANES), jnp.int32)
    for r in range(8):
        mine = (lane8 & 7) == r
        offs = jnp.where(mine, lane_gather(jnp.broadcast_to(wide_off[r:r + 1], (8, LANES)), entry), offs)
        places = jnp.where(mine, lane_gather(jnp.broadcast_to(wide_cols[r:r + 1], (8, LANES)), entry), places)
        diag_row = jnp.where((lane1 & 7) == r, diag_own[r], diag_row)
        id_row = jnp.where((lane1 & 7) == r, place_of(ids[r]), id_row)
    slot_cell = jnp.zeros((1, LANES), jnp.int32)
    for e in range(SLABS):
        slot_cell = jnp.where(lane1 == slot[0, 0, e], e >> 3, slot_cell)
    held = slot_cell.astype(jnp.float32)
    group = lane1 >> 3
    second = offs[1:2]
    second = jnp.where(group == nnz - 16, diag_row, second)
    second = jnp.where(group == nnz - 15, id_row.astype(jnp.float32), second)
    second = jnp.where(group >= 12, pltpu.roll(held, 96, 1), second)
    fourth = jnp.where(group >= nnz - 16, pltpu.roll(held, 48, 1), places[1:2])
    meta[0:1] = offs[0:1]
    meta[1:2] = second
    meta[2:3] = places[0:1]
    meta[3:4] = fourth

    e_at = lax.broadcasted_iota(jnp.int32, (SLABS, SLABS), 1)
    m_at = lax.broadcasted_iota(jnp.int32, (SLABS, SLABS), 0)
    limit = jnp.zeros((SLABS, SLABS), jnp.int32)
    for c in range(8):
        limit = jnp.where((e_at >> 3) == c, length[0, 0, c], limit)
    chosen = (slot_row[0] == m_at) & ((e_at & 7) < limit)
    chooser = chosen.astype(jnp.float32).astype(jnp.bfloat16)

    def choose(k):
        at = pl.ds(pl.multiple_of(k * LANES, LANES), LANES)
        block = basis[:, :, at].astype(jnp.float32).reshape(SLABS, LANES).astype(jnp.bfloat16)
        pieces[k & 1, pl.ds(k >> 1, SLABS, stride=depth), :] = jnp.dot(
            chooser, block, preferred_element_type=jnp.float32)

    loop(0, 2 * depth, choose, 4)

    def settle(m):
        for h in range(2):
            sent[m, :, h * LANES:(h + 1) * LANES] = pieces[h, pl.ds(m * depth, depth), :].astype(jnp.bfloat16)

    loop(0, SLABS, settle, 4)
    for load in loads[11:13]:
        load.wait()

    def fill(y):
        c = lookup(label[y], diffusivity)
        v = value[y]
        cpad[y + 1] = c
        vpad[y + 1] = v
        upad[y + 1] = c * v
        conduct[y] = c
        zface[0, 0, pl.ds(y, 1)] = c[0:1]
        zface[1, 0, pl.ds(y, 1)] = c[depth - 1:depth]
        zface[0, 1, pl.ds(y, 1)] = v[0:1]
        zface[1, 1, pl.ds(y, 1)] = v[depth - 1:depth]

    loop(0, rows, fill, 4)
    for side, at in ((0, 1), (1, rows)):
        yface[side, 0] = cpad[at]
        yface[side, 1] = vpad[at]

    pl.semaphore_wait(barrier, SLABS - 1 + XS * (YS - 1))

    halos = (
        remote(zface.at[1], zhalo.at[0], h_send.at[0], h_recv.at[0], to_slab(1)),
        remote(zface.at[0], zhalo.at[1], h_send.at[1], h_recv.at[1], to_slab(SLABS - 1)),
        remote(yface.at[1], yhalo.at[0], h_send.at[2], h_recv.at[2], (slab, (tile + 1) & 3)),
        remote(yface.at[0], yhalo.at[1], h_send.at[3], h_recv.at[3], (slab, (tile + 3) & 3)),
    )
    mine = pltpu.make_async_copy(meta, table.at[place], own.at[0])
    mine.start()
    kept = pltpu.make_async_copy(sent.at[slab], got.at[order], own.at[1])
    kept.start()
    block = table.at[pl.ds(far * NEAR, NEAR)]

    def near_copy(k):
        return remote(meta, table.at[place], n_send.at[k], n_recv.at[k], to_near(k))

    def line_copy(k):
        device = ((z << 3) | (((x + k) & 3) << 1) | core, tile)
        return remote(block, block, f_send.at[k], f_recv.at[k], device)

    def far_copy(k):
        device = ((z << 3) | (((x + k) & 3) << 1) | core, (tile + 1 + (k >> 2)) & (YS - 1))
        return remote(block, block, f_send.at[XS + k], f_recv.at[XS + k], device)

    def basis_copy(k):
        return remote(sent.at[(slab + k) & (SLABS - 1)], got.at[order], a_send.at[k], a_recv.at[k], to_slab(k))

    loop(1, NEAR, lambda k: near_copy(k).start())
    for copy in halos:
        copy.start()
    loop(1, SLABS, lambda k: basis_copy(k).start())
    mine.wait()
    kept.wait()
    loop(1, NEAR, lambda k: near_copy(k).wait())
    loop(1, XS, lambda k: line_copy(k).start())
    loop(0, XS * (YS - 1), lambda k: far_copy(k).start())
    for copy in halos:
        copy.wait()

    loads[13].wait()

    has_low = jnp.where(slab > 0, 1.0, 0.0)
    has_high = jnp.where(slab < SLABS - 1, 1.0, 0.0)
    for side, at, flag in ((0, 0, jnp.where(tile > 0, 1.0, 0.0)), (1, rows + 1, jnp.where(tile < YS - 1, 1.0, 0.0))):
        c = yhalo[side, 0] * flag
        v = yhalo[side, 1] * flag
        cpad[at] = c
        vpad[at] = v
        upad[at] = c * v

    def plane(y):
        c, v, u = cpad[y + 1], vpad[y + 1], upad[y + 1]
        clow = zhalo[0, 0, pl.ds(y, 1)] * has_low
        chigh = zhalo[1, 0, pl.ds(y, 1)] * has_high
        vlow = zhalo[0, 1, pl.ds(y, 1)] * has_low
        vhigh = zhalo[1, 1, pl.ds(y, 1)] * has_high
        csum = beside(c, cpad[y], cpad[y + 2], clow, chigh)
        vsum = beside(v, vpad[y], vpad[y + 2], vlow, vhigh)
        usum = beside(u, upad[y], upad[y + 2], clow * vlow, chigh * vhigh)
        diagonal = lookup(label[y], uptake) + 3.0 * c + 0.5 * csum
        residual = source[y] - (diagonal * v - 0.5 * (c * vsum + usum))
        tiles[y] = residual.astype(jnp.bfloat16).astype(jnp.float32)
        weight[y] = OMEGA / diagonal

    loop(0, rows, plane, 2)

    row_at = lax.broadcasted_iota(jnp.int32, (rows, LANES), 0)
    lane_at = lax.broadcasted_iota(jnp.int32, (rows, LANES), 1)
    to_row = jnp.full((rows, LANES), -1, jnp.int32)
    for p in range(SLABS):
        to_row = jnp.where(lane_at == p, send[0, 0, 0, ordered_slab(p)], to_row)
    selector[...] = jnp.where(to_row == row_at, 1.0, 0.0)

    loop(1, XS, lambda k: line_copy(k).wait())
    lane = lax.broadcasted_iota(jnp.int32, (NEAR, LANES), 1)
    own_row = lax.broadcasted_iota(jnp.int32, (NEAR, LANES), 0)
    for x_from in range(XS):
        own_rows = table[pl.ds(((x_from << 2) | tile) << 4, NEAR)]
        first, second = own_rows[:, 1], own_rows[:, 3]
        picked = jnp.where((lane == 96 + slab) & (slab < 32), first, 0.0)
        picked = picked + jnp.where((lane == 48 + slab) & (slab >= 32), second, 0.0)
        cell = jnp.sum(picked, axis=1, keepdims=True).astype(jnp.int32)
        index = jnp.sum(jnp.where(lane == 88 + cell, first, 0.0), axis=1, keepdims=True).astype(jnp.int32)
        target[x_from * NEAR:(x_from + 1) * NEAR, :] = jnp.broadcast_to(index, (NEAR, LANES))
        spot[x_from * NEAR:(x_from + 1) * NEAR, :] = own_row * 8 + cell
    own_place = jnp.zeros((NEAR, LANES), jnp.int32)
    for r in range(8):
        own_place = jnp.where(own_row == r, place_of(ids[r]), own_place)
    target[SLABS:] = own_place
    to_scalar = pltpu.make_async_copy(target, target_s, target_sem.at[0])
    to_scalar.start()


    loop(1, SLABS, lambda k: basis_copy(k).wait())

    def product(p):
        terms = got[p].astype(jnp.float32) * tiles[send[0, 0, 0, ordered_slab(p)]]
        folded = terms[:, :LANES] + terms[:, LANES:]
        sums[pl.ds(p, 1)] = jnp.sum(folded, axis=0, keepdims=True)

    loop(0, SLABS, product, 8)
    products = jnp.broadcast_to(jnp.sum(sums[...], axis=1, keepdims=True), (SLABS, LANES))
    lane64 = lax.broadcasted_iota(jnp.int32, (SLABS, LANES), 1)
    placed = jnp.where(lane64 == spot[...], products, 0.0)
    for x_to in range(XS):
        near_buf[near, pl.ds(x_to, 1)] = jnp.sum(placed[x_to * NEAR:(x_to + 1) * NEAR], axis=0, keepdims=True)

    def near_part(k):
        return remote(near_buf.at[near], near_buf.at[near], s_send.at[k], s_recv.at[k], to_near(k))

    def far_part(k):
        return remote(far_buf.at[far], far_buf.at[far], t_send.at[k], t_recv.at[k], to_far(k))

    loop(1, NEAR, lambda k: near_part(k).start())

    def unfold(p):
        for h in range(2):
            pieces[h, pl.ds(p * depth, depth), :] = got[p, :, h * LANES:(h + 1) * LANES].astype(jnp.float32)

    loop(0, SLABS, unfold, 4)

    def turn(k):
        turned[k] = pieces[k & 1, pl.ds(k >> 1, SLABS, stride=depth), :].astype(jnp.bfloat16)

    loop(0, 2 * depth, turn, 4)

    for side, at, inside in ((0, 0, slab > 0), (1, depth - 1, slab < SLABS - 1)):
        flag = jnp.where(inside, 0.5, 0.0)

        def gain(y):
            line = pl.ds(y, 1)
            pair = conduct[y][at:at + 1] + zhalo[side, 0, line]
            zgain[side, line] = weight[y][at:at + 1] * pair * flag

        loop(0, rows, gain, 4)
    for side, at, inside in ((0, 0, tile > 0), (1, rows - 1, tile < YS - 1)):
        flag = jnp.where(inside, 0.5, 0.0)
        ygain[side] = weight[at] * (conduct[at] + yhalo[side, 0]) * flag

    loop(1, NEAR, lambda k: near_part(k).wait())
    far_buf[far] = jnp.sum(near_buf[...], axis=0)
    loop(1, FAR, lambda k: far_part(k).start())
    loop(0, XS * (YS - 1), lambda k: far_copy(k).wait())

    mine = own_row == lane >> 3
    used = lane < (nnz - 16) * 8
    is_diag = lane >> 3 == nnz - 16

    def squeeze(values):
        for shift in (8, 16, 32, 64):
            values = values + pltpu.roll(values, shift, 1)
        return jnp.sum(jnp.where(mine, values, 0.0), axis=0, keepdims=True)

    def prepare(g):
        at = pl.ds(pl.multiple_of(g * NEAR, NEAR), NEAR)
        block = table[at]
        second = block[:, 1]
        diag[pl.ds(g, 1)] = squeeze(jnp.where(is_diag, second, 0.0))
        seconds[at] = second
        factor[0, at] = block[:, 0]
        factor[1, at] = jnp.where(used, second, 0.0)
        for b in range(2):
            index = block[:, 2 + b].astype(jnp.int32)
            low[b, at] = index & (LANES - 1)
            high[b, at] = index >> 7

    loop(0, groups, prepare, 2)
    to_scalar.wait()

    def fetch(p):
        index = target_s[p, 0]
        line, here = pl.ds((index >> 3) & (NEAR * FAR - 1), 1), pl.ds(p, 1)
        keep = (lane1 & 7) == (index & 7)
        for b in range(2):
            last_factor[b, here] = jnp.where(keep, factor[b, line], 0.0)
            last_low[b, here] = low[b, line]
            last_high[b, here] = high[b, line]

    loop(0, SLABS + NEAR, fetch, 4)

    line_at = lax.broadcasted_iota(jnp.int32, (NEAR * FAR, LANES), 0)
    lane_of = lax.broadcasted_iota(jnp.int32, (NEAR * FAR, LANES), 1)
    arrive = (((line_at >> 4) & 3) << 2) | (line_at >> 6)
    inverse[...] = jnp.zeros(inverse.shape, jnp.float32)

    def invert(c):
        number = lane_gather(seconds[...], jnp.full((NEAR * FAR, LANES), 88, jnp.int32) + c).astype(jnp.int32)
        code = jnp.where(lane_of < NEAR, arrive, ((line_at & (NEAR - 1)) << 3) + c)
        group_hit = ((number >> 7) == (lane_of & (NEAR - 1))) & (lane_of < 2 * NEAR)
        coded = jnp.where(group_hit, code, 0).astype(jnp.float32).astype(jnp.bfloat16)
        lane_hit = jnp.where((number & (LANES - 1)) == lane_of, 1.0, 0.0).astype(jnp.bfloat16)
        inverse[...] += lax.dot_general(coded, lane_hit, (((0,), (0,)), ((), ())),
                                        preferred_element_type=jnp.float32)[0:2 * NEAR]

    loop(0, 8, invert)

    loop(1, FAR, lambda k: far_part(k).wait())
    for y_from in range(YS):
        arrived = far_buf[y_from]
        for x_from in range(1, XS):
            arrived = arrived + far_buf[(x_from << 2) | y_from]
        state[y_from * XS:(y_from + 1) * XS] = arrived
    from_row, from_lane = inverse[0:NEAR].astype(jnp.int32), inverse[NEAR:].astype(jnp.int32)
    ordered = jnp.zeros((groups, LANES), jnp.float32)
    for g in range(groups):
        taken = lane_gather(jnp.broadcast_to(state[pl.ds(g, 1)], (groups, LANES)), from_lane)
        ordered = jnp.where(from_row == g, taken, ordered)
    rhs[...] = ordered

    state[...] = rhs[...] / diag[...]

    def pick(low_ref, high_ref, factor_ref, b, start):
        at = pl.ds(start, 8)
        lane_of, row = low_ref[b, at], high_ref[b, at]
        found = [lane_gather(packed[q], lane_of) for q in range(8)]
        bit = 1
        while len(found) > 1:
            odd = (row & bit) != 0
            found = [jnp.where(odd, found[2 * i + 1], found[2 * i]) for i in range(len(found) // 2)]
            bit = bit * 2
        word = found[0]
        number = jnp.where((row & 8) != 0, word >> 16, (word << 16) >> 16)
        return number.astype(jnp.float32) * factor_ref[b, at]

    def pack():
        now = state[...]
        top = jnp.maximum(jnp.max(jnp.max(jnp.abs(now), axis=1, keepdims=True), axis=0, keepdims=True), 1e-34)
        whole = jnp.round(now * (FULL / top)).astype(jnp.int32)
        word = (whole[8:16] << 16) + (whole[0:8] & 0xFFFF)
        for q in range(8):
            packed[q] = jnp.broadcast_to(word[q:q + 1], (8, LANES))
        return top * (1.0 / FULL)

    for repeat in range(COARSE_SWEEPS - 2):
        scale = pack()

        def relax_group(g):
            parts = []
            for half in range(2):
                start = pl.multiple_of(g * NEAR + half * 8, 8)
                parts.append(pick(low, high, factor, 0, start) + pick(low, high, factor, 1, start))
            total = jnp.concatenate(parts, axis=0)
            state[pl.ds(g, 1)] = (rhs[pl.ds(g, 1)] - squeeze(total) * scale) / diag[pl.ds(g, 1)]

        loop(0, groups, relax_group, 4)

    scale = pack()
    lane_all = lax.broadcasted_iota(jnp.int32, (SLABS + NEAR, LANES), 1)
    right = jnp.zeros((SLABS + NEAR, LANES), jnp.float32)
    below = jnp.zeros((SLABS + NEAR, LANES), jnp.float32)
    for g in range(groups):
        hit = target[...] - g * LANES == lane_all
        right = jnp.where(hit, rhs[pl.ds(g, 1)], right)
        below = jnp.where(hit, diag[pl.ds(g, 1)], below)
    coupled = jnp.concatenate([
        pick(last_low, last_high, last_factor, 0, p) + pick(last_low, last_high, last_factor, 1, p)
        for p in range(0, SLABS + NEAR, 8)], axis=0)
    solved = jnp.sum(right - coupled * scale, axis=1, keepdims=True) / jnp.sum(below, axis=1, keepdims=True)
    solved = jnp.broadcast_to(solved, (SLABS + NEAR, LANES))
    scaled = solved[0:SLABS]
    mine8 = solved[SLABS:SLABS + 8]
    correction[...] = jnp.sum(jnp.where(row8 == lane8, mine8, 0.0), axis=0, keepdims=True)[:, 0:8]

    chooser = selector[:, 0:SLABS].astype(jnp.bfloat16)

    def deposit(k):
        terms = (scaled * turned[k].astype(jnp.float32)).astype(jnp.bfloat16)
        pieces[k & 1, pl.ds(k >> 1, rows, stride=depth), :] = jnp.dot(chooser, terms, preferred_element_type=jnp.float32)

    loop(0, 2 * depth, deposit, 4)
    none = jnp.zeros((depth, width), jnp.float32)
    for pad in (vpad, cpad, upad):
        pad[0] = none
        pad[rows + 1] = none

    def correct(y):
        at = pl.ds(y * depth, depth)
        v = value[y] + jnp.concatenate([pieces[0, at, :], pieces[1, at, :]], axis=1)
        vpad[y + 1] = v
        upad[y + 1] = conduct[y] * v
        zsend[0, 0, pl.ds(y, 1)] = v[0:1]
        zsend[0, 1, pl.ds(y, 1)] = v[depth - 1:depth]

    loop(0, rows, correct, 4)

    around = (to_slab(1), to_slab(SLABS - 1), (slab, (tile + 1) & 3), (slab, (tile + 3) & 3))
    for step in range(SMOOTH_SWEEPS):
        now = vpad if step == 0 else cpad
        copies = (
            remote(zsend.at[step, 1], zrecv.at[step, 0], v_send.at[step, 0], v_recv.at[step, 0], around[0]),
            remote(zsend.at[step, 0], zrecv.at[step, 1], v_send.at[step, 1], v_recv.at[step, 1], around[1]),
            remote(now.at[rows], yrecv.at[step, 0], v_send.at[step, 2], v_recv.at[step, 2], around[2]),
            remote(now.at[1], yrecv.at[step, 1], v_send.at[step, 3], v_recv.at[step, 3], around[3]),
        )
        for copy in copies:
            copy.start()

        if step > 0:
            def product(y):
                upad[y + 1] = conduct[y] * now[y + 1]
            loop(0, rows, product, 4)

        def inner(y):
            v = now[y + 1]
            vsum = beside(v, now[y], now[y + 2], 0.0, 0.0)
            usum = beside(upad[y + 1], upad[y], upad[y + 2], 0.0, 0.0)
            coupled = 0.5 * (conduct[y] * vsum + usum)
            relaxed = (1.0 - OMEGA) * v + weight[y] * (source[y] + coupled)
            if step == 0:
                cpad[y + 1] = relaxed
            else:
                out[y] = relaxed

        loop(0, rows, inner, 2)
        for copy in copies:
            copy.wait()
        later, shift = (cpad, 1) if step == 0 else (out, 0)
        later[shift] = later[shift] + ygain[0] * yrecv[step, 0]
        later[shift + rows - 1] = later[shift + rows - 1] + ygain[1] * yrecv[step, 1]

        def close(y):
            line = pl.ds(y, 1)
            lowest = later[y + shift, 0:1] + zgain[0, line] * zrecv[step, 0, line]
            highest = later[y + shift, depth - 1:depth] + zgain[1, line] * zrecv[step, 1, line]
            later[y + shift, 0:1] = lowest
            later[y + shift, depth - 1:depth] = highest
            if step + 1 < SMOOTH_SWEEPS:
                zsend[step + 1, 0, line] = lowest
                zsend[step + 1, 1, line] = highest

        loop(0, rows, close, 4)


def cycle(nnz, cells, diffusivity, uptake, send, slot, length, ids, diag, off, cols, value, source, label, basis):
    rows, depth, width = value.shape
    f32, bf16, i32 = jnp.float32, jnp.bfloat16, jnp.int32
    vmem, smem, dma = pltpu.VMEM, pltpu.SMEM, pltpu.SemaphoreType.DMA
    groups = cells // LANES
    reads = SLABS + NEAR
    block, padded = vmem(value.shape, f32), vmem((rows + 2, depth, width), f32)
    zfaces, yfaces = vmem((2, 2, rows, width), f32), vmem((2, 2, depth, width), f32)
    entries = (2, NEAR * FAR, LANES)
    return pl.pallas_call(
        functools.partial(cycle_kernel, nnz),
        out_shape=(jax.ShapeDtypeStruct(value.shape, f32), jax.ShapeDtypeStruct((1, 8), f32)),
        in_specs=[HBM] * 13,
        out_specs=(VMEM,) * 2,
        scratch_shapes=[
            smem(diffusivity.shape, f32), smem(uptake.shape, f32), smem(send.shape, i32), smem(slot.shape, i32),
            smem(length.shape, i32), smem(ids.shape, i32), smem(diag.shape, f32),
            vmem(slot.shape, i32), vmem(off.shape, f32), vmem(cols.shape, i32),
            block, block, vmem(label.shape, i32), vmem(basis.shape, bf16),
            vmem((SLABS, depth, width), bf16), vmem((SLABS, depth, width), bf16), zfaces, yfaces, zfaces, yfaces,
            vmem((4, LANES), f32), vmem((NEAR * FAR, 4, LANES), f32), vmem((2, SLABS * depth, LANES), f32),
            vmem((2 * depth, SLABS, LANES), bf16),
            block, block, padded, padded, padded, block, vmem((SLABS, LANES), f32),
            vmem((NEAR, XS, LANES), f32), vmem((FAR, XS, LANES), f32),
            vmem((reads, LANES), i32), smem((reads, LANES), i32), vmem((SLABS, LANES), i32),
            vmem((NEAR * FAR, LANES), f32), vmem((2 * NEAR, LANES), f32), vmem((rows, LANES), f32),
            vmem((groups, LANES), f32), vmem((groups, LANES), f32), vmem((groups, LANES), f32),
            vmem((8, 8, LANES), i32), vmem(entries, i32), vmem(entries, i32), vmem(entries, f32),
            vmem((2, reads, LANES), i32), vmem((2, reads, LANES), i32), vmem((2, reads, LANES), f32),
            vmem((2, rows, width), f32), vmem((2, depth, width), f32),
            vmem((SMOOTH_SWEEPS, 2, rows, width), f32), vmem((SMOOTH_SWEEPS, 2, rows, width), f32),
            vmem((SMOOTH_SWEEPS, 2, depth, width), f32),
            dma((14,)), dma((1,)),
            dma((SLABS,)), dma((SLABS,)), dma((NEAR,)), dma((NEAR,)), dma((FAR,)), dma((FAR,)),
            dma((4,)), dma((4,)), dma((2,)), dma((NEAR,)), dma((NEAR,)), dma((FAR,)), dma((FAR,)),
            dma((SMOOTH_SWEEPS, 4)), dma((SMOOTH_SWEEPS, 4)),
        ],
        compiler_params=pltpu.CompilerParams(collective_id=0, has_side_effects=True, vmem_limit_bytes=60 << 20),
        name="cycle",
    )(diffusivity, uptake, send, slot, length, ids, diag, off, cols, value, source, label, basis)


def shards(solution, source, phase_label, phase_diffusivity, phase_uptake, send_tiles, support_slot, support_len,
           coarse_ids, basis_values, coarse_diag, coarse_off, coarse_cols):
    nnz = coarse_off.shape[1]
    cells = basis_values.shape[0] * NEAR * FAR
    send = send_tiles.transpose(0, 1, 3, 2)
    new_solution, correction = cycle(
        nnz, cells, phase_diffusivity, phase_uptake, send, support_slot, support_len, coarse_ids, coarse_diag,
        coarse_off, coarse_cols, solution, source, phase_label, basis_values)
    return new_solution, correction.reshape(correction.shape[1])


def solution(mesh):
    placed = (
        P("tile", "slab", None),
        P("tile", "slab", None),
        P("tile", "slab", None),
        P(),
        P(),
        P("slab", "tile", None, None),
        P("slab", "tile", None),
        P("slab", "tile", None),
        P(("slab", "tile")),
        P(("slab", "tile"), None, None),
        P(("slab", "tile")),
        P(("slab", "tile"), None),
        P(("slab", "tile"), None),
    )
    return jax.shard_map(
        shards,
        mesh=mesh,
        in_specs=placed,
        out_specs=(P("tile", "slab", None), P(("slab", "tile"))),
        check_vma=False,
    )
```

```python
import functools

import jax
import jax.numpy as jnp
from jax import lax
from jax.experimental import pallas as pl
from jax.experimental.pallas import tpu as pltpu
from jax.sharding import PartitionSpec as P

COARSE_SWEEPS = 4
SMOOTH_SWEEPS = 2
OMEGA = 0.8
MESH = pl.DeviceIdType.MESH
LANES = 128
FULL = 32760.0

ZS, XS, CORES, YS = 8, 4, 2, 4
NEAR = ZS * CORES
FAR = XS * YS
SLABS = ZS * XS * CORES


def split_slab(slab):
    return slab >> 3, (slab >> 1) & 3, slab & 1


def near_device(near, x, tile):
    return ((near >> 1) << 3) | (x << 1) | (near & 1), tile


def far_device(far, z, core):
    return (z << 3) | ((far >> 2) << 1) | core, far & 3


def ordered_slab(order):
    return near_device(order & (NEAR - 1), order >> 4, 0)[0]


def place_of(index):
    owner, row = index >> 3, index & 7
    slab, tile = owner >> 2, owner & 3
    z, x, core = split_slab(slab)
    return (((((x << 2) | tile) << 4) | (z << 1) | core) << 3) | row


VMEM = pl.BlockSpec(memory_space=pltpu.VMEM)
HBM = pl.BlockSpec(memory_space=pltpu.HBM)


def remote(src, dst, send_sem, recv_sem, device):
    return pltpu.make_async_remote_copy(
        src_ref=src, dst_ref=dst, send_sem=send_sem, recv_sem=recv_sem,
        device_id=device, device_id_type=MESH,
    )


def loop(low, high, act, unroll=1):
    def body(k, carry):
        act(k)
        return carry
    lax.fori_loop(low, high, body, 0, unroll=unroll)


def lane_gather(source, index):
    numbers = lax.GatherDimensionNumbers(
        offset_dims=(), collapsed_slice_dims=(1,), start_index_map=(1,),
        operand_batching_dims=(0,), start_indices_batching_dims=(0,),
    )
    return lax.gather(source, index[..., None], numbers, (1, 1), mode=lax.GatherScatterMode.PROMISE_IN_BOUNDS)


def beside(mid, below, above, zlow, zhigh):
    depth, width = mid.shape
    zi = lax.broadcasted_iota(jnp.int32, mid.shape, 0)
    xi = lax.broadcasted_iota(jnp.int32, mid.shape, 1)
    total = below + above
    total = total + jnp.where(zi == 0, zlow, pltpu.roll(mid, 1, 0))
    total = total + jnp.where(zi == depth - 1, zhigh, pltpu.roll(mid, depth - 1, 0))
    total = total + jnp.where(xi == 0, 0.0, pltpu.roll(mid, 1, 1))
    total = total + jnp.where(xi == width - 1, 0.0, pltpu.roll(mid, width - 1, 1))
    return total


def lookup(label, table):
    result = jnp.full(label.shape, table[0], jnp.float32)
    for category in range(1, table.shape[0]):
        result = jnp.where(label == category, table[category], result)
    return result


def cycle_kernel(nnz, diffusivity_h, uptake_h, send_h, slot_h, length_h, ids_h, diag_h, off_h, cols_h,
                 value_h, source_h, label_h, basis_h,
                 out, correction,
                 diffusivity, uptake, send, slot, length, ids, diag_own, slot_row, off, cols,
                 value, source, label, basis,
                 sent, got, zface, yface, zhalo, yhalo, meta, table, pieces, turned,
                 conduct, weight, cpad, vpad, upad, tiles, sums, near_buf, far_buf,
                 target, target_s, spot, seconds, inverse, selector, state, rhs, diag, packed, low, high, factor,
                 last_low, last_high, last_factor, zgain, ygain, zsend, zrecv, yrecv,
                 load_sem, target_sem, a_send, a_recv, n_send, n_recv, f_send, f_recv, h_send, h_recv, own,
                 s_send, s_recv, t_send, t_recv, v_send, v_recv):
    rows, depth, width = value.shape
    groups = rhs.shape[0]
    slab, tile = lax.axis_index("slab"), lax.axis_index("tile")
    z, x, core = split_slab(slab)
    near = (z << 1) | core
    far = (x << 2) | tile
    order = (x << 4) | near
    place = (far << 4) | near

    barrier = pltpu.get_barrier_semaphore()

    def to_near(k):
        return near_device((near + k) & (NEAR - 1), x, tile)

    def to_far(k):
        return far_device((far + k) & (FAR - 1), z, core)

    def to_slab(k):
        return (slab + k) & (SLABS - 1), tile

    def greet(device):
        pl.semaphore_signal(barrier, inc=1, device_id=device, device_id_type=MESH)

    loop(SLABS // 4, SLABS, lambda k: greet(to_slab(k)))
    loop(1, SLABS // 4, lambda k: greet(to_slab(k)))
    loop(0, XS * (YS - 1), lambda k: greet(
        ((z << 3) | (((x + k) & 3) << 1) | core, (tile + 1 + (k >> 2)) & (YS - 1))))
    loads = [pltpu.make_async_copy(*pair, load_sem.at[i]) for i, pair in enumerate((
        (slot_h, slot), (length_h, length), (slot_h, slot_row), (basis_h, basis), (off_h, off), (cols_h, cols),
        (ids_h, ids), (diag_h, diag_own), (diffusivity_h, diffusivity), (uptake_h, uptake), (send_h, send),
        (label_h, label), (value_h, value), (source_h, source)))]
    for load in loads:
        load.start()
    for load in loads[:11]:
        load.wait()

    lane8 = lax.broadcasted_iota(jnp.int32, (8, LANES), 1)
    row8 = lax.broadcasted_iota(jnp.int32, (8, LANES), 0)
    lane1 = lax.broadcasted_iota(jnp.int32, (1, LANES), 1)
    entry = jnp.minimum(((row8 & 1) << 4) + (lane8 >> 3), nnz - 1)
    blank = jnp.zeros((8, LANES - nnz), jnp.float32)
    wide_off = jnp.concatenate([off[...], blank], axis=1)
    wide_cols = jnp.concatenate([place_of(cols[...]).astype(jnp.float32), blank], axis=1)
    offs = jnp.zeros((8, LANES), jnp.float32)
    places = jnp.zeros((8, LANES), jnp.float32)
    diag_row = jnp.zeros((1, LANES), jnp.float32)
    id_row = jnp.zeros((1, LANES), jnp.int32)
    for r in range(8):
        mine = (lane8 & 7) == r
        offs = jnp.where(mine, lane_gather(jnp.broadcast_to(wide_off[r:r + 1], (8, LANES)), entry), offs)
        places = jnp.where(mine, lane_gather(jnp.broadcast_to(wide_cols[r:r + 1], (8, LANES)), entry), places)
        diag_row = jnp.where((lane1 & 7) == r, diag_own[r], diag_row)
        id_row = jnp.where((lane1 & 7) == r, place_of(ids[r]), id_row)
    slot_cell = jnp.zeros((1, LANES), jnp.int32)
    for e in range(SLABS):
        slot_cell = jnp.where(lane1 == slot[0, 0, e], e >> 3, slot_cell)
    held = slot_cell.astype(jnp.float32)
    group = lane1 >> 3
    second = offs[1:2]
    second = jnp.where(group == nnz - 16, diag_row, second)
    second = jnp.where(group == nnz - 15, id_row.astype(jnp.float32), second)
    second = jnp.where(group >= 12, pltpu.roll(held, 96, 1), second)
    fourth = jnp.where(group >= nnz - 16, pltpu.roll(held, 48, 1), places[1:2])
    meta[0:1] = offs[0:1]
    meta[1:2] = second
    meta[2:3] = places[0:1]
    meta[3:4] = fourth

    e_at = lax.broadcasted_iota(jnp.int32, (SLABS, SLABS), 1)
    m_at = lax.broadcasted_iota(jnp.int32, (SLABS, SLABS), 0)
    limit = jnp.zeros((SLABS, SLABS), jnp.int32)
    for c in range(8):
        limit = jnp.where((e_at >> 3) == c, length[0, 0, c], limit)
    chosen = (slot_row[0] == m_at) & ((e_at & 7) < limit)
    chooser = chosen.astype(jnp.float32).astype(jnp.bfloat16)

    def choose(k):
        at = pl.ds(pl.multiple_of(k * LANES, LANES), LANES)
        block = basis[:, :, at].astype(jnp.float32).reshape(SLABS, LANES).astype(jnp.bfloat16)
        pieces[k & 1, pl.ds(k >> 1, SLABS, stride=depth), :] = jnp.dot(
            chooser, block, preferred_element_type=jnp.float32)

    loop(0, 2 * depth, choose, 4)

    def settle(m):
        for h in range(2):
            sent[m, :, h * LANES:(h + 1) * LANES] = pieces[h, pl.ds(m * depth, depth), :].astype(jnp.bfloat16)

    loop(0, SLABS, settle, 4)
    for load in loads[11:13]:
        load.wait()

    def fill(y):
        c = lookup(label[y], diffusivity)
        v = value[y]
        cpad[y + 1] = c
        vpad[y + 1] = v
        upad[y + 1] = c * v
        conduct[y] = c
        zface[0, 0, pl.ds(y, 1)] = c[0:1]
        zface[1, 0, pl.ds(y, 1)] = c[depth - 1:depth]
        zface[0, 1, pl.ds(y, 1)] = v[0:1]
        zface[1, 1, pl.ds(y, 1)] = v[depth - 1:depth]

    loop(0, rows, fill, 4)
    for side, at in ((0, 1), (1, rows)):
        yface[side, 0] = cpad[at]
        yface[side, 1] = vpad[at]

    pl.semaphore_wait(barrier, SLABS - 1 + XS * (YS - 1))

    halos = (
        remote(zface.at[1], zhalo.at[0], h_send.at[0], h_recv.at[0], to_slab(1)),
        remote(zface.at[0], zhalo.at[1], h_send.at[1], h_recv.at[1], to_slab(SLABS - 1)),
        remote(yface.at[1], yhalo.at[0], h_send.at[2], h_recv.at[2], (slab, (tile + 1) & 3)),
        remote(yface.at[0], yhalo.at[1], h_send.at[3], h_recv.at[3], (slab, (tile + 3) & 3)),
    )
    mine = pltpu.make_async_copy(meta, table.at[place], own.at[0])
    mine.start()
    kept = pltpu.make_async_copy(sent.at[slab], got.at[order], own.at[1])
    kept.start()
    block = table.at[pl.ds(far * NEAR, NEAR)]

    def near_copy(k):
        return remote(meta, table.at[place], n_send.at[k], n_recv.at[k], to_near(k))

    def line_copy(k):
        device = ((z << 3) | (((x + k) & 3) << 1) | core, tile)
        return remote(block, block, f_send.at[k], f_recv.at[k], device)

    def far_copy(k):
        device = ((z << 3) | (((x + k) & 3) << 1) | core, (tile + 1 + (k >> 2)) & (YS - 1))
        return remote(block, block, f_send.at[XS + k], f_recv.at[XS + k], device)

    def basis_copy(k):
        return remote(sent.at[(slab + k) & (SLABS - 1)], got.at[order], a_send.at[k], a_recv.at[k], to_slab(k))

    loop(1, NEAR, lambda k: near_copy(k).start())
    for copy in halos:
        copy.start()
    loop(1, SLABS, lambda k: basis_copy(k).start())
    mine.wait()
    kept.wait()
    loop(1, NEAR, lambda k: near_copy(k).wait())
    loop(1, XS, lambda k: line_copy(k).start())
    loop(0, XS * (YS - 1), lambda k: far_copy(k).start())
    for copy in halos:
        copy.wait()

    loads[13].wait()

    has_low = jnp.where(slab > 0, 1.0, 0.0)
    has_high = jnp.where(slab < SLABS - 1, 1.0, 0.0)
    for side, at, flag in ((0, 0, jnp.where(tile > 0, 1.0, 0.0)), (1, rows + 1, jnp.where(tile < YS - 1, 1.0, 0.0))):
        c = yhalo[side, 0] * flag
        v = yhalo[side, 1] * flag
        cpad[at] = c
        vpad[at] = v
        upad[at] = c * v

    def plane(y):
        c, v, u = cpad[y + 1], vpad[y + 1], upad[y + 1]
        clow = zhalo[0, 0, pl.ds(y, 1)] * has_low
        chigh = zhalo[1, 0, pl.ds(y, 1)] * has_high
        vlow = zhalo[0, 1, pl.ds(y, 1)] * has_low
        vhigh = zhalo[1, 1, pl.ds(y, 1)] * has_high
        csum = beside(c, cpad[y], cpad[y + 2], clow, chigh)
        vsum = beside(v, vpad[y], vpad[y + 2], vlow, vhigh)
        usum = beside(u, upad[y], upad[y + 2], clow * vlow, chigh * vhigh)
        diagonal = lookup(label[y], uptake) + 3.0 * c + 0.5 * csum
        residual = source[y] - (diagonal * v - 0.5 * (c * vsum + usum))
        tiles[y] = residual.astype(jnp.bfloat16).astype(jnp.float32)
        weight[y] = OMEGA / diagonal

    loop(0, rows, plane, 2)

    row_at = lax.broadcasted_iota(jnp.int32, (rows, LANES), 0)
    lane_at = lax.broadcasted_iota(jnp.int32, (rows, LANES), 1)
    to_row = jnp.full((rows, LANES), -1, jnp.int32)
    for p in range(SLABS):
        to_row = jnp.where(lane_at == p, send[0, 0, 0, ordered_slab(p)], to_row)
    selector[...] = jnp.where(to_row == row_at, 1.0, 0.0)

    loop(1, XS, lambda k: line_copy(k).wait())
    lane = lax.broadcasted_iota(jnp.int32, (NEAR, LANES), 1)
    own_row = lax.broadcasted_iota(jnp.int32, (NEAR, LANES), 0)
    for x_from in range(XS):
        own_rows = table[pl.ds(((x_from << 2) | tile) << 4, NEAR)]
        first, second = own_rows[:, 1], own_rows[:, 3]
        picked = jnp.where((lane == 96 + slab) & (slab < 32), first, 0.0)
        picked = picked + jnp.where((lane == 48 + slab) & (slab >= 32), second, 0.0)
        cell = jnp.sum(picked, axis=1, keepdims=True).astype(jnp.int32)
        index = jnp.sum(jnp.where(lane == 88 + cell, first, 0.0), axis=1, keepdims=True).astype(jnp.int32)
        target[x_from * NEAR:(x_from + 1) * NEAR, :] = jnp.broadcast_to(index, (NEAR, LANES))
        spot[x_from * NEAR:(x_from + 1) * NEAR, :] = own_row * 8 + cell
    own_place = jnp.zeros((NEAR, LANES), jnp.int32)
    for r in range(8):
        own_place = jnp.where(own_row == r, place_of(ids[r]), own_place)
    target[SLABS:] = own_place
    to_scalar = pltpu.make_async_copy(target, target_s, target_sem.at[0])
    to_scalar.start()


    loop(1, SLABS, lambda k: basis_copy(k).wait())

    def product(p):
        terms = got[p].astype(jnp.float32) * tiles[send[0, 0, 0, ordered_slab(p)]]
        folded = terms[:, :LANES] + terms[:, LANES:]
        sums[pl.ds(p, 1)] = jnp.sum(folded, axis=0, keepdims=True)

    loop(0, SLABS, product, 8)
    products = jnp.broadcast_to(jnp.sum(sums[...], axis=1, keepdims=True), (SLABS, LANES))
    lane64 = lax.broadcasted_iota(jnp.int32, (SLABS, LANES), 1)
    placed = jnp.where(lane64 == spot[...], products, 0.0)
    for x_to in range(XS):
        near_buf[near, pl.ds(x_to, 1)] = jnp.sum(placed[x_to * NEAR:(x_to + 1) * NEAR], axis=0, keepdims=True)

    def near_part(k):
        return remote(near_buf.at[near], near_buf.at[near], s_send.at[k], s_recv.at[k], to_near(k))

    def far_part(k):
        return remote(far_buf.at[far], far_buf.at[far], t_send.at[k], t_recv.at[k], to_far(k))

    loop(1, NEAR, lambda k: near_part(k).start())

    def unfold(p):
        for h in range(2):
            pieces[h, pl.ds(p * depth, depth), :] = got[p, :, h * LANES:(h + 1) * LANES].astype(jnp.float32)

    loop(0, SLABS, unfold, 4)

    def turn(k):
        turned[k] = pieces[k & 1, pl.ds(k >> 1, SLABS, stride=depth), :].astype(jnp.bfloat16)

    loop(0, 2 * depth, turn, 4)

    for side, at, inside in ((0, 0, slab > 0), (1, depth - 1, slab < SLABS - 1)):
        flag = jnp.where(inside, 0.5, 0.0)

        def gain(y):
            line = pl.ds(y, 1)
            pair = conduct[y][at:at + 1] + zhalo[side, 0, line]
            zgain[side, line] = weight[y][at:at + 1] * pair * flag

        loop(0, rows, gain, 4)
    for side, at, inside in ((0, 0, tile > 0), (1, rows - 1, tile < YS - 1)):
        flag = jnp.where(inside, 0.5, 0.0)
        ygain[side] = weight[at] * (conduct[at] + yhalo[side, 0]) * flag

    loop(1, NEAR, lambda k: near_part(k).wait())
    far_buf[far] = jnp.sum(near_buf[...], axis=0)
    loop(1, FAR, lambda k: far_part(k).start())
    loop(0, XS * (YS - 1), lambda k: far_copy(k).wait())

    mine = own_row == lane >> 3
    used = lane < (nnz - 16) * 8
    is_diag = lane >> 3 == nnz - 16

    def squeeze(values):
        for shift in (8, 16, 32, 64):
            values = values + pltpu.roll(values, shift, 1)
        return jnp.sum(jnp.where(mine, values, 0.0), axis=0, keepdims=True)

    def prepare(g):
        at = pl.ds(pl.multiple_of(g * NEAR, NEAR), NEAR)
        block = table[at]
        second = block[:, 1]
        diag[pl.ds(g, 1)] = squeeze(jnp.where(is_diag, second, 0.0))
        seconds[at] = second
        factor[0, at] = block[:, 0]
        factor[1, at] = jnp.where(used, second, 0.0)
        for b in range(2):
            index = block[:, 2 + b].astype(jnp.int32)
            low[b, at] = index & (LANES - 1)
            high[b, at] = index >> 7

    loop(0, groups, prepare, 2)
    to_scalar.wait()

    def fetch(p):
        index = target_s[p, 0]
        line, here = pl.ds((index >> 3) & (NEAR * FAR - 1), 1), pl.ds(p, 1)
        keep = (lane1 & 7) == (index & 7)
        for b in range(2):
            last_factor[b, here] = jnp.where(keep, factor[b, line], 0.0)
            last_low[b, here] = low[b, line]
            last_high[b, here] = high[b, line]

    loop(0, SLABS + NEAR, fetch, 4)

    line_at = lax.broadcasted_iota(jnp.int32, (NEAR * FAR, LANES), 0)
    lane_of = lax.broadcasted_iota(jnp.int32, (NEAR * FAR, LANES), 1)
    arrive = (((line_at >> 4) & 3) << 2) | (line_at >> 6)
    inverse[...] = jnp.zeros(inverse.shape, jnp.float32)

    def invert(c):
        number = lane_gather(seconds[...], jnp.full((NEAR * FAR, LANES), 88, jnp.int32) + c).astype(jnp.int32)
        code = jnp.where(lane_of < NEAR, arrive, ((line_at & (NEAR - 1)) << 3) + c)
        group_hit = ((number >> 7) == (lane_of & (NEAR - 1))) & (lane_of < 2 * NEAR)
        coded = jnp.where(group_hit, code, 0).astype(jnp.float32).astype(jnp.bfloat16)
        lane_hit = jnp.where((number & (LANES - 1)) == lane_of, 1.0, 0.0).astype(jnp.bfloat16)
        inverse[...] += lax.dot_general(coded, lane_hit, (((0,), (0,)), ((), ())),
                                        preferred_element_type=jnp.float32)[0:2 * NEAR]

    loop(0, 8, invert)

    loop(1, FAR, lambda k: far_part(k).wait())
    for y_from in range(YS):
        arrived = far_buf[y_from]
        for x_from in range(1, XS):
            arrived = arrived + far_buf[(x_from << 2) | y_from]
        state[y_from * XS:(y_from + 1) * XS] = arrived
    from_row, from_lane = inverse[0:NEAR].astype(jnp.int32), inverse[NEAR:].astype(jnp.int32)
    ordered = jnp.zeros((groups, LANES), jnp.float32)
    for g in range(groups):
        taken = lane_gather(jnp.broadcast_to(state[pl.ds(g, 1)], (groups, LANES)), from_lane)
        ordered = jnp.where(from_row == g, taken, ordered)
    rhs[...] = ordered

    state[...] = rhs[...] / diag[...]

    def pick(low_ref, high_ref, factor_ref, b, start):
        at = pl.ds(start, 8)
        lane_of, row = low_ref[b, at], high_ref[b, at]
        found = [lane_gather(packed[q], lane_of) for q in range(8)]
        bit = 1
        while len(found) > 1:
            odd = (row & bit) != 0
            found = [jnp.where(odd, found[2 * i + 1], found[2 * i]) for i in range(len(found) // 2)]
            bit = bit * 2
        word = found[0]
        number = jnp.where((row & 8) != 0, word >> 16, (word << 16) >> 16)
        return number.astype(jnp.float32) * factor_ref[b, at]

    def pack():
        now = state[...]
        top = jnp.maximum(jnp.max(jnp.max(jnp.abs(now), axis=1, keepdims=True), axis=0, keepdims=True), 1e-34)
        whole = jnp.round(now * (FULL / top)).astype(jnp.int32)
        word = (whole[8:16] << 16) + (whole[0:8] & 0xFFFF)
        for q in range(8):
            packed[q] = jnp.broadcast_to(word[q:q + 1], (8, LANES))
        return top * (1.0 / FULL)

    for repeat in range(COARSE_SWEEPS - 2):
        scale = pack()

        def relax_group(g):
            parts = []
            for half in range(2):
                start = pl.multiple_of(g * NEAR + half * 8, 8)
                parts.append(pick(low, high, factor, 0, start) + pick(low, high, factor, 1, start))
            total = jnp.concatenate(parts, axis=0)
            state[pl.ds(g, 1)] = (rhs[pl.ds(g, 1)] - squeeze(total) * scale) / diag[pl.ds(g, 1)]

        loop(0, groups, relax_group, 4)

    scale = pack()
    lane_all = lax.broadcasted_iota(jnp.int32, (SLABS + NEAR, LANES), 1)
    right = jnp.zeros((SLABS + NEAR, LANES), jnp.float32)
    below = jnp.zeros((SLABS + NEAR, LANES), jnp.float32)
    for g in range(groups):
        hit = target[...] - g * LANES == lane_all
        right = jnp.where(hit, rhs[pl.ds(g, 1)], right)
        below = jnp.where(hit, diag[pl.ds(g, 1)], below)
    coupled = jnp.concatenate([
        pick(last_low, last_high, last_factor, 0, p) + pick(last_low, last_high, last_factor, 1, p)
        for p in range(0, SLABS + NEAR, 8)], axis=0)
    solved = jnp.sum(right - coupled * scale, axis=1, keepdims=True) / jnp.sum(below, axis=1, keepdims=True)
    solved = jnp.broadcast_to(solved, (SLABS + NEAR, LANES))
    scaled = solved[0:SLABS]
    mine8 = solved[SLABS:SLABS + 8]
    correction[...] = jnp.sum(jnp.where(row8 == lane8, mine8, 0.0), axis=0, keepdims=True)[:, 0:8]

    chooser = selector[:, 0:SLABS].astype(jnp.bfloat16)

    def deposit(k):
        terms = (scaled * turned[k].astype(jnp.float32)).astype(jnp.bfloat16)
        pieces[k & 1, pl.ds(k >> 1, rows, stride=depth), :] = jnp.dot(chooser, terms, preferred_element_type=jnp.float32)

    loop(0, 2 * depth, deposit, 4)
    none = jnp.zeros((depth, width), jnp.float32)
    for pad in (vpad, cpad, upad):
        pad[0] = none
        pad[rows + 1] = none

    def correct(y):
        at = pl.ds(y * depth, depth)
        v = value[y] + jnp.concatenate([pieces[0, at, :], pieces[1, at, :]], axis=1)
        vpad[y + 1] = v
        upad[y + 1] = conduct[y] * v
        zsend[0, 0, pl.ds(y, 1)] = v[0:1]
        zsend[0, 1, pl.ds(y, 1)] = v[depth - 1:depth]

    loop(0, rows, correct, 4)

    around = (to_slab(1), to_slab(SLABS - 1), (slab, (tile + 1) & 3), (slab, (tile + 3) & 3))
    for step in range(SMOOTH_SWEEPS):
        now = vpad if step == 0 else cpad
        copies = (
            remote(zsend.at[step, 1], zrecv.at[step, 0], v_send.at[step, 0], v_recv.at[step, 0], around[0]),
            remote(zsend.at[step, 0], zrecv.at[step, 1], v_send.at[step, 1], v_recv.at[step, 1], around[1]),
            remote(now.at[rows], yrecv.at[step, 0], v_send.at[step, 2], v_recv.at[step, 2], around[2]),
            remote(now.at[1], yrecv.at[step, 1], v_send.at[step, 3], v_recv.at[step, 3], around[3]),
        )
        for copy in copies:
            copy.start()

        if step > 0:
            def product(y):
                upad[y + 1] = conduct[y] * now[y + 1]
            loop(0, rows, product, 4)

        def inner(y):
            v = now[y + 1]
            vsum = beside(v, now[y], now[y + 2], 0.0, 0.0)
            usum = beside(upad[y + 1], upad[y], upad[y + 2], 0.0, 0.0)
            coupled = 0.5 * (conduct[y] * vsum + usum)
            relaxed = (1.0 - OMEGA) * v + weight[y] * (source[y] + coupled)
            if step == 0:
                cpad[y + 1] = relaxed
            else:
                out[y] = relaxed

        loop(0, rows, inner, 2)
        for copy in copies:
            copy.wait()
        later, shift = (cpad, 1) if step == 0 else (out, 0)
        later[shift] = later[shift] + ygain[0] * yrecv[step, 0]
        later[shift + rows - 1] = later[shift + rows - 1] + ygain[1] * yrecv[step, 1]

        def close(y):
            line = pl.ds(y, 1)
            lowest = later[y + shift, 0:1] + zgain[0, line] * zrecv[step, 0, line]
            highest = later[y + shift, depth - 1:depth] + zgain[1, line] * zrecv[step, 1, line]
            later[y + shift, 0:1] = lowest
            later[y + shift, depth - 1:depth] = highest
            if step + 1 < SMOOTH_SWEEPS:
                zsend[step + 1, 0, line] = lowest
                zsend[step + 1, 1, line] = highest

        loop(0, rows, close, 4)


def cycle(nnz, cells, diffusivity, uptake, send, slot, length, ids, diag, off, cols, value, source, label, basis):
    rows, depth, width = value.shape
    f32, bf16, i32 = jnp.float32, jnp.bfloat16, jnp.int32
    vmem, smem, dma = pltpu.VMEM, pltpu.SMEM, pltpu.SemaphoreType.DMA
    groups = cells // LANES
    reads = SLABS + NEAR
    block, padded = vmem(value.shape, f32), vmem((rows + 2, depth, width), f32)
    zfaces, yfaces = vmem((2, 2, rows, width), f32), vmem((2, 2, depth, width), f32)
    entries = (2, NEAR * FAR, LANES)
    return pl.pallas_call(
        functools.partial(cycle_kernel, nnz),
        out_shape=(jax.ShapeDtypeStruct(value.shape, f32), jax.ShapeDtypeStruct((1, 8), f32)),
        in_specs=[HBM] * 13,
        out_specs=(VMEM,) * 2,
        scratch_shapes=[
            smem(diffusivity.shape, f32), smem(uptake.shape, f32), smem(send.shape, i32), smem(slot.shape, i32),
            smem(length.shape, i32), smem(ids.shape, i32), smem(diag.shape, f32),
            vmem(slot.shape, i32), vmem(off.shape, f32), vmem(cols.shape, i32),
            block, block, vmem(label.shape, i32), vmem(basis.shape, bf16),
            vmem((SLABS, depth, width), bf16), vmem((SLABS, depth, width), bf16), zfaces, yfaces, zfaces, yfaces,
            vmem((4, LANES), f32), vmem((NEAR * FAR, 4, LANES), f32), vmem((2, SLABS * depth, LANES), f32),
            vmem((2 * depth, SLABS, LANES), bf16),
            block, block, padded, padded, padded, block, vmem((SLABS, LANES), f32),
            vmem((NEAR, XS, LANES), f32), vmem((FAR, XS, LANES), f32),
            vmem((reads, LANES), i32), smem((reads, LANES), i32), vmem((SLABS, LANES), i32),
            vmem((NEAR * FAR, LANES), f32), vmem((2 * NEAR, LANES), f32), vmem((rows, LANES), f32),
            vmem((groups, LANES), f32), vmem((groups, LANES), f32), vmem((groups, LANES), f32),
            vmem((8, 8, LANES), i32), vmem(entries, i32), vmem(entries, i32), vmem(entries, f32),
            vmem((2, reads, LANES), i32), vmem((2, reads, LANES), i32), vmem((2, reads, LANES), f32),
            vmem((2, rows, width), f32), vmem((2, depth, width), f32),
            vmem((SMOOTH_SWEEPS, 2, rows, width), f32), vmem((SMOOTH_SWEEPS, 2, rows, width), f32),
            vmem((SMOOTH_SWEEPS, 2, depth, width), f32),
            dma((14,)), dma((1,)),
            dma((SLABS,)), dma((SLABS,)), dma((NEAR,)), dma((NEAR,)), dma((FAR,)), dma((FAR,)),
            dma((4,)), dma((4,)), dma((2,)), dma((NEAR,)), dma((NEAR,)), dma((FAR,)), dma((FAR,)),
            dma((SMOOTH_SWEEPS, 4)), dma((SMOOTH_SWEEPS, 4)),
        ],
        compiler_params=pltpu.CompilerParams(collective_id=0, has_side_effects=True, vmem_limit_bytes=48 << 20),
        name="cycle",
    )(diffusivity, uptake, send, slot, length, ids, diag, off, cols, value, source, label, basis)


def shards(solution, source, phase_label, phase_diffusivity, phase_uptake, send_tiles, support_slot, support_len,
           coarse_ids, basis_values, coarse_diag, coarse_off, coarse_cols):
    nnz = coarse_off.shape[1]
    cells = basis_values.shape[0] * NEAR * FAR
    send = send_tiles.transpose(0, 1, 3, 2)
    operands = [pltpu.with_memory_space_constraint(operand, pltpu.HBM) for operand in (
        solution, source, phase_label, basis_values, coarse_off, coarse_cols, phase_diffusivity, phase_uptake, send,
        support_slot, support_len, coarse_ids, coarse_diag)]
    (solution, source, phase_label, basis_values, coarse_off, coarse_cols, phase_diffusivity, phase_uptake, send,
     support_slot, support_len, coarse_ids, coarse_diag) = operands
    new_solution, correction = cycle(
        nnz, cells, phase_diffusivity, phase_uptake, send, support_slot, support_len, coarse_ids, coarse_diag,
        coarse_off, coarse_cols, solution, source, phase_label, basis_values)
    return new_solution, correction.reshape(correction.shape[1])


def solution(mesh):
    placed = (
        P("tile", "slab", None),
        P("tile", "slab", None),
        P("tile", "slab", None),
        P(),
        P(),
        P("slab", "tile", None, None),
        P("slab", "tile", None),
        P("slab", "tile", None),
        P(("slab", "tile")),
        P(("slab", "tile"), None, None),
        P(("slab", "tile")),
        P(("slab", "tile"), None),
        P(("slab", "tile"), None),
    )
    return jax.shard_map(
        shards,
        mesh=mesh,
        in_specs=placed,
        out_specs=(P("tile", "slab", None), P(("slab", "tile"))),
        check_vma=False,
    )
```

```python
import functools

import jax
import jax.numpy as jnp
from jax import lax
from jax.experimental import pallas as pl
from jax.experimental.pallas import tpu as pltpu
from jax.sharding import PartitionSpec as P

COARSE_SWEEPS = 4
SMOOTH_SWEEPS = 2
OMEGA = 0.8
MESH = pl.DeviceIdType.MESH
LANES = 128
FULL = 32760.0

ZS, XS, CORES, YS = 8, 4, 2, 4
NEAR = ZS * CORES
FAR = XS * YS
SLABS = ZS * XS * CORES


def split_slab(slab):
    return slab >> 3, (slab >> 1) & 3, slab & 1


def near_device(near, x, tile):
    return ((near >> 1) << 3) | (x << 1) | (near & 1), tile


def far_device(far, z, core):
    return (z << 3) | ((far >> 2) << 1) | core, far & 3


def ordered_slab(order):
    return near_device(order & (NEAR - 1), order >> 4, 0)[0]


def table_row(far, near):
    return ((near >> 3) << 7) | (far << 3) | (near & 7)


def place_of(index):
    owner, row = index >> 3, index & 7
    slab, tile = owner >> 2, owner & 3
    z, x, core = split_slab(slab)
    return (table_row((x << 2) | tile, (z << 1) | core) << 3) | row


VMEM = pl.BlockSpec(memory_space=pltpu.VMEM)
HBM = pl.BlockSpec(memory_space=pltpu.HBM)


def remote(src, dst, send_sem, recv_sem, device):
    return pltpu.make_async_remote_copy(
        src_ref=src, dst_ref=dst, send_sem=send_sem, recv_sem=recv_sem,
        device_id=device, device_id_type=MESH,
    )


def loop(low, high, act, unroll=1):
    def body(k, carry):
        act(k)
        return carry
    lax.fori_loop(low, high, body, 0, unroll=unroll)


def lane_gather(source, index):
    numbers = lax.GatherDimensionNumbers(
        offset_dims=(), collapsed_slice_dims=(1,), start_index_map=(1,),
        operand_batching_dims=(0,), start_indices_batching_dims=(0,),
    )
    return lax.gather(source, index[..., None], numbers, (1, 1), mode=lax.GatherScatterMode.PROMISE_IN_BOUNDS)


def beside(mid, below, above, zlow, zhigh):
    depth, width = mid.shape
    zi = lax.broadcasted_iota(jnp.int32, mid.shape, 0)
    xi = lax.broadcasted_iota(jnp.int32, mid.shape, 1)
    total = below + above
    total = total + jnp.where(zi == 0, zlow, pltpu.roll(mid, 1, 0))
    total = total + jnp.where(zi == depth - 1, zhigh, pltpu.roll(mid, depth - 1, 0))
    total = total + jnp.where(xi == 0, 0.0, pltpu.roll(mid, 1, 1))
    total = total + jnp.where(xi == width - 1, 0.0, pltpu.roll(mid, width - 1, 1))
    return total


def lookup(label, table):
    result = jnp.full(label.shape, table[0], jnp.float32)
    for category in range(1, table.shape[0]):
        result = jnp.where(label == category, table[category], result)
    return result


def cycle_kernel(nnz, diffusivity_h, uptake_h, send_h, slot_h, length_h, ids_h, diag_h, off_h, cols_h,
                 value_h, source_h, label_h, basis_h,
                 out, correction,
                 diffusivity, uptake, send, slot, length, ids, diag_own, slot_row, off, cols,
                 value, source, label, basis,
                 sent, got, zface, yface, zhalo, yhalo, meta, near_table, table, pieces, turned,
                 conduct, weight, cpad, vpad, upad, tiles, sums, near_buf, far_buf,
                 target, target_s, spot, seconds, inverse, selector, state, rhs, diag, packed, low, high, factor,
                 last_low, last_high, last_factor, zgain, ygain, zsend, zrecv, yrecv,
                 load_sem, target_sem, swap_sem, a_send, a_recv, n_send, n_recv, f_send, f_recv, h_send, h_recv, own,
                 s_send, s_recv, t_send, t_recv, v_send, v_recv):
    rows, depth, width = value.shape
    groups = rhs.shape[0]
    slab, tile = lax.axis_index("slab"), lax.axis_index("tile")
    z, x, core = split_slab(slab)
    near = (z << 1) | core
    far = (x << 2) | tile
    order = (x << 4) | near

    barrier = pltpu.get_barrier_semaphore()

    def to_near(k):
        return near_device((near + k) & (NEAR - 1), x, tile)

    def to_far(k):
        return far_device((far + k) & (FAR - 1), z, core)

    def to_slab(k):
        return (slab + k) & (SLABS - 1), tile

    def greet(device):
        pl.semaphore_signal(barrier, inc=1, device_id=device, device_id_type=MESH)

    for k in range(SLABS // 2, SLABS // 2 + SLABS - 1):
        greet(to_slab(k % SLABS + (k >= SLABS)))
    for k in range(XS * (YS - 1)):
        greet(((z << 3) | (((x + k) & 3) << 1) | core, (tile + 1 + (k >> 2)) & (YS - 1)))
    loads = [pltpu.make_async_copy(*pair, load_sem.at[i]) for i, pair in enumerate((
        (slot_h, slot), (length_h, length), (slot_h, slot_row), (basis_h, basis), (off_h, off), (cols_h, cols),
        (ids_h, ids), (diag_h, diag_own), (diffusivity_h, diffusivity), (uptake_h, uptake), (send_h, send),
        (label_h, label), (value_h, value), (source_h, source)))]
    for load in loads:
        load.start()
    for load in loads[:11]:
        load.wait()

    lane8 = lax.broadcasted_iota(jnp.int32, (8, LANES), 1)
    row8 = lax.broadcasted_iota(jnp.int32, (8, LANES), 0)
    lane1 = lax.broadcasted_iota(jnp.int32, (1, LANES), 1)
    entry = jnp.minimum(((row8 & 1) << 4) + (lane8 >> 3), nnz - 1)
    blank = jnp.zeros((8, LANES - nnz), jnp.float32)
    wide_off = jnp.concatenate([off[...], blank], axis=1)
    wide_cols = jnp.concatenate([place_of(cols[...]).astype(jnp.float32), blank], axis=1)
    offs = jnp.zeros((8, LANES), jnp.float32)
    places = jnp.zeros((8, LANES), jnp.float32)
    diag_row = jnp.zeros((1, LANES), jnp.float32)
    id_row = jnp.zeros((1, LANES), jnp.int32)
    for r in range(8):
        mine = (lane8 & 7) == r
        offs = jnp.where(mine, lane_gather(jnp.broadcast_to(wide_off[r:r + 1], (8, LANES)), entry), offs)
        places = jnp.where(mine, lane_gather(jnp.broadcast_to(wide_cols[r:r + 1], (8, LANES)), entry), places)
        diag_row = jnp.where((lane1 & 7) == r, diag_own[r], diag_row)
        id_row = jnp.where((lane1 & 7) == r, place_of(ids[r]), id_row)
    slot_cell = jnp.zeros((1, LANES), jnp.int32)
    for e in range(SLABS):
        slot_cell = jnp.where(lane1 == slot[0, 0, e], e >> 3, slot_cell)
    held = slot_cell.astype(jnp.float32)
    group = lane1 >> 3
    second = offs[1:2]
    second = jnp.where(group == nnz - 16, diag_row, second)
    second = jnp.where(group == nnz - 15, id_row.astype(jnp.float32), second)
    second = jnp.where(group >= 12, pltpu.roll(held, 96, 1), second)
    fourth = jnp.where(group >= nnz - 16, pltpu.roll(held, 48, 1), places[1:2])
    meta[0:1] = offs[0:1]
    meta[1:2] = second
    meta[2:3] = places[0:1]
    meta[3:4] = fourth

    e_at = lax.broadcasted_iota(jnp.int32, (SLABS, SLABS), 1)
    m_at = lax.broadcasted_iota(jnp.int32, (SLABS, SLABS), 0)
    limit = jnp.zeros((SLABS, SLABS), jnp.int32)
    for c in range(8):
        limit = jnp.where((e_at >> 3) == c, length[0, 0, c], limit)
    chosen = (slot_row[0] == m_at) & ((e_at & 7) < limit)
    chooser = chosen.astype(jnp.float32).astype(jnp.bfloat16)

    def choose(k):
        at = pl.ds(pl.multiple_of(k * LANES, LANES), LANES)
        block = basis[:, :, at].astype(jnp.float32).reshape(SLABS, LANES).astype(jnp.bfloat16)
        pieces[k & 1, pl.ds(k >> 1, SLABS, stride=depth), :] = jnp.dot(
            chooser, block, preferred_element_type=jnp.float32)

    loop(0, 2 * depth, choose, 4)

    def settle(m):
        for h in range(2):
            sent[m, :, h * LANES:(h + 1) * LANES] = pieces[h, pl.ds(m * depth, depth), :].astype(jnp.bfloat16)

    loop(0, SLABS, settle, 4)
    for load in loads[11:13]:
        load.wait()

    def fill(y):
        c = lookup(label[y], diffusivity)
        v = value[y]
        cpad[y + 1] = c
        vpad[y + 1] = v
        upad[y + 1] = c * v
        conduct[y] = c
        zface[0, 0, pl.ds(y, 1)] = c[0:1]
        zface[1, 0, pl.ds(y, 1)] = c[depth - 1:depth]
        zface[0, 1, pl.ds(y, 1)] = v[0:1]
        zface[1, 1, pl.ds(y, 1)] = v[depth - 1:depth]

    loop(0, rows, fill, 4)
    for side, at in ((0, 1), (1, rows)):
        yface[side, 0] = cpad[at]
        yface[side, 1] = vpad[at]

    pl.semaphore_wait(barrier, SLABS - 1 + XS * (YS - 1))

    halos = (
        remote(zface.at[1], zhalo.at[0], h_send.at[0], h_recv.at[0], to_slab(1)),
        remote(zface.at[0], zhalo.at[1], h_send.at[1], h_recv.at[1], to_slab(SLABS - 1)),
        remote(yface.at[1], yhalo.at[0], h_send.at[2], h_recv.at[2], (slab, (tile + 1) & 3)),
        remote(yface.at[0], yhalo.at[1], h_send.at[3], h_recv.at[3], (slab, (tile + 3) & 3)),
    )
    mine = pltpu.make_async_copy(meta, near_table.at[near], own.at[0])
    mine.start()
    kept = pltpu.make_async_copy(sent.at[slab], got.at[order], own.at[1])
    kept.start()
    half = core * (NEAR * FAR // 2)
    near_half = near_table.at[pl.ds(core * (NEAR // 2), NEAR // 2)]
    block = table.at[pl.ds(half + far * (NEAR // 2), NEAR // 2)]
    half_table = table.at[pl.ds(half, NEAR * FAR // 2)]
    swap = remote(half_table, half_table, swap_sem.at[0], swap_sem.at[1], (slab ^ 1, tile))

    def near_copy(k):
        return remote(meta, near_table.at[near], n_send.at[k], n_recv.at[k], to_near(k))

    def far_copy(k):
        return remote(near_half, block, f_send.at[k], f_recv.at[k], to_far(k))

    def basis_copy(k):
        return remote(sent.at[(slab + k) & (SLABS - 1)], got.at[order], a_send.at[k], a_recv.at[k], to_slab(k))

    loop(1, NEAR, lambda k: near_copy(k).start())
    for copy in halos:
        copy.start()
    loop(1, SLABS, lambda k: basis_copy(k).start())
    mine.wait()
    kept.wait()
    loop(1, NEAR, lambda k: near_copy(k).wait())
    loop(1, FAR, lambda k: far_copy(k).start())
    table[pl.ds(half + far * (NEAR // 2), NEAR // 2)] = near_table[pl.ds(core * (NEAR // 2), NEAR // 2)]
    for copy in halos:
        copy.wait()

    loads[13].wait()

    has_low = jnp.where(slab > 0, 1.0, 0.0)
    has_high = jnp.where(slab < SLABS - 1, 1.0, 0.0)
    for side, at, flag in ((0, 0, jnp.where(tile > 0, 1.0, 0.0)), (1, rows + 1, jnp.where(tile < YS - 1, 1.0, 0.0))):
        c = yhalo[side, 0] * flag
        v = yhalo[side, 1] * flag
        cpad[at] = c
        vpad[at] = v
        upad[at] = c * v

    def plane(y):
        c, v, u = cpad[y + 1], vpad[y + 1], upad[y + 1]
        clow = zhalo[0, 0, pl.ds(y, 1)] * has_low
        chigh = zhalo[1, 0, pl.ds(y, 1)] * has_high
        vlow = zhalo[0, 1, pl.ds(y, 1)] * has_low
        vhigh = zhalo[1, 1, pl.ds(y, 1)] * has_high
        csum = beside(c, cpad[y], cpad[y + 2], clow, chigh)
        vsum = beside(v, vpad[y], vpad[y + 2], vlow, vhigh)
        usum = beside(u, upad[y], upad[y + 2], clow * vlow, chigh * vhigh)
        diagonal = lookup(label[y], uptake) + 3.0 * c + 0.5 * csum
        residual = source[y] - (diagonal * v - 0.5 * (c * vsum + usum))
        tiles[y] = residual.astype(jnp.bfloat16).astype(jnp.float32)
        weight[y] = OMEGA / diagonal

    loop(0, rows, plane, 2)

    row_at = lax.broadcasted_iota(jnp.int32, (rows, LANES), 0)
    lane_at = lax.broadcasted_iota(jnp.int32, (rows, LANES), 1)
    to_row = jnp.full((rows, LANES), -1, jnp.int32)
    for p in range(SLABS):
        to_row = jnp.where(lane_at == p, send[0, 0, 0, ordered_slab(p)], to_row)
    selector[...] = jnp.where(to_row == row_at, 1.0, 0.0)

    loop(1, FAR, lambda k: far_copy(k).wait())
    swap.start()
    swap.wait()
    lane = lax.broadcasted_iota(jnp.int32, (NEAR, LANES), 1)
    own_row = lax.broadcasted_iota(jnp.int32, (NEAR, LANES), 0)
    for x_from in range(XS):
        at = ((x_from << 2) | tile) * (NEAR // 2)
        own_rows = jnp.concatenate(
            [table[pl.ds(at, NEAR // 2)], table[pl.ds(NEAR * FAR // 2 + at, NEAR // 2)]], axis=0)
        first, second = own_rows[:, 1], own_rows[:, 3]
        picked = jnp.where((lane == 96 + slab) & (slab < 32), first, 0.0)
        picked = picked + jnp.where((lane == 48 + slab) & (slab >= 32), second, 0.0)
        cell = jnp.sum(picked, axis=1, keepdims=True).astype(jnp.int32)
        index = jnp.sum(jnp.where(lane == 88 + cell, first, 0.0), axis=1, keepdims=True).astype(jnp.int32)
        target[x_from * NEAR:(x_from + 1) * NEAR, :] = jnp.broadcast_to(index, (NEAR, LANES))
        spot[x_from * NEAR:(x_from + 1) * NEAR, :] = own_row * 8 + cell
    own_place = jnp.zeros((NEAR, LANES), jnp.int32)
    for r in range(8):
        own_place = jnp.where(own_row == r, place_of(ids[r]), own_place)
    target[SLABS:] = own_place
    to_scalar = pltpu.make_async_copy(target, target_s, target_sem.at[0])
    to_scalar.start()


    loop(1, SLABS, lambda k: basis_copy(k).wait())

    def product(p):
        terms = got[p].astype(jnp.float32) * tiles[send[0, 0, 0, ordered_slab(p)]]
        folded = terms[:, :LANES] + terms[:, LANES:]
        sums[pl.ds(p, 1)] = jnp.sum(folded, axis=0, keepdims=True)

    loop(0, SLABS, product, 8)
    products = jnp.broadcast_to(jnp.sum(sums[...], axis=1, keepdims=True), (SLABS, LANES))
    lane64 = lax.broadcasted_iota(jnp.int32, (SLABS, LANES), 1)
    placed = jnp.where(lane64 == spot[...], products, 0.0)
    for x_to in range(XS):
        near_buf[near, pl.ds(x_to, 1)] = jnp.sum(placed[x_to * NEAR:(x_to + 1) * NEAR], axis=0, keepdims=True)

    def near_part(k):
        return remote(near_buf.at[near], near_buf.at[near], s_send.at[k], s_recv.at[k], to_near(k))

    def far_part(k):
        return remote(far_buf.at[far], far_buf.at[far], t_send.at[k], t_recv.at[k], to_far(k))

    loop(1, NEAR, lambda k: near_part(k).start())

    def unfold(p):
        for h in range(2):
            pieces[h, pl.ds(p * depth, depth), :] = got[p, :, h * LANES:(h + 1) * LANES].astype(jnp.float32)

    loop(0, SLABS, unfold, 4)

    def turn(k):
        turned[k] = pieces[k & 1, pl.ds(k >> 1, SLABS, stride=depth), :].astype(jnp.bfloat16)

    loop(0, 2 * depth, turn, 4)

    for side, at, inside in ((0, 0, slab > 0), (1, depth - 1, slab < SLABS - 1)):
        flag = jnp.where(inside, 0.5, 0.0)

        def gain(y):
            line = pl.ds(y, 1)
            pair = conduct[y][at:at + 1] + zhalo[side, 0, line]
            zgain[side, line] = weight[y][at:at + 1] * pair * flag

        loop(0, rows, gain, 4)
    for side, at, inside in ((0, 0, tile > 0), (1, rows - 1, tile < YS - 1)):
        flag = jnp.where(inside, 0.5, 0.0)
        ygain[side] = weight[at] * (conduct[at] + yhalo[side, 0]) * flag

    loop(1, NEAR, lambda k: near_part(k).wait())
    far_buf[far] = jnp.sum(near_buf[...], axis=0)
    loop(1, FAR, lambda k: far_part(k).start())

    mine = own_row == lane >> 3
    used = lane < (nnz - 16) * 8
    is_diag = lane >> 3 == nnz - 16

    def squeeze(values):
        for shift in (8, 16, 32, 64):
            values = values + pltpu.roll(values, shift, 1)
        return jnp.sum(jnp.where(mine, values, 0.0), axis=0, keepdims=True)

    def prepare(g):
        at = pl.ds(pl.multiple_of(g * NEAR, NEAR), NEAR)
        block = table[at]
        second = block[:, 1]
        diag[pl.ds(g, 1)] = squeeze(jnp.where(is_diag, second, 0.0))
        seconds[at] = second
        factor[0, at] = block[:, 0]
        factor[1, at] = jnp.where(used, second, 0.0)
        for b in range(2):
            index = block[:, 2 + b].astype(jnp.int32)
            low[b, at] = index & (LANES - 1)
            high[b, at] = index >> 7

    loop(0, groups, prepare, 2)
    to_scalar.wait()

    def fetch(p):
        index = target_s[p, 0]
        line, here = pl.ds((index >> 3) & (NEAR * FAR - 1), 1), pl.ds(p, 1)
        keep = (lane1 & 7) == (index & 7)
        for b in range(2):
            last_factor[b, here] = jnp.where(keep, factor[b, line], 0.0)
            last_low[b, here] = low[b, line]
            last_high[b, here] = high[b, line]

    loop(0, SLABS + NEAR, fetch, 4)

    line_at = lax.broadcasted_iota(jnp.int32, (NEAR * FAR, LANES), 0)
    lane_of = lax.broadcasted_iota(jnp.int32, (NEAR * FAR, LANES), 1)
    line_far = (line_at >> 3) & (FAR - 1)
    line_near = ((line_at >> 7) << 3) | (line_at & 7)
    arrive = ((line_far & 3) << 2) | (line_far >> 2)
    inverse[...] = jnp.zeros(inverse.shape, jnp.float32)

    def invert(c):
        number = lane_gather(seconds[...], jnp.full((NEAR * FAR, LANES), 88, jnp.int32) + c).astype(jnp.int32)
        code = jnp.where(lane_of < NEAR, arrive, (line_near << 3) + c)
        group_hit = ((number >> 7) == (lane_of & (NEAR - 1))) & (lane_of < 2 * NEAR)
        coded = jnp.where(group_hit, code, 0).astype(jnp.float32).astype(jnp.bfloat16)
        lane_hit = jnp.where((number & (LANES - 1)) == lane_of, 1.0, 0.0).astype(jnp.bfloat16)
        inverse[...] += lax.dot_general(coded, lane_hit, (((0,), (0,)), ((), ())),
                                        preferred_element_type=jnp.float32)[0:2 * NEAR]

    loop(0, 8, invert)

    loop(1, FAR, lambda k: far_part(k).wait())
    for y_from in range(YS):
        arrived = far_buf[y_from]
        for x_from in range(1, XS):
            arrived = arrived + far_buf[(x_from << 2) | y_from]
        state[y_from * XS:(y_from + 1) * XS] = arrived
    from_row, from_lane = inverse[0:NEAR].astype(jnp.int32), inverse[NEAR:].astype(jnp.int32)
    ordered = jnp.zeros((groups, LANES), jnp.float32)
    for g in range(groups):
        taken = lane_gather(jnp.broadcast_to(state[pl.ds(g, 1)], (groups, LANES)), from_lane)
        ordered = jnp.where(from_row == g, taken, ordered)
    rhs[...] = ordered

    state[...] = rhs[...] / diag[...]

    def pick(low_ref, high_ref, factor_ref, b, start):
        at = pl.ds(start, 8)
        lane_of, row = low_ref[b, at], high_ref[b, at]
        found = [lane_gather(packed[q], lane_of) for q in range(8)]
        bit = 1
        while len(found) > 1:
            odd = (row & bit) != 0
            found = [jnp.where(odd, found[2 * i + 1], found[2 * i]) for i in range(len(found) // 2)]
            bit = bit * 2
        word = found[0]
        number = jnp.where((row & 8) != 0, word >> 16, (word << 16) >> 16)
        return number.astype(jnp.float32) * factor_ref[b, at]

    def pack():
        now = state[...]
        top = jnp.maximum(jnp.max(jnp.max(jnp.abs(now), axis=1, keepdims=True), axis=0, keepdims=True), 1e-34)
        whole = jnp.round(now * (FULL / top)).astype(jnp.int32)
        word = (whole[8:16] << 16) + (whole[0:8] & 0xFFFF)
        for q in range(8):
            packed[q] = jnp.broadcast_to(word[q:q + 1], (8, LANES))
        return top * (1.0 / FULL)

    for repeat in range(COARSE_SWEEPS - 2):
        scale = pack()

        def relax_group(g):
            parts = []
            for half in range(2):
                start = pl.multiple_of(g * NEAR + half * 8, 8)
                parts.append(pick(low, high, factor, 0, start) + pick(low, high, factor, 1, start))
            total = jnp.concatenate(parts, axis=0)
            state[pl.ds(g, 1)] = (rhs[pl.ds(g, 1)] - squeeze(total) * scale) / diag[pl.ds(g, 1)]

        loop(0, groups, relax_group, 4)

    scale = pack()
    lane_all = lax.broadcasted_iota(jnp.int32, (SLABS + NEAR, LANES), 1)
    right = jnp.zeros((SLABS + NEAR, LANES), jnp.float32)
    below = jnp.zeros((SLABS + NEAR, LANES), jnp.float32)
    for g in range(groups):
        hit = target[...] - g * LANES == lane_all
        right = jnp.where(hit, rhs[pl.ds(g, 1)], right)
        below = jnp.where(hit, diag[pl.ds(g, 1)], below)
    coupled = jnp.concatenate([
        pick(last_low, last_high, last_factor, 0, p) + pick(last_low, last_high, last_factor, 1, p)
        for p in range(0, SLABS + NEAR, 8)], axis=0)
    solved = jnp.sum(right - coupled * scale, axis=1, keepdims=True) / jnp.sum(below, axis=1, keepdims=True)
    solved = jnp.broadcast_to(solved, (SLABS + NEAR, LANES))
    scaled = solved[0:SLABS]
    mine8 = solved[SLABS:SLABS + 8]
    correction[...] = jnp.sum(jnp.where(row8 == lane8, mine8, 0.0), axis=0, keepdims=True)[:, 0:8]

    chooser = selector[:, 0:SLABS].astype(jnp.bfloat16)

    def deposit(k):
        terms = (scaled * turned[k].astype(jnp.float32)).astype(jnp.bfloat16)
        pieces[k & 1, pl.ds(k >> 1, rows, stride=depth), :] = jnp.dot(chooser, terms, preferred_element_type=jnp.float32)

    loop(0, 2 * depth, deposit, 16)
    none = jnp.zeros((depth, width), jnp.float32)
    for pad in (vpad, cpad, upad):
        pad[0] = none
        pad[rows + 1] = none

    def correct(y):
        at = pl.ds(y * depth, depth)
        v = value[y] + jnp.concatenate([pieces[0, at, :], pieces[1, at, :]], axis=1)
        vpad[y + 1] = v
        upad[y + 1] = conduct[y] * v
        zsend[0, 0, pl.ds(y, 1)] = v[0:1]
        zsend[0, 1, pl.ds(y, 1)] = v[depth - 1:depth]

    loop(0, rows, correct, 4)

    around = (to_slab(1), to_slab(SLABS - 1), (slab, (tile + 1) & 3), (slab, (tile + 3) & 3))
    for step in range(SMOOTH_SWEEPS):
        now = vpad if step == 0 else cpad
        copies = (
            remote(zsend.at[step, 1], zrecv.at[step, 0], v_send.at[step, 0], v_recv.at[step, 0], around[0]),
            remote(zsend.at[step, 0], zrecv.at[step, 1], v_send.at[step, 1], v_recv.at[step, 1], around[1]),
            remote(now.at[rows], yrecv.at[step, 0], v_send.at[step, 2], v_recv.at[step, 2], around[2]),
            remote(now.at[1], yrecv.at[step, 1], v_send.at[step, 3], v_recv.at[step, 3], around[3]),
        )
        for copy in copies:
            copy.start()

        if step > 0:
            def product(y):
                upad[y + 1] = conduct[y] * now[y + 1]
            loop(0, rows, product, 4)

        def inner(y):
            v = now[y + 1]
            vsum = beside(v, now[y], now[y + 2], 0.0, 0.0)
            usum = beside(upad[y + 1], upad[y], upad[y + 2], 0.0, 0.0)
            coupled = 0.5 * (conduct[y] * vsum + usum)
            relaxed = (1.0 - OMEGA) * v + weight[y] * (source[y] + coupled)
            if step == 0:
                cpad[y + 1] = relaxed
            else:
                out[y] = relaxed

        loop(0, rows, inner, 2)
        for copy in copies:
            copy.wait()
        later, shift = (cpad, 1) if step == 0 else (out, 0)
        later[shift] = later[shift] + ygain[0] * yrecv[step, 0]
        later[shift + rows - 1] = later[shift + rows - 1] + ygain[1] * yrecv[step, 1]

        def close(y):
            line = pl.ds(y, 1)
            lowest = later[y + shift, 0:1] + zgain[0, line] * zrecv[step, 0, line]
            highest = later[y + shift, depth - 1:depth] + zgain[1, line] * zrecv[step, 1, line]
            later[y + shift, 0:1] = lowest
            later[y + shift, depth - 1:depth] = highest
            if step + 1 < SMOOTH_SWEEPS:
                zsend[step + 1, 0, line] = lowest
                zsend[step + 1, 1, line] = highest

        loop(0, rows, close, 4)


def cycle(nnz, cells, diffusivity, uptake, send, slot, length, ids, diag, off, cols, value, source, label, basis):
    rows, depth, width = value.shape
    f32, bf16, i32 = jnp.float32, jnp.bfloat16, jnp.int32
    vmem, smem, dma = pltpu.VMEM, pltpu.SMEM, pltpu.SemaphoreType.DMA
    groups = cells // LANES
    reads = SLABS + NEAR
    block, padded = vmem(value.shape, f32), vmem((rows + 2, depth, width), f32)
    zfaces, yfaces = vmem((2, 2, rows, width), f32), vmem((2, 2, depth, width), f32)
    entries = (2, NEAR * FAR, LANES)
    return pl.pallas_call(
        functools.partial(cycle_kernel, nnz),
        out_shape=(jax.ShapeDtypeStruct(value.shape, f32), jax.ShapeDtypeStruct((1, 8), f32)),
        in_specs=[HBM] * 13,
        out_specs=(VMEM,) * 2,
        scratch_shapes=[
            smem(diffusivity.shape, f32), smem(uptake.shape, f32), smem(send.shape, i32), smem(slot.shape, i32),
            smem(length.shape, i32), smem(ids.shape, i32), smem(diag.shape, f32),
            vmem(slot.shape, i32), vmem(off.shape, f32), vmem(cols.shape, i32),
            block, block, vmem(label.shape, i32), vmem(basis.shape, bf16),
            vmem((SLABS, depth, width), bf16), vmem((SLABS, depth, width), bf16), zfaces, yfaces, zfaces, yfaces,
            vmem((4, LANES), f32), vmem((NEAR, 4, LANES), f32), vmem((NEAR * FAR, 4, LANES), f32), vmem((2, SLABS * depth, LANES), f32),
            vmem((2 * depth, SLABS, LANES), bf16),
            block, block, padded, padded, padded, block, vmem((SLABS, LANES), f32),
            vmem((NEAR, XS, LANES), f32), vmem((FAR, XS, LANES), f32),
            vmem((reads, LANES), i32), smem((reads, LANES), i32), vmem((SLABS, LANES), i32),
            vmem((NEAR * FAR, LANES), f32), vmem((2 * NEAR, LANES), f32), vmem((rows, LANES), f32),
            vmem((groups, LANES), f32), vmem((groups, LANES), f32), vmem((groups, LANES), f32),
            vmem((8, 8, LANES), i32), vmem(entries, i32), vmem(entries, i32), vmem(entries, f32),
            vmem((2, reads, LANES), i32), vmem((2, reads, LANES), i32), vmem((2, reads, LANES), f32),
            vmem((2, rows, width), f32), vmem((2, depth, width), f32),
            vmem((SMOOTH_SWEEPS, 2, rows, width), f32), vmem((SMOOTH_SWEEPS, 2, rows, width), f32),
            vmem((SMOOTH_SWEEPS, 2, depth, width), f32),
            dma((14,)), dma((1,)), dma((2,)),
            dma((SLABS,)), dma((SLABS,)), dma((NEAR,)), dma((NEAR,)), dma((FAR,)), dma((FAR,)),
            dma((4,)), dma((4,)), dma((2,)), dma((NEAR,)), dma((NEAR,)), dma((FAR,)), dma((FAR,)),
            dma((SMOOTH_SWEEPS, 4)), dma((SMOOTH_SWEEPS, 4)),
        ],
        compiler_params=pltpu.CompilerParams(collective_id=0, has_side_effects=True, vmem_limit_bytes=48 << 20),
        name="cycle",
    )(diffusivity, uptake, send, slot, length, ids, diag, off, cols, value, source, label, basis)


def shards(solution, source, phase_label, phase_diffusivity, phase_uptake, send_tiles, support_slot, support_len,
           coarse_ids, basis_values, coarse_diag, coarse_off, coarse_cols):
    nnz = coarse_off.shape[1]
    cells = basis_values.shape[0] * NEAR * FAR
    send = send_tiles.transpose(0, 1, 3, 2)
    operands = [pltpu.with_memory_space_constraint(operand, pltpu.HBM) for operand in (
        solution, source, phase_label, basis_values, coarse_off, coarse_cols, phase_diffusivity, phase_uptake, send,
        support_slot, support_len, coarse_ids, coarse_diag)]
    (solution, source, phase_label, basis_values, coarse_off, coarse_cols, phase_diffusivity, phase_uptake, send,
     support_slot, support_len, coarse_ids, coarse_diag) = operands
    new_solution, correction = cycle(
        nnz, cells, phase_diffusivity, phase_uptake, send, support_slot, support_len, coarse_ids, coarse_diag,
        coarse_off, coarse_cols, solution, source, phase_label, basis_values)
    return new_solution, correction.reshape(correction.shape[1])


def solution(mesh):
    placed = (
        P("tile", "slab", None),
        P("tile", "slab", None),
        P("tile", "slab", None),
        P(),
        P(),
        P("slab", "tile", None, None),
        P("slab", "tile", None),
        P("slab", "tile", None),
        P(("slab", "tile")),
        P(("slab", "tile"), None, None),
        P(("slab", "tile")),
        P(("slab", "tile"), None),
        P(("slab", "tile"), None),
    )
    return jax.shard_map(
        shards,
        mesh=mesh,
        in_specs=placed,
        out_specs=(P("tile", "slab", None), P(("slab", "tile"))),
        check_vma=False,
    )
```

```python
import functools

import jax
import jax.numpy as jnp
from jax import lax
from jax.experimental import pallas as pl
from jax.experimental.pallas import tpu as pltpu
from jax.sharding import PartitionSpec as P

COARSE_SWEEPS = 4
SMOOTH_SWEEPS = 2
OMEGA = 0.8
MESH = pl.DeviceIdType.MESH
LANES = 128
FULL = 32760.0

ZS, XS, CORES, YS = 8, 4, 2, 4
NEAR = ZS * CORES
FAR = XS * YS
SLABS = ZS * XS * CORES

NEAR_ORDER = sorted(range(1, NEAR), key=lambda k: abs(k - NEAR // 2))
FAR_ORDER = sorted(range(1, FAR), key=lambda k: abs((k >> 2) - XS // 2) + abs((k & 3) - YS // 2))


def split_slab(slab):
    return slab >> 3, (slab >> 1) & 3, slab & 1


def near_device(near, x, tile):
    return ((near >> 1) << 3) | (x << 1) | (near & 1), tile


def far_device(far, z, core):
    return (z << 3) | ((far >> 2) << 1) | core, far & 3


def ordered_slab(order):
    return near_device(order & (NEAR - 1), order >> 4, 0)[0]


def table_row(far, near):
    return ((near >> 3) << 7) | (far << 3) | (near & 7)


def place_of(index):
    owner, row = index >> 3, index & 7
    slab, tile = owner >> 2, owner & 3
    z, x, core = split_slab(slab)
    return (table_row((x << 2) | tile, (z << 1) | core) << 3) | row


VMEM = pl.BlockSpec(memory_space=pltpu.VMEM)
HBM = pl.BlockSpec(memory_space=pltpu.HBM)


def remote(src, dst, send_sem, recv_sem, device):
    return pltpu.make_async_remote_copy(
        src_ref=src, dst_ref=dst, send_sem=send_sem, recv_sem=recv_sem,
        device_id=device, device_id_type=MESH,
    )


def loop(low, high, act, unroll=1):
    def body(k, carry):
        act(k)
        return carry
    lax.fori_loop(low, high, body, 0, unroll=unroll)


def lane_gather(source, index):
    numbers = lax.GatherDimensionNumbers(
        offset_dims=(), collapsed_slice_dims=(1,), start_index_map=(1,),
        operand_batching_dims=(0,), start_indices_batching_dims=(0,),
    )
    return lax.gather(source, index[..., None], numbers, (1, 1), mode=lax.GatherScatterMode.PROMISE_IN_BOUNDS)


def beside(mid, below, above, zlow, zhigh):
    depth, width = mid.shape
    zi = lax.broadcasted_iota(jnp.int32, mid.shape, 0)
    xi = lax.broadcasted_iota(jnp.int32, mid.shape, 1)
    total = below + above
    total = total + jnp.where(zi == 0, zlow, pltpu.roll(mid, 1, 0))
    total = total + jnp.where(zi == depth - 1, zhigh, pltpu.roll(mid, depth - 1, 0))
    total = total + jnp.where(xi == 0, 0.0, pltpu.roll(mid, 1, 1))
    total = total + jnp.where(xi == width - 1, 0.0, pltpu.roll(mid, width - 1, 1))
    return total


def lookup(label, table):
    result = jnp.full(label.shape, table[0], jnp.float32)
    for category in range(1, table.shape[0]):
        result = jnp.where(label == category, table[category], result)
    return result


def cycle_kernel(nnz, diffusivity_h, uptake_h, send_h, slot_h, length_h, ids_h, diag_h, off_h, cols_h,
                 value_h, source_h, label_h, basis_h,
                 out, correction,
                 diffusivity, uptake, send, slot, length, ids, diag_own, slot_row, off, cols,
                 value, source, label, basis,
                 sent, got, zface, yface, zhalo, yhalo, meta, near_table, table, pieces, turned,
                 conduct, weight, cpad, vpad, upad, tiles, sums, near_buf, far_buf,
                 target, target_s, spot, seconds, inverse, selector, state, rhs, diag, packed, low, high, factor,
                 last_low, last_high, last_factor, zgain, ygain, zsend, zrecv, yrecv,
                 load_sem, target_sem, swap_sem, a_send, a_recv, n_send, n_recv, f_send, f_recv, h_send, h_recv, own,
                 s_send, s_recv, t_send, t_recv, v_send, v_recv):
    rows, depth, width = value.shape
    groups = rhs.shape[0]
    slab, tile = lax.axis_index("slab"), lax.axis_index("tile")
    z, x, core = split_slab(slab)
    near = (z << 1) | core
    far = (x << 2) | tile
    order = (x << 4) | near

    barrier = pltpu.get_barrier_semaphore()

    def to_near(k):
        return near_device((near + k) & (NEAR - 1), x, tile)

    def to_far(k):
        return far_device((far + k) & (FAR - 1), z, core)

    def to_slab(k):
        return (slab + k) & (SLABS - 1), tile

    def greet(device):
        pl.semaphore_signal(barrier, inc=1, device_id=device, device_id_type=MESH)

    for k in sorted(range(1, SLABS), key=lambda k: abs(k - SLABS // 2)):
        greet(to_slab(k))
    for k in range(XS * (YS - 1)):
        greet(((z << 3) | (((x + k) & 3) << 1) | core, (tile + 1 + (k >> 2)) & (YS - 1)))
    loads = [pltpu.make_async_copy(*pair, load_sem.at[i]) for i, pair in enumerate((
        (slot_h, slot), (length_h, length), (slot_h, slot_row), (basis_h, basis), (off_h, off), (cols_h, cols),
        (ids_h, ids), (diag_h, diag_own), (diffusivity_h, diffusivity), (uptake_h, uptake), (send_h, send),
        (label_h, label), (value_h, value), (source_h, source)))]
    for load in loads:
        load.start()
    for load in loads[:11]:
        load.wait()

    lane8 = lax.broadcasted_iota(jnp.int32, (8, LANES), 1)
    row8 = lax.broadcasted_iota(jnp.int32, (8, LANES), 0)
    lane1 = lax.broadcasted_iota(jnp.int32, (1, LANES), 1)
    entry = jnp.minimum(((row8 & 1) << 4) + (lane8 >> 3), nnz - 1)
    blank = jnp.zeros((8, LANES - nnz), jnp.float32)
    wide_off = jnp.concatenate([off[...], blank], axis=1)
    wide_cols = jnp.concatenate([place_of(cols[...]).astype(jnp.float32), blank], axis=1)
    offs = jnp.zeros((8, LANES), jnp.float32)
    places = jnp.zeros((8, LANES), jnp.float32)
    diag_row = jnp.zeros((1, LANES), jnp.float32)
    id_row = jnp.zeros((1, LANES), jnp.int32)
    for r in range(8):
        mine = (lane8 & 7) == r
        offs = jnp.where(mine, lane_gather(jnp.broadcast_to(wide_off[r:r + 1], (8, LANES)), entry), offs)
        places = jnp.where(mine, lane_gather(jnp.broadcast_to(wide_cols[r:r + 1], (8, LANES)), entry), places)
        diag_row = jnp.where((lane1 & 7) == r, diag_own[r], diag_row)
        id_row = jnp.where((lane1 & 7) == r, place_of(ids[r]), id_row)
    slot_cell = jnp.zeros((1, LANES), jnp.int32)
    for e in range(SLABS):
        slot_cell = jnp.where(lane1 == slot[0, 0, e], e >> 3, slot_cell)
    held = slot_cell.astype(jnp.float32)
    group = lane1 >> 3
    second = offs[1:2]
    second = jnp.where(group == nnz - 16, diag_row, second)
    second = jnp.where(group == nnz - 15, id_row.astype(jnp.float32), second)
    second = jnp.where(group >= 12, pltpu.roll(held, 96, 1), second)
    fourth = jnp.where(group >= nnz - 16, pltpu.roll(held, 48, 1), places[1:2])
    meta[0:1] = offs[0:1]
    meta[1:2] = second
    meta[2:3] = places[0:1]
    meta[3:4] = fourth

    e_at = lax.broadcasted_iota(jnp.int32, (SLABS, SLABS), 1)
    m_at = lax.broadcasted_iota(jnp.int32, (SLABS, SLABS), 0)
    limit = jnp.zeros((SLABS, SLABS), jnp.int32)
    for c in range(8):
        limit = jnp.where((e_at >> 3) == c, length[0, 0, c], limit)
    chosen = (slot_row[0] == m_at) & ((e_at & 7) < limit)
    chooser = chosen.astype(jnp.float32).astype(jnp.bfloat16)

    def choose(k):
        at = pl.ds(pl.multiple_of(k * LANES, LANES), LANES)
        block = basis[:, :, at].astype(jnp.float32).reshape(SLABS, LANES).astype(jnp.bfloat16)
        pieces[k & 1, pl.ds(k >> 1, SLABS, stride=depth), :] = jnp.dot(
            chooser, block, preferred_element_type=jnp.float32)

    loop(0, 2 * depth, choose, 4)

    def settle(m):
        for h in range(2):
            sent[m, :, h * LANES:(h + 1) * LANES] = pieces[h, pl.ds(m * depth, depth), :].astype(jnp.bfloat16)

    loop(0, SLABS, settle, 4)
    for load in loads[11:13]:
        load.wait()

    def fill(y):
        c = lookup(label[y], diffusivity)
        v = value[y]
        cpad[y + 1] = c
        vpad[y + 1] = v
        upad[y + 1] = c * v
        conduct[y] = c
        zface[0, 0, pl.ds(y, 1)] = c[0:1]
        zface[1, 0, pl.ds(y, 1)] = c[depth - 1:depth]
        zface[0, 1, pl.ds(y, 1)] = v[0:1]
        zface[1, 1, pl.ds(y, 1)] = v[depth - 1:depth]

    loop(0, rows, fill, 4)
    for side, at in ((0, 1), (1, rows)):
        yface[side, 0] = cpad[at]
        yface[side, 1] = vpad[at]

    pl.semaphore_wait(barrier, SLABS - 1 + XS * (YS - 1))

    halos = (
        remote(zface.at[1], zhalo.at[0], h_send.at[0], h_recv.at[0], to_slab(1)),
        remote(zface.at[0], zhalo.at[1], h_send.at[1], h_recv.at[1], to_slab(SLABS - 1)),
        remote(yface.at[1], yhalo.at[0], h_send.at[2], h_recv.at[2], (slab, (tile + 1) & 3)),
        remote(yface.at[0], yhalo.at[1], h_send.at[3], h_recv.at[3], (slab, (tile + 3) & 3)),
    )
    mine = pltpu.make_async_copy(meta, near_table.at[near], own.at[0])
    mine.start()
    kept = pltpu.make_async_copy(sent.at[slab], got.at[order], own.at[1])
    kept.start()
    half = core * (NEAR * FAR // 2)
    near_half = near_table.at[pl.ds(core * (NEAR // 2), NEAR // 2)]
    block = table.at[pl.ds(half + far * (NEAR // 2), NEAR // 2)]
    half_table = table.at[pl.ds(half, NEAR * FAR // 2)]
    swap = remote(half_table, half_table, swap_sem.at[0], swap_sem.at[1], (slab ^ 1, tile))

    def near_copy(k):
        return remote(meta, near_table.at[near], n_send.at[k], n_recv.at[k], to_near(k))

    def far_copy(k):
        return remote(near_half, block, f_send.at[k], f_recv.at[k], to_far(k))

    def basis_copy(k):
        return remote(sent.at[(slab + k) & (SLABS - 1)], got.at[order], a_send.at[k], a_recv.at[k], to_slab(k))

    loop(1, NEAR, lambda k: near_copy(k).start())
    for copy in halos:
        copy.start()
    loop(1, SLABS, lambda k: basis_copy(k).start())
    mine.wait()
    kept.wait()
    loop(1, NEAR, lambda k: near_copy(k).wait())
    loop(1, FAR, lambda k: far_copy(k).start())
    table[pl.ds(half + far * (NEAR // 2), NEAR // 2)] = near_table[pl.ds(core * (NEAR // 2), NEAR // 2)]
    for copy in halos:
        copy.wait()

    loads[13].wait()

    has_low = jnp.where(slab > 0, 1.0, 0.0)
    has_high = jnp.where(slab < SLABS - 1, 1.0, 0.0)
    for side, at, flag in ((0, 0, jnp.where(tile > 0, 1.0, 0.0)), (1, rows + 1, jnp.where(tile < YS - 1, 1.0, 0.0))):
        c = yhalo[side, 0] * flag
        v = yhalo[side, 1] * flag
        cpad[at] = c
        vpad[at] = v
        upad[at] = c * v

    def plane(y):
        c, v, u = cpad[y + 1], vpad[y + 1], upad[y + 1]
        clow = zhalo[0, 0, pl.ds(y, 1)] * has_low
        chigh = zhalo[1, 0, pl.ds(y, 1)] * has_high
        vlow = zhalo[0, 1, pl.ds(y, 1)] * has_low
        vhigh = zhalo[1, 1, pl.ds(y, 1)] * has_high
        csum = beside(c, cpad[y], cpad[y + 2], clow, chigh)
        vsum = beside(v, vpad[y], vpad[y + 2], vlow, vhigh)
        usum = beside(u, upad[y], upad[y + 2], clow * vlow, chigh * vhigh)
        diagonal = lookup(label[y], uptake) + 3.0 * c + 0.5 * csum
        residual = source[y] - (diagonal * v - 0.5 * (c * vsum + usum))
        tiles[y] = residual.astype(jnp.bfloat16).astype(jnp.float32)
        weight[y] = OMEGA / diagonal

    loop(0, rows, plane, 2)

    row_at = lax.broadcasted_iota(jnp.int32, (rows, LANES), 0)
    lane_at = lax.broadcasted_iota(jnp.int32, (rows, LANES), 1)
    to_row = jnp.full((rows, LANES), -1, jnp.int32)
    for p in range(SLABS):
        to_row = jnp.where(lane_at == p, send[0, 0, 0, ordered_slab(p)], to_row)
    selector[...] = jnp.where(to_row == row_at, 1.0, 0.0)

    loop(1, FAR, lambda k: far_copy(k).wait())
    swap.start()
    swap.wait()
    lane = lax.broadcasted_iota(jnp.int32, (NEAR, LANES), 1)
    own_row = lax.broadcasted_iota(jnp.int32, (NEAR, LANES), 0)
    for x_from in range(XS):
        at = ((x_from << 2) | tile) * (NEAR // 2)
        own_rows = jnp.concatenate(
            [table[pl.ds(at, NEAR // 2)], table[pl.ds(NEAR * FAR // 2 + at, NEAR // 2)]], axis=0)
        first, second = own_rows[:, 1], own_rows[:, 3]
        picked = jnp.where((lane == 96 + slab) & (slab < 32), first, 0.0)
        picked = picked + jnp.where((lane == 48 + slab) & (slab >= 32), second, 0.0)
        cell = jnp.sum(picked, axis=1, keepdims=True).astype(jnp.int32)
        index = jnp.sum(jnp.where(lane == 88 + cell, first, 0.0), axis=1, keepdims=True).astype(jnp.int32)
        target[x_from * NEAR:(x_from + 1) * NEAR, :] = jnp.broadcast_to(index, (NEAR, LANES))
        spot[x_from * NEAR:(x_from + 1) * NEAR, :] = own_row * 8 + cell
    own_place = jnp.zeros((NEAR, LANES), jnp.int32)
    for r in range(8):
        own_place = jnp.where(own_row == r, place_of(ids[r]), own_place)
    target[SLABS:] = own_place
    to_scalar = pltpu.make_async_copy(target, target_s, target_sem.at[0])
    to_scalar.start()


    loop(1, SLABS, lambda k: basis_copy(k).wait())

    def product(p):
        terms = got[p].astype(jnp.float32) * tiles[send[0, 0, 0, ordered_slab(p)]]
        folded = terms[:, :LANES] + terms[:, LANES:]
        sums[pl.ds(p, 1)] = jnp.sum(folded, axis=0, keepdims=True)

    loop(0, SLABS, product, 8)
    products = jnp.broadcast_to(jnp.sum(sums[...], axis=1, keepdims=True), (SLABS, LANES))
    lane64 = lax.broadcasted_iota(jnp.int32, (SLABS, LANES), 1)
    placed = jnp.where(lane64 == spot[...], products, 0.0)
    for x_to in range(XS):
        near_buf[near, pl.ds(x_to, 1)] = jnp.sum(placed[x_to * NEAR:(x_to + 1) * NEAR], axis=0, keepdims=True)

    def near_part(k):
        return remote(near_buf.at[near], near_buf.at[near], s_send.at[k], s_recv.at[k], to_near(k))

    def far_part(k):
        return remote(far_buf.at[far], far_buf.at[far], t_send.at[k], t_recv.at[k], to_far(k))

    for k in NEAR_ORDER:
        near_part(k).start()

    def unfold(p):
        for h in range(2):
            pieces[h, pl.ds(p * depth, depth), :] = got[p, :, h * LANES:(h + 1) * LANES].astype(jnp.float32)

    loop(0, SLABS, unfold, 4)

    def turn(k):
        turned[k] = pieces[k & 1, pl.ds(k >> 1, SLABS, stride=depth), :].astype(jnp.bfloat16)

    loop(0, 2 * depth, turn, 4)

    for side, at, inside in ((0, 0, slab > 0), (1, depth - 1, slab < SLABS - 1)):
        flag = jnp.where(inside, 0.5, 0.0)

        def gain(y):
            line = pl.ds(y, 1)
            pair = conduct[y][at:at + 1] + zhalo[side, 0, line]
            zgain[side, line] = weight[y][at:at + 1] * pair * flag

        loop(0, rows, gain, 4)
    for side, at, inside in ((0, 0, tile > 0), (1, rows - 1, tile < YS - 1)):
        flag = jnp.where(inside, 0.5, 0.0)
        ygain[side] = weight[at] * (conduct[at] + yhalo[side, 0]) * flag

    loop(1, NEAR, lambda k: near_part(k).wait(), 15)
    far_buf[far] = jnp.sum(near_buf[...], axis=0)
    for k in FAR_ORDER:
        far_part(k).start()

    mine = own_row == lane >> 3
    used = lane < (nnz - 16) * 8
    is_diag = lane >> 3 == nnz - 16

    def squeeze(values):
        for shift in (8, 16, 32, 64):
            values = values + pltpu.roll(values, shift, 1)
        return jnp.sum(jnp.where(mine, values, 0.0), axis=0, keepdims=True)

    def prepare(g):
        at = pl.ds(pl.multiple_of(g * NEAR, NEAR), NEAR)
        block = table[at]
        second = block[:, 1]
        diag[pl.ds(g, 1)] = squeeze(jnp.where(is_diag, second, 0.0))
        seconds[at] = second
        factor[0, at] = block[:, 0]
        factor[1, at] = jnp.where(used, second, 0.0)
        for b in range(2):
            index = block[:, 2 + b].astype(jnp.int32)
            low[b, at] = index & (LANES - 1)
            high[b, at] = index >> 7

    loop(0, groups, prepare, 2)
    to_scalar.wait()

    def fetch(p):
        index = target_s[p, 0]
        line, here = pl.ds((index >> 3) & (NEAR * FAR - 1), 1), pl.ds(p, 1)
        keep = (lane1 & 7) == (index & 7)
        for b in range(2):
            last_factor[b, here] = jnp.where(keep, factor[b, line], 0.0)
            last_low[b, here] = low[b, line]
            last_high[b, here] = high[b, line]

    loop(0, SLABS + NEAR, fetch, 4)

    line_at = lax.broadcasted_iota(jnp.int32, (NEAR * FAR, LANES), 0)
    lane_of = lax.broadcasted_iota(jnp.int32, (NEAR * FAR, LANES), 1)
    line_far = (line_at >> 3) & (FAR - 1)
    line_near = ((line_at >> 7) << 3) | (line_at & 7)
    arrive = ((line_far & 3) << 2) | (line_far >> 2)
    inverse[...] = jnp.zeros(inverse.shape, jnp.float32)

    def invert(c):
        number = lane_gather(seconds[...], jnp.full((NEAR * FAR, LANES), 88, jnp.int32) + c).astype(jnp.int32)
        code = jnp.where(lane_of < NEAR, arrive, (line_near << 3) + c)
        group_hit = ((number >> 7) == (lane_of & (NEAR - 1))) & (lane_of < 2 * NEAR)
        coded = jnp.where(group_hit, code, 0).astype(jnp.float32).astype(jnp.bfloat16)
        lane_hit = jnp.where((number & (LANES - 1)) == lane_of, 1.0, 0.0).astype(jnp.bfloat16)
        inverse[...] += lax.dot_general(coded, lane_hit, (((0,), (0,)), ((), ())),
                                        preferred_element_type=jnp.float32)[0:2 * NEAR]

    loop(0, 8, invert)

    loop(1, FAR, lambda k: far_part(k).wait(), 15)
    for y_from in range(YS):
        arrived = far_buf[y_from]
        for x_from in range(1, XS):
            arrived = arrived + far_buf[(x_from << 2) | y_from]
        state[y_from * XS:(y_from + 1) * XS] = arrived
    from_row, from_lane = inverse[0:NEAR].astype(jnp.int32), inverse[NEAR:].astype(jnp.int32)
    ordered = jnp.zeros((groups, LANES), jnp.float32)
    for g in range(groups):
        taken = lane_gather(jnp.broadcast_to(state[pl.ds(g, 1)], (groups, LANES)), from_lane)
        ordered = jnp.where(from_row == g, taken, ordered)
    rhs[...] = ordered

    state[...] = rhs[...] / diag[...]

    def pick(low_ref, high_ref, factor_ref, b, start):
        at = pl.ds(start, 8)
        lane_of, row = low_ref[b, at], high_ref[b, at]
        found = [lane_gather(packed[q], lane_of) for q in range(8)]
        bit = 1
        while len(found) > 1:
            odd = (row & bit) != 0
            found = [jnp.where(odd, found[2 * i + 1], found[2 * i]) for i in range(len(found) // 2)]
            bit = bit * 2
        word = found[0]
        number = jnp.where((row & 8) != 0, word >> 16, (word << 16) >> 16)
        return number.astype(jnp.float32) * factor_ref[b, at]

    first_top = jnp.max(jnp.max(jnp.abs(state[...]), axis=1, keepdims=True), axis=0, keepdims=True)

    def pack(sweeps):
        now = state[...]
        top = jnp.maximum(first_top * (1.0 + sweeps), 1e-34)
        whole = jnp.round(now * (FULL / top)).astype(jnp.int32)
        word = (whole[8:16] << 16) + (whole[0:8] & 0xFFFF)
        for q in range(8):
            packed[q] = jnp.broadcast_to(word[q:q + 1], (8, LANES))
        return top * (1.0 / FULL)

    for repeat in range(COARSE_SWEEPS - 2):
        scale = pack(repeat)

        def relax_group(g):
            parts = []
            for half in range(2):
                start = pl.multiple_of(g * NEAR + half * 8, 8)
                parts.append(pick(low, high, factor, 0, start) + pick(low, high, factor, 1, start))
            total = jnp.concatenate(parts, axis=0)
            state[pl.ds(g, 1)] = (rhs[pl.ds(g, 1)] - squeeze(total) * scale) / diag[pl.ds(g, 1)]

        loop(0, groups, relax_group, 4)

    scale = pack(COARSE_SWEEPS - 2)
    lane_all = lax.broadcasted_iota(jnp.int32, (SLABS + NEAR, LANES), 1)
    right = jnp.zeros((SLABS + NEAR, LANES), jnp.float32)
    below = jnp.zeros((SLABS + NEAR, LANES), jnp.float32)
    for g in range(groups):
        hit = target[...] - g * LANES == lane_all
        right = jnp.where(hit, rhs[pl.ds(g, 1)], right)
        below = jnp.where(hit, diag[pl.ds(g, 1)], below)
    coupled = jnp.concatenate([
        pick(last_low, last_high, last_factor, 0, p) + pick(last_low, last_high, last_factor, 1, p)
        for p in range(0, SLABS + NEAR, 8)], axis=0)
    solved = jnp.sum(right - coupled * scale, axis=1, keepdims=True) / jnp.sum(below, axis=1, keepdims=True)
    solved = jnp.broadcast_to(solved, (SLABS + NEAR, LANES))
    scaled = solved[0:SLABS]
    mine8 = solved[SLABS:SLABS + 8]
    correction[...] = jnp.sum(jnp.where(row8 == lane8, mine8, 0.0), axis=0, keepdims=True)[:, 0:8]

    chooser = selector[:, 0:SLABS].astype(jnp.bfloat16)

    def deposit(k):
        terms = (scaled * turned[k].astype(jnp.float32)).astype(jnp.bfloat16)
        pieces[k & 1, pl.ds(k >> 1, rows, stride=depth), :] = jnp.dot(chooser, terms, preferred_element_type=jnp.float32)

    loop(0, 2 * depth, deposit, 32)
    none = jnp.zeros((depth, width), jnp.float32)
    for pad in (vpad, cpad, upad):
        pad[0] = none
        pad[rows + 1] = none

    def correct(y):
        at = pl.ds(y * depth, depth)
        v = value[y] + jnp.concatenate([pieces[0, at, :], pieces[1, at, :]], axis=1)
        vpad[y + 1] = v
        upad[y + 1] = conduct[y] * v
        zsend[0, 0, pl.ds(y, 1)] = v[0:1]
        zsend[0, 1, pl.ds(y, 1)] = v[depth - 1:depth]

    loop(0, rows, correct, 8)

    around = (to_slab(1), to_slab(SLABS - 1), (slab, (tile + 1) & 3), (slab, (tile + 3) & 3))
    for step in range(SMOOTH_SWEEPS):
        now = vpad if step == 0 else cpad
        copies = (
            remote(zsend.at[step, 1], zrecv.at[step, 0], v_send.at[step, 0], v_recv.at[step, 0], around[0]),
            remote(zsend.at[step, 0], zrecv.at[step, 1], v_send.at[step, 1], v_recv.at[step, 1], around[1]),
            remote(now.at[rows], yrecv.at[step, 0], v_send.at[step, 2], v_recv.at[step, 2], around[2]),
            remote(now.at[1], yrecv.at[step, 1], v_send.at[step, 3], v_recv.at[step, 3], around[3]),
        )
        for copy in copies:
            copy.start()

        if step > 0:
            def product(y):
                upad[y + 1] = conduct[y] * now[y + 1]
            loop(0, rows, product, 4)

        def inner(y):
            v = now[y + 1]
            vsum = beside(v, now[y], now[y + 2], 0.0, 0.0)
            usum = beside(upad[y + 1], upad[y], upad[y + 2], 0.0, 0.0)
            coupled = 0.5 * (conduct[y] * vsum + usum)
            relaxed = (1.0 - OMEGA) * v + weight[y] * (source[y] + coupled)
            if step == 0:
                cpad[y + 1] = relaxed
            else:
                out[y] = relaxed

        loop(0, rows, inner, 2)
        for copy in copies:
            copy.wait()
        later, shift = (cpad, 1) if step == 0 else (out, 0)
        later[shift] = later[shift] + ygain[0] * yrecv[step, 0]
        later[shift + rows - 1] = later[shift + rows - 1] + ygain[1] * yrecv[step, 1]

        def close(y):
            line = pl.ds(y, 1)
            lowest = later[y + shift, 0:1] + zgain[0, line] * zrecv[step, 0, line]
            highest = later[y + shift, depth - 1:depth] + zgain[1, line] * zrecv[step, 1, line]
            later[y + shift, 0:1] = lowest
            later[y + shift, depth - 1:depth] = highest
            if step + 1 < SMOOTH_SWEEPS:
                zsend[step + 1, 0, line] = lowest
                zsend[step + 1, 1, line] = highest

        loop(0, rows, close, 16)


def cycle(nnz, cells, diffusivity, uptake, send, slot, length, ids, diag, off, cols, value, source, label, basis):
    rows, depth, width = value.shape
    f32, bf16, i32 = jnp.float32, jnp.bfloat16, jnp.int32
    vmem, smem, dma = pltpu.VMEM, pltpu.SMEM, pltpu.SemaphoreType.DMA
    groups = cells // LANES
    reads = SLABS + NEAR
    block, padded = vmem(value.shape, f32), vmem((rows + 2, depth, width), f32)
    zfaces, yfaces = vmem((2, 2, rows, width), f32), vmem((2, 2, depth, width), f32)
    entries = (2, NEAR * FAR, LANES)
    return pl.pallas_call(
        functools.partial(cycle_kernel, nnz),
        out_shape=(jax.ShapeDtypeStruct(value.shape, f32), jax.ShapeDtypeStruct((1, 8), f32)),
        in_specs=[HBM] * 13,
        out_specs=(VMEM,) * 2,
        scratch_shapes=[
            smem(diffusivity.shape, f32), smem(uptake.shape, f32), smem(send.shape, i32), smem(slot.shape, i32),
            smem(length.shape, i32), smem(ids.shape, i32), smem(diag.shape, f32),
            vmem(slot.shape, i32), vmem(off.shape, f32), vmem(cols.shape, i32),
            block, block, vmem(label.shape, i32), vmem(basis.shape, bf16),
            vmem((SLABS, depth, width), bf16), vmem((SLABS, depth, width), bf16), zfaces, yfaces, zfaces, yfaces,
            vmem((4, LANES), f32), vmem((NEAR, 4, LANES), f32), vmem((NEAR * FAR, 4, LANES), f32), vmem((2, SLABS * depth, LANES), f32),
            vmem((2 * depth, SLABS, LANES), bf16),
            block, block, padded, padded, padded, block, vmem((SLABS, LANES), f32),
            vmem((NEAR, XS, LANES), f32), vmem((FAR, XS, LANES), f32),
            vmem((reads, LANES), i32), smem((reads, LANES), i32), vmem((SLABS, LANES), i32),
            vmem((NEAR * FAR, LANES), f32), vmem((2 * NEAR, LANES), f32), vmem((rows, LANES), f32),
            vmem((groups, LANES), f32), vmem((groups, LANES), f32), vmem((groups, LANES), f32),
            vmem((8, 8, LANES), i32), vmem(entries, i32), vmem(entries, i32), vmem(entries, f32),
            vmem((2, reads, LANES), i32), vmem((2, reads, LANES), i32), vmem((2, reads, LANES), f32),
            vmem((2, rows, width), f32), vmem((2, depth, width), f32),
            vmem((SMOOTH_SWEEPS, 2, rows, width), f32), vmem((SMOOTH_SWEEPS, 2, rows, width), f32),
            vmem((SMOOTH_SWEEPS, 2, depth, width), f32),
            dma((14,)), dma((1,)), dma((2,)),
            dma((SLABS,)), dma((SLABS,)), dma((NEAR,)), dma((NEAR,)), dma((FAR,)), dma((FAR,)),
            dma((4,)), dma((4,)), dma((2,)), dma((NEAR,)), dma((NEAR,)), dma((FAR,)), dma((FAR,)),
            dma((SMOOTH_SWEEPS, 4)), dma((SMOOTH_SWEEPS, 4)),
        ],
        compiler_params=pltpu.CompilerParams(collective_id=0, has_side_effects=True, vmem_limit_bytes=48 << 20),
        name="cycle",
    )(diffusivity, uptake, send, slot, length, ids, diag, off, cols, value, source, label, basis)


def shards(solution, source, phase_label, phase_diffusivity, phase_uptake, send_tiles, support_slot, support_len,
           coarse_ids, basis_values, coarse_diag, coarse_off, coarse_cols):
    nnz = coarse_off.shape[1]
    cells = basis_values.shape[0] * NEAR * FAR
    send = send_tiles.transpose(0, 1, 3, 2)
    operands = [pltpu.with_memory_space_constraint(operand, pltpu.HBM) for operand in (
        solution, source, phase_label, basis_values, coarse_off, coarse_cols, phase_diffusivity, phase_uptake, send,
        support_slot, support_len, coarse_ids, coarse_diag)]
    (solution, source, phase_label, basis_values, coarse_off, coarse_cols, phase_diffusivity, phase_uptake, send,
     support_slot, support_len, coarse_ids, coarse_diag) = operands
    new_solution, correction = cycle(
        nnz, cells, phase_diffusivity, phase_uptake, send, support_slot, support_len, coarse_ids, coarse_diag,
        coarse_off, coarse_cols, solution, source, phase_label, basis_values)
    return new_solution, correction.reshape(correction.shape[1])


def solution(mesh):
    placed = (
        P("tile", "slab", None),
        P("tile", "slab", None),
        P("tile", "slab", None),
        P(),
        P(),
        P("slab", "tile", None, None),
        P("slab", "tile", None),
        P("slab", "tile", None),
        P(("slab", "tile")),
        P(("slab", "tile"), None, None),
        P(("slab", "tile")),
        P(("slab", "tile"), None),
        P(("slab", "tile"), None),
    )
    return jax.shard_map(
        shards,
        mesh=mesh,
        in_specs=placed,
        out_specs=(P("tile", "slab", None), P(("slab", "tile"))),
        check_vma=False,
    )
```

```python
import functools

import jax
import jax.numpy as jnp
from jax import lax
from jax.experimental import pallas as pl
from jax.experimental.pallas import tpu as pltpu
from jax.sharding import PartitionSpec as P

COARSE_SWEEPS = 4
SMOOTH_SWEEPS = 2
OMEGA = 0.8
MESH = pl.DeviceIdType.MESH
LANES = 128
FULL = 32760.0

ZS, XS, CORES, YS = 8, 4, 2, 4
NEAR = ZS * CORES
FAR = XS * YS
SLABS = ZS * XS * CORES

NEAR_ORDER = sorted(range(1, NEAR), key=lambda k: abs(k - NEAR // 2))
FAR_ORDER = sorted(range(1, FAR), key=lambda k: abs((k >> 2) - XS // 2) + abs((k & 3) - YS // 2))


def split_slab(slab):
    return slab >> 3, (slab >> 1) & 3, slab & 1


def near_device(near, x, tile):
    return ((near >> 1) << 3) | (x << 1) | (near & 1), tile


def far_device(far, z, core):
    return (z << 3) | ((far >> 2) << 1) | core, far & 3


def ordered_slab(order):
    return near_device(order & (NEAR - 1), order >> 4, 0)[0]


def table_row(far, near):
    return ((near >> 3) << 7) | (far << 3) | (near & 7)


def place_of(index):
    owner, row = index >> 3, index & 7
    slab, tile = owner >> 2, owner & 3
    z, x, core = split_slab(slab)
    return (table_row((x << 2) | tile, (z << 1) | core) << 3) | row


VMEM = pl.BlockSpec(memory_space=pltpu.VMEM)
HBM = pl.BlockSpec(memory_space=pltpu.HBM)


def remote(src, dst, send_sem, recv_sem, device):
    return pltpu.make_async_remote_copy(
        src_ref=src, dst_ref=dst, send_sem=send_sem, recv_sem=recv_sem,
        device_id=device, device_id_type=MESH,
    )


def loop(low, high, act, unroll=1):
    def body(k, carry):
        act(k)
        return carry
    lax.fori_loop(low, high, body, 0, unroll=unroll)


def lane_gather(source, index):
    numbers = lax.GatherDimensionNumbers(
        offset_dims=(), collapsed_slice_dims=(1,), start_index_map=(1,),
        operand_batching_dims=(0,), start_indices_batching_dims=(0,),
    )
    return lax.gather(source, index[..., None], numbers, (1, 1), mode=lax.GatherScatterMode.PROMISE_IN_BOUNDS)


def beside(mid, below, above, zlow, zhigh):
    depth, width = mid.shape
    zi = lax.broadcasted_iota(jnp.int32, mid.shape, 0)
    xi = lax.broadcasted_iota(jnp.int32, mid.shape, 1)
    total = below + above
    total = total + jnp.where(zi == 0, zlow, pltpu.roll(mid, 1, 0))
    total = total + jnp.where(zi == depth - 1, zhigh, pltpu.roll(mid, depth - 1, 0))
    total = total + jnp.where(xi == 0, 0.0, pltpu.roll(mid, 1, 1))
    total = total + jnp.where(xi == width - 1, 0.0, pltpu.roll(mid, width - 1, 1))
    return total


def lookup(label, table):
    result = jnp.full(label.shape, table[0], jnp.float32)
    for category in range(1, table.shape[0]):
        result = jnp.where(label == category, table[category], result)
    return result


def cycle_kernel(nnz, diffusivity_h, uptake_h, send_h, slot_h, length_h, ids_h, diag_h, off_h, cols_h,
                 value_h, source_h, label_h, basis_h,
                 out, correction,
                 diffusivity, uptake, send, slot, length, ids, diag_own, slot_row, off, cols,
                 value, source, label, basis,
                 sent, got, zface, yface, zhalo, yhalo, meta, near_table, table, pieces, turned,
                 conduct, weight, cpad, vpad, upad, tiles, sums, near_buf, far_buf,
                 target, target_s, spot, seconds, inverse, selector, state, rhs, diag, packed, low, high, factor,
                 last_low, last_high, last_factor, zgain, ygain, zsend, zrecv, yrecv,
                 load_sem, target_sem, swap_sem, a_send, a_recv, n_send, n_recv, f_send, f_recv, h_send, h_recv, own,
                 s_send, s_recv, t_send, t_recv, v_send, v_recv):
    rows, depth, width = value.shape
    groups = rhs.shape[0]
    slab, tile = lax.axis_index("slab"), lax.axis_index("tile")
    z, x, core = split_slab(slab)
    near = (z << 1) | core
    far = (x << 2) | tile
    order = (x << 4) | near

    barrier = pltpu.get_barrier_semaphore()

    def to_near(k):
        return near_device((near + k) & (NEAR - 1), x, tile)

    def to_far(k):
        return far_device((far + k) & (FAR - 1), z, core)

    def to_slab(k):
        return (slab + k) & (SLABS - 1), tile

    def greet(device):
        pl.semaphore_signal(barrier, inc=1, device_id=device, device_id_type=MESH)

    for k in sorted(range(1, SLABS), key=lambda k: abs(k - SLABS // 2)):
        greet(to_slab(k))
    for k in range(XS * (YS - 1)):
        greet(((z << 3) | (((x + k) & 3) << 1) | core, (tile + 1 + (k >> 2)) & (YS - 1)))
    loads = [pltpu.make_async_copy(*pair, load_sem.at[i]) for i, pair in enumerate((
        (slot_h, slot), (length_h, length), (slot_h, slot_row), (basis_h, basis), (off_h, off), (cols_h, cols),
        (ids_h, ids), (diag_h, diag_own), (diffusivity_h, diffusivity), (uptake_h, uptake), (send_h, send),
        (label_h, label), (value_h, value), (source_h, source)))]
    for load in loads:
        load.start()
    for load in loads[:11]:
        load.wait()

    lane8 = lax.broadcasted_iota(jnp.int32, (8, LANES), 1)
    row8 = lax.broadcasted_iota(jnp.int32, (8, LANES), 0)
    lane1 = lax.broadcasted_iota(jnp.int32, (1, LANES), 1)
    entry = jnp.minimum(((row8 & 1) << 4) + (lane8 >> 3), nnz - 1)
    blank = jnp.zeros((8, LANES - nnz), jnp.float32)
    wide_off = jnp.concatenate([off[...], blank], axis=1)
    wide_cols = jnp.concatenate([place_of(cols[...]).astype(jnp.float32), blank], axis=1)
    offs = jnp.zeros((8, LANES), jnp.float32)
    places = jnp.zeros((8, LANES), jnp.float32)
    diag_row = jnp.zeros((1, LANES), jnp.float32)
    id_row = jnp.zeros((1, LANES), jnp.int32)
    for r in range(8):
        mine = (lane8 & 7) == r
        offs = jnp.where(mine, lane_gather(jnp.broadcast_to(wide_off[r:r + 1], (8, LANES)), entry), offs)
        places = jnp.where(mine, lane_gather(jnp.broadcast_to(wide_cols[r:r + 1], (8, LANES)), entry), places)
        diag_row = jnp.where((lane1 & 7) == r, diag_own[r], diag_row)
        id_row = jnp.where((lane1 & 7) == r, place_of(ids[r]), id_row)
    slot_cell = jnp.zeros((1, LANES), jnp.int32)
    for e in range(SLABS):
        slot_cell = jnp.where(lane1 == slot[0, 0, e], e >> 3, slot_cell)
    held = slot_cell.astype(jnp.float32)
    group = lane1 >> 3
    second = offs[1:2]
    second = jnp.where(group == nnz - 16, diag_row, second)
    second = jnp.where(group == nnz - 15, id_row.astype(jnp.float32), second)
    second = jnp.where(group >= 12, pltpu.roll(held, 96, 1), second)
    fourth = jnp.where(group >= nnz - 16, pltpu.roll(held, 48, 1), places[1:2])
    meta[0:1] = offs[0:1]
    meta[1:2] = second
    meta[2:3] = places[0:1]
    meta[3:4] = fourth

    e_at = lax.broadcasted_iota(jnp.int32, (SLABS, SLABS), 1)
    m_at = lax.broadcasted_iota(jnp.int32, (SLABS, SLABS), 0)
    limit = jnp.zeros((SLABS, SLABS), jnp.int32)
    for c in range(8):
        limit = jnp.where((e_at >> 3) == c, length[0, 0, c], limit)
    chosen = (slot_row[0] == m_at) & ((e_at & 7) < limit)
    chooser = chosen.astype(jnp.float32).astype(jnp.bfloat16)

    def choose(k):
        at = pl.ds(pl.multiple_of(k * LANES, LANES), LANES)
        block = basis[:, :, at].astype(jnp.float32).reshape(SLABS, LANES).astype(jnp.bfloat16)
        pieces[k & 1, pl.ds(k >> 1, SLABS, stride=depth), :] = jnp.dot(
            chooser, block, preferred_element_type=jnp.float32)

    loop(0, 2 * depth, choose, 4)

    def settle(m):
        for h in range(2):
            sent[m, :, h * LANES:(h + 1) * LANES] = pieces[h, pl.ds(m * depth, depth), :].astype(jnp.bfloat16)

    loop(0, SLABS, settle, 4)
    for load in loads[11:13]:
        load.wait()

    def fill(y):
        c = lookup(label[y], diffusivity)
        v = value[y]
        cpad[y + 1] = c
        vpad[y + 1] = v
        upad[y + 1] = c * v
        conduct[y] = c
        zface[0, 0, pl.ds(y, 1)] = c[0:1]
        zface[1, 0, pl.ds(y, 1)] = c[depth - 1:depth]
        zface[0, 1, pl.ds(y, 1)] = v[0:1]
        zface[1, 1, pl.ds(y, 1)] = v[depth - 1:depth]

    loop(0, rows, fill, 4)
    for side, at in ((0, 1), (1, rows)):
        yface[side, 0] = cpad[at]
        yface[side, 1] = vpad[at]

    pl.semaphore_wait(barrier, SLABS - 1 + XS * (YS - 1))

    halos = (
        remote(zface.at[1], zhalo.at[0], h_send.at[0], h_recv.at[0], to_slab(1)),
        remote(zface.at[0], zhalo.at[1], h_send.at[1], h_recv.at[1], to_slab(SLABS - 1)),
        remote(yface.at[1], yhalo.at[0], h_send.at[2], h_recv.at[2], (slab, (tile + 1) & 3)),
        remote(yface.at[0], yhalo.at[1], h_send.at[3], h_recv.at[3], (slab, (tile + 3) & 3)),
    )
    mine = pltpu.make_async_copy(meta, near_table.at[near], own.at[0])
    mine.start()
    kept = pltpu.make_async_copy(sent.at[slab], got.at[order], own.at[1])
    kept.start()
    half = core * (NEAR * FAR // 2)
    near_half = near_table.at[pl.ds(core * (NEAR // 2), NEAR // 2)]
    block = table.at[pl.ds(half + far * (NEAR // 2), NEAR // 2)]
    half_table = table.at[pl.ds(half, NEAR * FAR // 2)]
    swap = remote(half_table, half_table, swap_sem.at[0], swap_sem.at[1], (slab ^ 1, tile))

    def near_copy(k):
        return remote(meta, near_table.at[near], n_send.at[k], n_recv.at[k], to_near(k))

    def far_copy(k):
        return remote(near_half, block, f_send.at[k], f_recv.at[k], to_far(k))

    def basis_copy(k):
        return remote(sent.at[(slab + k) & (SLABS - 1)], got.at[order], a_send.at[k], a_recv.at[k], to_slab(k))

    for k in NEAR_ORDER:
        near_copy(k).start()
    for copy in halos:
        copy.start()
    loop(1, SLABS, lambda k: basis_copy(k).start())
    mine.wait()
    kept.wait()
    loop(1, NEAR, lambda k: near_copy(k).wait())
    for k in FAR_ORDER:
        far_copy(k).start()
    table[pl.ds(half + far * (NEAR // 2), NEAR // 2)] = near_table[pl.ds(core * (NEAR // 2), NEAR // 2)]
    for copy in halos:
        copy.wait()

    loads[13].wait()

    has_low = jnp.where(slab > 0, 1.0, 0.0)
    has_high = jnp.where(slab < SLABS - 1, 1.0, 0.0)
    for side, at, flag in ((0, 0, jnp.where(tile > 0, 1.0, 0.0)), (1, rows + 1, jnp.where(tile < YS - 1, 1.0, 0.0))):
        c = yhalo[side, 0] * flag
        v = yhalo[side, 1] * flag
        cpad[at] = c
        vpad[at] = v
        upad[at] = c * v

    def plane(y):
        c, v, u = cpad[y + 1], vpad[y + 1], upad[y + 1]
        clow = zhalo[0, 0, pl.ds(y, 1)] * has_low
        chigh = zhalo[1, 0, pl.ds(y, 1)] * has_high
        vlow = zhalo[0, 1, pl.ds(y, 1)] * has_low
        vhigh = zhalo[1, 1, pl.ds(y, 1)] * has_high
        csum = beside(c, cpad[y], cpad[y + 2], clow, chigh)
        vsum = beside(v, vpad[y], vpad[y + 2], vlow, vhigh)
        usum = beside(u, upad[y], upad[y + 2], clow * vlow, chigh * vhigh)
        diagonal = lookup(label[y], uptake) + 3.0 * c + 0.5 * csum
        residual = source[y] - (diagonal * v - 0.5 * (c * vsum + usum))
        tiles[y] = residual.astype(jnp.bfloat16).astype(jnp.float32)
        weight[y] = OMEGA / diagonal

    loop(0, rows, plane, 2)

    row_at = lax.broadcasted_iota(jnp.int32, (rows, LANES), 0)
    lane_at = lax.broadcasted_iota(jnp.int32, (rows, LANES), 1)
    to_row = jnp.full((rows, LANES), -1, jnp.int32)
    for p in range(SLABS):
        to_row = jnp.where(lane_at == p, send[0, 0, 0, ordered_slab(p)], to_row)
    selector[...] = jnp.where(to_row == row_at, 1.0, 0.0)

    loop(1, FAR, lambda k: far_copy(k).wait())
    swap.start()
    swap.wait()
    lane = lax.broadcasted_iota(jnp.int32, (NEAR, LANES), 1)
    own_row = lax.broadcasted_iota(jnp.int32, (NEAR, LANES), 0)
    for x_from in range(XS):
        at = ((x_from << 2) | tile) * (NEAR // 2)
        own_rows = jnp.concatenate(
            [table[pl.ds(at, NEAR // 2)], table[pl.ds(NEAR * FAR // 2 + at, NEAR // 2)]], axis=0)
        first, second = own_rows[:, 1], own_rows[:, 3]
        picked = jnp.where((lane == 96 + slab) & (slab < 32), first, 0.0)
        picked = picked + jnp.where((lane == 48 + slab) & (slab >= 32), second, 0.0)
        cell = jnp.sum(picked, axis=1, keepdims=True).astype(jnp.int32)
        index = jnp.sum(jnp.where(lane == 88 + cell, first, 0.0), axis=1, keepdims=True).astype(jnp.int32)
        target[x_from * NEAR:(x_from + 1) * NEAR, :] = jnp.broadcast_to(index, (NEAR, LANES))
        spot[x_from * NEAR:(x_from + 1) * NEAR, :] = own_row * 8 + cell
    own_place = jnp.zeros((NEAR, LANES), jnp.int32)
    for r in range(8):
        own_place = jnp.where(own_row == r, place_of(ids[r]), own_place)
    target[SLABS:] = own_place
    to_scalar = pltpu.make_async_copy(target, target_s, target_sem.at[0])
    to_scalar.start()


    loop(1, SLABS, lambda k: basis_copy(k).wait())

    def product(p):
        terms = got[p].astype(jnp.float32) * tiles[send[0, 0, 0, ordered_slab(p)]]
        folded = terms[:, :LANES] + terms[:, LANES:]
        sums[pl.ds(p, 1)] = jnp.sum(folded, axis=0, keepdims=True)

    loop(0, SLABS, product, 8)
    products = jnp.broadcast_to(jnp.sum(sums[...], axis=1, keepdims=True), (SLABS, LANES))
    lane64 = lax.broadcasted_iota(jnp.int32, (SLABS, LANES), 1)
    placed = jnp.where(lane64 == spot[...], products, 0.0)
    for x_to in range(XS):
        near_buf[near, pl.ds(x_to, 1)] = jnp.sum(placed[x_to * NEAR:(x_to + 1) * NEAR], axis=0, keepdims=True)

    def near_part(k):
        return remote(near_buf.at[near], near_buf.at[near], s_send.at[k], s_recv.at[k], to_near(k))

    def far_part(k):
        return remote(far_buf.at[far], far_buf.at[far], t_send.at[k], t_recv.at[k], to_far(k))

    for k in NEAR_ORDER:
        near_part(k).start()

    def unfold(p):
        for h in range(2):
            pieces[h, pl.ds(p * depth, depth), :] = got[p, :, h * LANES:(h + 1) * LANES].astype(jnp.float32)

    loop(0, SLABS, unfold, 4)

    def turn(k):
        turned[k] = pieces[k & 1, pl.ds(k >> 1, SLABS, stride=depth), :].astype(jnp.bfloat16)

    loop(0, 2 * depth, turn, 4)

    for side, at, inside in ((0, 0, slab > 0), (1, depth - 1, slab < SLABS - 1)):
        flag = jnp.where(inside, 0.5, 0.0)

        def gain(y):
            line = pl.ds(y, 1)
            pair = conduct[y][at:at + 1] + zhalo[side, 0, line]
            zgain[side, line] = weight[y][at:at + 1] * pair * flag

        loop(0, rows, gain, 4)
    for side, at, inside in ((0, 0, tile > 0), (1, rows - 1, tile < YS - 1)):
        flag = jnp.where(inside, 0.5, 0.0)
        ygain[side] = weight[at] * (conduct[at] + yhalo[side, 0]) * flag

    loop(1, NEAR, lambda k: near_part(k).wait(), 15)
    far_buf[far] = jnp.sum(near_buf[...], axis=0)
    for k in FAR_ORDER:
        far_part(k).start()

    mine = own_row == lane >> 3
    used = lane < (nnz - 16) * 8
    is_diag = lane >> 3 == nnz - 16

    def squeeze(values):
        for shift in (8, 16, 32, 64):
            values = values + pltpu.roll(values, shift, 1)
        return jnp.sum(jnp.where(mine, values, 0.0), axis=0, keepdims=True)

    def prepare(g):
        at = pl.ds(pl.multiple_of(g * NEAR, NEAR), NEAR)
        block = table[at]
        second = block[:, 1]
        diag[pl.ds(g, 1)] = squeeze(jnp.where(is_diag, second, 0.0))
        seconds[at] = second
        factor[0, at] = block[:, 0]
        factor[1, at] = jnp.where(used, second, 0.0)
        for b in range(2):
            index = block[:, 2 + b].astype(jnp.int32)
            low[b, at] = index & (LANES - 1)
            high[b, at] = index >> 7

    loop(0, groups, prepare, 2)
    to_scalar.wait()

    def fetch(p):
        index = target_s[p, 0]
        line, here = pl.ds((index >> 3) & (NEAR * FAR - 1), 1), pl.ds(p, 1)
        keep = (lane1 & 7) == (index & 7)
        for b in range(2):
            last_factor[b, here] = jnp.where(keep, factor[b, line], 0.0)
            last_low[b, here] = low[b, line]
            last_high[b, here] = high[b, line]

    loop(0, SLABS + NEAR, fetch, 4)

    line_at = lax.broadcasted_iota(jnp.int32, (NEAR * FAR, LANES), 0)
    lane_of = lax.broadcasted_iota(jnp.int32, (NEAR * FAR, LANES), 1)
    line_far = (line_at >> 3) & (FAR - 1)
    line_near = ((line_at >> 7) << 3) | (line_at & 7)
    arrive = ((line_far & 3) << 2) | (line_far >> 2)
    inverse[...] = jnp.zeros(inverse.shape, jnp.float32)

    def invert(c):
        number = lane_gather(seconds[...], jnp.full((NEAR * FAR, LANES), 88, jnp.int32) + c).astype(jnp.int32)
        code = jnp.where(lane_of < NEAR, arrive, (line_near << 3) + c)
        group_hit = ((number >> 7) == (lane_of & (NEAR - 1))) & (lane_of < 2 * NEAR)
        coded = jnp.where(group_hit, code, 0).astype(jnp.float32).astype(jnp.bfloat16)
        lane_hit = jnp.where((number & (LANES - 1)) == lane_of, 1.0, 0.0).astype(jnp.bfloat16)
        inverse[...] += lax.dot_general(coded, lane_hit, (((0,), (0,)), ((), ())),
                                        preferred_element_type=jnp.float32)[0:2 * NEAR]

    loop(0, 8, invert)

    loop(1, FAR, lambda k: far_part(k).wait(), 15)
    for y_from in range(YS):
        arrived = far_buf[y_from]
        for x_from in range(1, XS):
            arrived = arrived + far_buf[(x_from << 2) | y_from]
        state[y_from * XS:(y_from + 1) * XS] = arrived
    from_row, from_lane = inverse[0:NEAR].astype(jnp.int32), inverse[NEAR:].astype(jnp.int32)
    ordered = jnp.zeros((groups, LANES), jnp.float32)
    for g in range(groups):
        taken = lane_gather(jnp.broadcast_to(state[pl.ds(g, 1)], (groups, LANES)), from_lane)
        ordered = jnp.where(from_row == g, taken, ordered)
    rhs[...] = ordered

    state[...] = rhs[...] / diag[...]

    def pick(low_ref, high_ref, factor_ref, b, start):
        at = pl.ds(start, 8)
        lane_of, row = low_ref[b, at], high_ref[b, at]
        found = [lane_gather(packed[q], lane_of) for q in range(8)]
        bit = 1
        while len(found) > 1:
            odd = (row & bit) != 0
            found = [jnp.where(odd, found[2 * i + 1], found[2 * i]) for i in range(len(found) // 2)]
            bit = bit * 2
        word = found[0]
        number = jnp.where((row & 8) != 0, word >> 16, (word << 16) >> 16)
        return number.astype(jnp.float32) * factor_ref[b, at]

    first_top = jnp.max(jnp.max(jnp.abs(state[...]), axis=1, keepdims=True), axis=0, keepdims=True)

    def pack(sweeps):
        now = state[...]
        top = jnp.maximum(first_top * (1.0 + sweeps), 1e-34)
        whole = jnp.round(now * (FULL / top)).astype(jnp.int32)
        word = (whole[8:16] << 16) + (whole[0:8] & 0xFFFF)
        for q in range(8):
            packed[q] = jnp.broadcast_to(word[q:q + 1], (8, LANES))
        return top * (1.0 / FULL)

    for repeat in range(COARSE_SWEEPS - 2):
        scale = pack(repeat)

        def relax_group(g):
            parts = []
            for half in range(2):
                start = pl.multiple_of(g * NEAR + half * 8, 8)
                parts.append(pick(low, high, factor, 0, start) + pick(low, high, factor, 1, start))
            total = jnp.concatenate(parts, axis=0)
            state[pl.ds(g, 1)] = (rhs[pl.ds(g, 1)] - squeeze(total) * scale) / diag[pl.ds(g, 1)]

        loop(0, groups, relax_group, 4)

    scale = pack(COARSE_SWEEPS - 2)
    lane_all = lax.broadcasted_iota(jnp.int32, (SLABS + NEAR, LANES), 1)
    right = jnp.zeros((SLABS + NEAR, LANES), jnp.float32)
    below = jnp.zeros((SLABS + NEAR, LANES), jnp.float32)
    for g in range(groups):
        hit = target[...] - g * LANES == lane_all
        right = jnp.where(hit, rhs[pl.ds(g, 1)], right)
        below = jnp.where(hit, diag[pl.ds(g, 1)], below)
    coupled = jnp.concatenate([
        pick(last_low, last_high, last_factor, 0, p) + pick(last_low, last_high, last_factor, 1, p)
        for p in range(0, SLABS + NEAR, 8)], axis=0)
    solved = jnp.sum(right - coupled * scale, axis=1, keepdims=True) / jnp.sum(below, axis=1, keepdims=True)
    solved = jnp.broadcast_to(solved, (SLABS + NEAR, LANES))
    scaled = solved[0:SLABS]
    mine8 = solved[SLABS:SLABS + 8]
    correction[...] = jnp.sum(jnp.where(row8 == lane8, mine8, 0.0), axis=0, keepdims=True)[:, 0:8]

    chooser = selector[:, 0:SLABS].astype(jnp.bfloat16)

    def deposit(k):
        terms = (scaled * turned[k].astype(jnp.float32)).astype(jnp.bfloat16)
        pieces[k & 1, pl.ds(k >> 1, rows, stride=depth), :] = jnp.dot(chooser, terms, preferred_element_type=jnp.float32)

    loop(0, 2 * depth, deposit, 32)
    none = jnp.zeros((depth, width), jnp.float32)
    for pad in (vpad, cpad, upad):
        pad[0] = none
        pad[rows + 1] = none

    def correct(y):
        at = pl.ds(y * depth, depth)
        v = value[y] + jnp.concatenate([pieces[0, at, :], pieces[1, at, :]], axis=1)
        vpad[y + 1] = v
        upad[y + 1] = conduct[y] * v
        zsend[0, 0, pl.ds(y, 1)] = v[0:1]
        zsend[0, 1, pl.ds(y, 1)] = v[depth - 1:depth]

    loop(0, rows, correct, 8)

    around = (to_slab(1), to_slab(SLABS - 1), (slab, (tile + 1) & 3), (slab, (tile + 3) & 3))
    for step in range(SMOOTH_SWEEPS):
        now = vpad if step == 0 else cpad
        copies = (
            remote(zsend.at[step, 1], zrecv.at[step, 0], v_send.at[step, 0], v_recv.at[step, 0], around[0]),
            remote(zsend.at[step, 0], zrecv.at[step, 1], v_send.at[step, 1], v_recv.at[step, 1], around[1]),
            remote(now.at[rows], yrecv.at[step, 0], v_send.at[step, 2], v_recv.at[step, 2], around[2]),
            remote(now.at[1], yrecv.at[step, 1], v_send.at[step, 3], v_recv.at[step, 3], around[3]),
        )
        for copy in copies:
            copy.start()

        if step > 0:
            def product(y):
                upad[y + 1] = conduct[y] * now[y + 1]
            loop(0, rows, product, 4)

        def inner(y):
            v = now[y + 1]
            vsum = beside(v, now[y], now[y + 2], 0.0, 0.0)
            usum = beside(upad[y + 1], upad[y], upad[y + 2], 0.0, 0.0)
            coupled = 0.5 * (conduct[y] * vsum + usum)
            relaxed = (1.0 - OMEGA) * v + weight[y] * (source[y] + coupled)
            if step == 0:
                cpad[y + 1] = relaxed
            else:
                out[y] = relaxed

        loop(0, rows, inner, 2)
        for copy in copies:
            copy.wait()
        later, shift = (cpad, 1) if step == 0 else (out, 0)
        later[shift] = later[shift] + ygain[0] * yrecv[step, 0]
        later[shift + rows - 1] = later[shift + rows - 1] + ygain[1] * yrecv[step, 1]

        def close(y):
            line = pl.ds(y, 1)
            lowest = later[y + shift, 0:1] + zgain[0, line] * zrecv[step, 0, line]
            highest = later[y + shift, depth - 1:depth] + zgain[1, line] * zrecv[step, 1, line]
            later[y + shift, 0:1] = lowest
            later[y + shift, depth - 1:depth] = highest
            if step + 1 < SMOOTH_SWEEPS:
                zsend[step + 1, 0, line] = lowest
                zsend[step + 1, 1, line] = highest

        loop(0, rows, close, 16)


def cycle(nnz, cells, diffusivity, uptake, send, slot, length, ids, diag, off, cols, value, source, label, basis):
    rows, depth, width = value.shape
    f32, bf16, i32 = jnp.float32, jnp.bfloat16, jnp.int32
    vmem, smem, dma = pltpu.VMEM, pltpu.SMEM, pltpu.SemaphoreType.DMA
    groups = cells // LANES
    reads = SLABS + NEAR
    block, padded = vmem(value.shape, f32), vmem((rows + 2, depth, width), f32)
    zfaces, yfaces = vmem((2, 2, rows, width), f32), vmem((2, 2, depth, width), f32)
    entries = (2, NEAR * FAR, LANES)
    return pl.pallas_call(
        functools.partial(cycle_kernel, nnz),
        out_shape=(jax.ShapeDtypeStruct(value.shape, f32), jax.ShapeDtypeStruct((1, 8), f32)),
        in_specs=[HBM] * 13,
        out_specs=(VMEM,) * 2,
        scratch_shapes=[
            smem(diffusivity.shape, f32), smem(uptake.shape, f32), smem(send.shape, i32), smem(slot.shape, i32),
            smem(length.shape, i32), smem(ids.shape, i32), smem(diag.shape, f32),
            vmem(slot.shape, i32), vmem(off.shape, f32), vmem(cols.shape, i32),
            block, block, vmem(label.shape, i32), vmem(basis.shape, bf16),
            vmem((SLABS, depth, width), bf16), vmem((SLABS, depth, width), bf16), zfaces, yfaces, zfaces, yfaces,
            vmem((4, LANES), f32), vmem((NEAR, 4, LANES), f32), vmem((NEAR * FAR, 4, LANES), f32), vmem((2, SLABS * depth, LANES), f32),
            vmem((2 * depth, SLABS, LANES), bf16),
            block, block, padded, padded, padded, block, vmem((SLABS, LANES), f32),
            vmem((NEAR, XS, LANES), f32), vmem((FAR, XS, LANES), f32),
            vmem((reads, LANES), i32), smem((reads, LANES), i32), vmem((SLABS, LANES), i32),
            vmem((NEAR * FAR, LANES), f32), vmem((2 * NEAR, LANES), f32), vmem((rows, LANES), f32),
            vmem((groups, LANES), f32), vmem((groups, LANES), f32), vmem((groups, LANES), f32),
            vmem((8, 8, LANES), i32), vmem(entries, i32), vmem(entries, i32), vmem(entries, f32),
            vmem((2, reads, LANES), i32), vmem((2, reads, LANES), i32), vmem((2, reads, LANES), f32),
            vmem((2, rows, width), f32), vmem((2, depth, width), f32),
            vmem((SMOOTH_SWEEPS, 2, rows, width), f32), vmem((SMOOTH_SWEEPS, 2, rows, width), f32),
            vmem((SMOOTH_SWEEPS, 2, depth, width), f32),
            dma((14,)), dma((1,)), dma((2,)),
            dma((SLABS,)), dma((SLABS,)), dma((NEAR,)), dma((NEAR,)), dma((FAR,)), dma((FAR,)),
            dma((4,)), dma((4,)), dma((2,)), dma((NEAR,)), dma((NEAR,)), dma((FAR,)), dma((FAR,)),
            dma((SMOOTH_SWEEPS, 4)), dma((SMOOTH_SWEEPS, 4)),
        ],
        compiler_params=pltpu.CompilerParams(collective_id=0, has_side_effects=True, vmem_limit_bytes=48 << 20),
        name="cycle",
    )(diffusivity, uptake, send, slot, length, ids, diag, off, cols, value, source, label, basis)


def shards(solution, source, phase_label, phase_diffusivity, phase_uptake, send_tiles, support_slot, support_len,
           coarse_ids, basis_values, coarse_diag, coarse_off, coarse_cols):
    nnz = coarse_off.shape[1]
    cells = basis_values.shape[0] * NEAR * FAR
    send = send_tiles.transpose(0, 1, 3, 2)
    operands = [pltpu.with_memory_space_constraint(operand, pltpu.HBM) for operand in (
        solution, source, phase_label, basis_values, coarse_off, coarse_cols, phase_diffusivity, phase_uptake, send,
        support_slot, support_len, coarse_ids, coarse_diag)]
    (solution, source, phase_label, basis_values, coarse_off, coarse_cols, phase_diffusivity, phase_uptake, send,
     support_slot, support_len, coarse_ids, coarse_diag) = operands
    new_solution, correction = cycle(
        nnz, cells, phase_diffusivity, phase_uptake, send, support_slot, support_len, coarse_ids, coarse_diag,
        coarse_off, coarse_cols, solution, source, phase_label, basis_values)
    return new_solution, correction.reshape(correction.shape[1])


def solution(mesh):
    placed = (
        P("tile", "slab", None),
        P("tile", "slab", None),
        P("tile", "slab", None),
        P(),
        P(),
        P("slab", "tile", None, None),
        P("slab", "tile", None),
        P("slab", "tile", None),
        P(("slab", "tile")),
        P(("slab", "tile"), None, None),
        P(("slab", "tile")),
        P(("slab", "tile"), None),
        P(("slab", "tile"), None),
    )
    return jax.shard_map(
        shards,
        mesh=mesh,
        in_specs=placed,
        out_specs=(P("tile", "slab", None), P(("slab", "tile"))),
        check_vma=False,
    )
```
